128 devices in a mesh: dom: 32 (over y, x, core), sub: 4 (over z).
Axes of the slice: x: 4, y: 4, z: 4, core: 2. Of those that a mesh axis runs over, the one named last changes fastest.
Arguments:
- field_state: float32 [9, 20, 32768], P(None, None, ('dom', 'sub')), may hold values from -6 to 6
- adjoint: float32 [9, 20, 32768], P(None, None, ('dom', 'sub')), may hold values from -6 to 6
- eps_inf: float32 [32768], P(('dom', 'sub')), may hold values from 2 to 8
- eps_delta: float32 [32768], P(('dom', 'sub')), may hold values from 2 to 30
- relax_time: float32 [32768], P(('dom', 'sub')), may hold values from 0.2 to 2
- metric: float32 [9, 32768], P(None, ('dom', 'sub')), may hold values from -4 to 4
- face_scale: float32 [4, 32768], P(None, ('dom', 'sub')), may hold values from 0.5 to 2
- face_angles: float32 [2, 4, 32768], P(None, None, ('dom', 'sub')), may hold values from -3.140625 to 3.140625
- nbr_index: int32 [40, 32768], P(None, ('dom', 'sub')), may hold values from 0 to 11263, as said below
- dom_export: int32 [32768], P(('dom', 'sub')), may hold values from 0 to 10239
- sub_export: int32 [128, 4, 128], P(('dom', 'sub')), may hold values from 0 to 10239
- send_slot: int32 [32768], P(('dom', 'sub')), may hold values from 0 to 255, as said below
- recv_index: int32 [128, 128, 2], P(('dom', 'sub')), may hold values from 0 to 64, as said below
Outputs:
- adjoint_out: float32 [9, 20, 32768], P(None, None, ('dom', 'sub'))
- thermal_grad: float32 [3, 8192], P(None, ('dom', 'sub'))
The draws below stay inside these ranges and needn't reach their ends.
Inputs may be any that keep to these rules, and one draw needn't show every extreme that they name: `nbr_index`: pool rows (10880) to (11135) are never named. `send_slot`: elements of one device that share a slot share a thermal element. `recv_index`: slots that the source leaves empty hold 64.
All inputs are finite; a program needn't handle non-finite values.
Results may differ from the reference program's by a relative error of at most 0.0003.
Values sent between devices are 32-bit elements; how exact they have to be, the bound alone decides.
A program may use at most 128 MiB of HBM per device.

```python
import math
import jax
import jax.numpy as jnp
from jax import lax

NP = 20
K_DEV = 256
XR = 128
XSP = 128
SUB_ROWS = 512
KT = 64
CAP = 2
NE = 32768
NT = 8192
N_DOM = 32
N_SUB = 4


def draw_nbr_index(key, part):
    keys = jax.random.split(jax.random.fold_in(key, 3), 4)
    shape = (40, NE)
    region = jax.random.randint(keys[0], shape, 0, 20)
    own_rows = jax.random.randint(keys[1], shape, 0, 40 * K_DEV)
    sub_rows = 40 * K_DEV + jax.random.randint(keys[2], shape, 0, SUB_ROWS)
    rim = jax.random.randint(keys[3], shape, 0, XR)
    base = 40 * K_DEV + SUB_ROWS
    picked = jnp.where(region < 2, sub_rows, jnp.where(region == 2, base + rim, jnp.where(region == 3, base + 3 * XR + rim, own_rows)))
    element_col = jnp.arange(NE)[None, :] % K_DEV
    face_row = jnp.arange(40)[:, None]
    top_row = base + 4 * XR - 1
    return jnp.where((element_col == 0) & (face_row == 0), top_row, picked).astype(jnp.int32)


def slot_plan(key):
    devices = NE // K_DEV
    keys = jax.random.split(jax.random.fold_in(key, 7), 2)
    target = jax.random.randint(keys[0], (NE,), 0, devices)
    slot_no = jax.random.randint(keys[1], (NE,), 0, CAP)
    flat_slot = target * CAP + slot_no
    first = jnp.arange(NE) % K_DEV == 0
    return jnp.where(first, devices * CAP - 1, flat_slot).astype(jnp.int32)


def draw_send_slot(key, part):
    return slot_plan(key)


def draw_recv_index(key, part):
    devices = NE // K_DEV
    flat_slot = slot_plan(key)
    source_dev = jnp.arange(NE) // K_DEV
    target = flat_slot // CAP
    slot_no = flat_slot % CAP
    used = jnp.zeros((devices * devices * CAP,), jnp.int32).at[(target * devices + source_dev) * CAP + slot_no].max(1)
    thermal_ids = jax.random.randint(jax.random.fold_in(key, 11), (devices * devices * CAP,), 0, KT)
    return jnp.where(used > 0, thermal_ids, KT).reshape(devices, devices, CAP).astype(jnp.int32)


def plant(entries, rng, low, largest):
    index_at = [jax.random.randint(jax.random.fold_in(rng, axis), (), 0, length) for axis, length in enumerate(entries.shape)]
    widest = entries.shape.index(max(entries.shape))
    beside = index_at[:widest] + [(index_at[widest] + 1) % entries.shape[widest]] + index_at[widest + 1:]
    return entries.at[tuple(index_at)].set(low).at[tuple(beside)].set(largest)


def shard_levels(key, extent, cuts, smallest, high):
    def one(position, shards_of):
        steps = jax.random.uniform(jax.random.fold_in(jax.random.fold_in(key, 6), position), (shards_of,), jnp.float32, smallest / len(cuts), high / len(cuts))
        return jnp.repeat(jnp.exp(steps), extent[position] // shards_of).reshape((-1,) + (1,) * (len(extent) - position - 1))

    gain = one(*cuts[0])
    for cut in cuts[1:]:
        gain = gain * one(*cut)
    return gain


def centred(rng, extent, scale, limit, pieces=(), kind=jnp.bfloat16):
    entries = jax.random.normal(rng, extent, jnp.float32) * scale
    if len(pieces) > 0:
        entries = shard_levels(rng, extent, pieces, -0.22, 0.18) * entries
    return jnp.clip(entries, min=-limit, max=limit).astype(kind)


def setup_inputs(seed: int = 0) -> dict:
    key_of = jax.random.split(jax.random.key(seed), 14)
    field_state = centred(key_of[0], (9, NP, NE), 1.0, 6.0, ((2, 128),), jnp.float32)
    adjoint = centred(key_of[1], (9, NP, NE), 1.0, 6.0, ((2, 128),), jnp.float32)
    eps_inf = jnp.clip(jnp.exp(math.log(8.0) - 1.3862944 * jax.random.uniform(key_of[2], (NE,), jnp.float32) ** shard_levels(key_of[2], (NE,), ((0, 128),), -0.2, 0.2)), 2.0, 8.0)
    eps_delta = jnp.clip(jnp.exp(math.log(30.0) - 2.7080502 * jax.random.uniform(key_of[3], (NE,), jnp.float32) ** shard_levels(key_of[3], (NE,), ((0, 128),), -0.2, 0.2)), 2.0, 30.0)
    relax_time = jnp.clip(jnp.exp(math.log(2.0) - 2.3025851 * jax.random.uniform(key_of[4], (NE,), jnp.float32) ** shard_levels(key_of[4], (NE,), ((0, 128),), -0.2, 0.2)), 0.2, 2.0)
    metric = centred(key_of[5], (9, NE), 1.0, 4.0, ((1, 128),), jnp.float32)
    face_scale = jnp.clip(jnp.exp(math.log(2.0) - 1.3862944 * jax.random.uniform(key_of[6], (4, NE), jnp.float32) ** shard_levels(key_of[6], (4, NE), ((1, 128),), -0.2, 0.2)), 0.5, 2.0)
    face_angles = jnp.clip(jax.random.uniform(key_of[7], (2, 4, NE), jnp.float32, -3.140625, 3.140625), -3.140625, 3.140625)
    nbr_index = draw_nbr_index(jax.random.fold_in(key_of[13], 71), 0)
    dom_export = plant(jax.random.randint(key_of[9], (2 * XR * N_DOM * N_SUB,), 0, 40 * K_DEV), jax.random.fold_in(key_of[9], 1), 0, (40 * K_DEV) - 1).astype(jnp.int32)
    sub_export = plant(jax.random.randint(key_of[10], (N_DOM * N_SUB, N_SUB, XSP), 0, 40 * K_DEV), jax.random.fold_in(key_of[10], 1), 0, (40 * K_DEV) - 1).astype(jnp.int32)
    send_slot = draw_send_slot(jax.random.fold_in(key_of[13], 71), 0)
    recv_index = draw_recv_index(jax.random.fold_in(key_of[13], 71), 0)
    return dict(field_state=field_state, adjoint=adjoint, eps_inf=eps_inf, eps_delta=eps_delta, relax_time=relax_time, metric=metric, face_scale=face_scale, face_angles=face_angles, nbr_index=nbr_index, dom_export=dom_export, sub_export=sub_export, send_slot=send_slot, recv_index=recv_index)


time_step = 0.014

def mat_mul(left, right):
    inner = len(right)
    return [[sum((left[row_no][k] * right[k][col_no] for k in range(inner))) for col_no in range(len(right[0]))] for row_no in range(len(left))]

def transposed(matrix):
    return [list(column) for column in zip(*matrix)]

def solve_linear(matrix, rhs_rows):
    order = len(matrix)
    work = [list(matrix[row_no]) + list(rhs_rows[row_no]) for row_no in range(order)]
    for col_no in range(order):

        def magnitude(row_no):
            return abs(work[row_no][col_no])
        pivot = max(range(col_no, order), key=magnitude)
        work[col_no], work[pivot] = (work[pivot], work[col_no])
        head = work[col_no][col_no]
        work[col_no] = [value / head for value in work[col_no]]
        for row_no in range(order):
            if row_no != col_no:
                factor = work[row_no][col_no]
                work[row_no] = [value - factor * other for value, other in zip(work[row_no], work[col_no])]
    return [row[order:] for row in work]

def reference_element():
    lattice = [(i, j, k) for k in range(4) for j in range(4 - k) for i in range(4 - j - k)]
    points = [[float(v) / 3.0 for v in node] for node in lattice]
    vander = [[0.0] * 20 for node_no in range(20)]
    slopes = [[[0.0] * 20 for node_no in range(20)] for axis_no in range(3)]
    for node_no in range(20):
        for mono_no in range(20):
            power = lattice[mono_no]
            value = 1.0
            for axis_no in range(3):
                value *= points[node_no][axis_no] ** power[axis_no]
            vander[node_no][mono_no] = value
            for axis_no in range(3):
                if power[axis_no] > 0:
                    term = float(power[axis_no])
                    for other_no in range(3):
                        expo_val = power[other_no] - (1 if other_no == axis_no else 0)
                        term *= points[node_no][other_no] ** expo_val
                    slopes[axis_no][node_no][mono_no] = term
    identity = [[1.0 if row_no == col_no else 0.0 for col_no in range(20)] for row_no in range(20)]
    inverse = solve_linear(vander, identity)
    deriv_mats = [mat_mul(slopes[axis_no], inverse) for axis_no in range(3)]
    fact = math.factorial

    def face_integral(face_no, a, b, c):
        if face_no == 0:
            return 0.0 if c > 0 else fact(a) * fact(b) / fact(a + b + 2)
        if face_no == 1:
            return 0.0 if b > 0 else fact(a) * fact(c) / fact(a + c + 2)
        if face_no == 2:
            return math.sqrt(3.0) * fact(a) * fact(b) * fact(c) / fact(a + b + c + 2)
        return 0.0 if a > 0 else fact(b) * fact(c) / fact(b + c + 2)
    inverse_t = transposed(inverse)
    mono_mass = [[0.0] * 20 for node_no in range(20)]
    for first_no in range(20):
        for second_no in range(20):
            a = lattice[first_no][0] + lattice[second_no][0]
            b = lattice[first_no][1] + lattice[second_no][1]
            c = lattice[first_no][2] + lattice[second_no][2]
            mono_mass[first_no][second_no] = fact(a) * fact(b) * fact(c) / fact(a + b + c + 3)
    mass_mat = mat_mul(mat_mul(inverse_t, mono_mass), inverse)
    columns = [[] for node_no in range(20)]
    index_list = []
    for face_no in range(4):
        mono_face = [[0.0] * 20 for node_no in range(20)]
        for first_no in range(20):
            for second_no in range(20):
                a = lattice[first_no][0] + lattice[second_no][0]
                b = lattice[first_no][1] + lattice[second_no][1]
                c = lattice[first_no][2] + lattice[second_no][2]
                mono_face[first_no][second_no] = face_integral(face_no, a, b, c)
        face_mass = mat_mul(mat_mul(inverse_t, mono_face), inverse)
        tests = [k == 0 for i, j, k in lattice]
        if face_no == 1:
            tests = [j == 0 for i, j, k in lattice]
        if face_no == 2:
            tests = [i + j + k == 3 for i, j, k in lattice]
        if face_no == 3:
            tests = [i == 0 for i, j, k in lattice]
        chosen = [node_no for node_no in range(20) if tests[node_no]]
        for row_no in range(20):
            columns[row_no].extend([face_mass[row_no][col_no] for col_no in chosen])
        index_list.extend(chosen)
    lift_mat = solve_linear(mass_mat, columns)
    return (deriv_mats, lift_mat, index_list)

def cross_product(left, right):
    return jnp.stack([left[1] * right[2] - left[2] * right[1], left[2] * right[0] - left[0] * right[2], left[0] * right[1] - left[1] * right[0]])

def curl_of(gradient, offset):
    return jnp.stack([gradient[1, offset + 2] - gradient[2, offset + 1], gradient[2, offset] - gradient[0, offset + 2], gradient[0, offset + 1] - gradient[1, offset]])

def element_rhs(fields, neighbour, eps_inf, eps_delta, relax_time, metric, face_scale, face_angles):
    highest = lax.Precision.HIGHEST
    deriv_table, lift_table, face_index = reference_element()
    deriv_mats = jnp.asarray(deriv_table, dtype=jnp.float32)
    lift_mat = jnp.asarray(lift_table, dtype=jnp.float32)
    face_rows = jnp.asarray(face_index, dtype=jnp.int32)
    elements = fields.shape[-1]
    traces = fields[0:6][:, face_rows, :]
    jump_e = traces[0:3] - neighbour[0:3]
    jump_h = traces[3:6] - neighbour[3:6]
    polar_angle = face_angles[0]
    azimuth = face_angles[1]
    normal = jnp.stack([jnp.sin(polar_angle) * jnp.cos(azimuth), jnp.sin(polar_angle) * jnp.sin(azimuth), jnp.cos(polar_angle)])
    normal = jnp.repeat(normal, 10, axis=1)
    scale_rows = jnp.repeat(face_scale, 10, axis=0)
    normal_e = lax.optimization_barrier(jnp.sum(normal * jump_e, axis=0))
    normal_h = lax.optimization_barrier(jnp.sum(normal * jump_h, axis=0))
    flux_e = normal * normal_e - jump_e - cross_product(normal, jump_h)
    flux_h = cross_product(normal, jump_e) + normal * normal_h - jump_h
    face_flux = jnp.concatenate([flux_e, flux_h]) * (0.5 * scale_rows)
    lifted = jnp.einsum('nf,cfk->cnk', lift_mat, face_flux, precision=highest)
    derived = jnp.einsum('dij,cjk->dcik', deriv_mats, fields[0:6], precision=highest)
    gradient = jnp.einsum('dik,dcnk->icnk', metric.reshape(3, 3, elements), derived, precision=highest)
    current = (eps_delta * fields[0:3] - fields[6:9]) / relax_time
    rhs_e = (curl_of(gradient, 3) + lifted[0:3] - current) / eps_inf
    rhs_h = lifted[3:6] - curl_of(gradient, 0)
    return jnp.concatenate([rhs_e, rhs_h, current])

def neighbour_rows(nbr_index, dom_export, sub_export):
    devices = N_DOM * N_SUB
    rows = 40 * K_DEV
    local = nbr_index.reshape(40, devices, K_DEV)
    device = jnp.arange(devices, dtype=jnp.int32)[None, :, None]
    dom_pos = device // N_SUB
    sub_pos = device % N_SUB
    own_rows = device * rows + local
    sub_off = jnp.clip(local - rows, 0, SUB_ROWS - 1)
    source = sub_off // XSP
    place = sub_off % XSP
    sender = dom_pos * N_SUB + source
    sub_rows = sender * rows + sub_export[sender, sub_pos, place]
    rim = local - rows - SUB_ROWS
    pairs = dom_export.reshape(devices, 2 * XR)
    lower_dev = jnp.clip(dom_pos - 1, 0, N_DOM - 1) * N_SUB + sub_pos
    upper_dev = jnp.clip(dom_pos + 1, 0, N_DOM - 1) * N_SUB + sub_pos
    lower_rows = lower_dev * rows + pairs[lower_dev, XR + jnp.clip(rim, 0, XR - 1)]
    upper_rows = upper_dev * rows + pairs[upper_dev, jnp.clip(rim - 3 * XR, 0, XR - 1)]
    empty_row = devices * rows
    lower_rows = jnp.where(dom_pos > 0, lower_rows, empty_row)
    upper_rows = jnp.where(dom_pos < N_DOM - 1, upper_rows, empty_row)
    result = jnp.where(local < rows, own_rows, jnp.where(local < rows + SUB_ROWS, sub_rows, jnp.where(rim < XR, lower_rows, upper_rows)))
    return result.reshape(-1).astype(jnp.int32)

def reference(field_state, adjoint, eps_inf, eps_delta, relax_time, metric, face_scale, face_angles, nbr_index, dom_export, sub_export, send_slot, recv_index):
    devices = N_DOM * N_SUB
    gather_rows = neighbour_rows(nbr_index, dom_export, sub_export)
    face_rows = jnp.asarray(reference_element()[2], dtype=jnp.int32)

    def operator(values, e_inf, e_del, tau):
        traces = values[0:6][:, face_rows, :].reshape(6, 40, devices, K_DEV)
        table = jnp.transpose(traces, (0, 2, 1, 3)).reshape(6, devices * 40 * K_DEV)
        table = jnp.concatenate([table, jnp.zeros((6, 1), values.dtype)], axis=1)
        neighbour = table[:, gather_rows].reshape(6, 40, NE)
        return element_rhs(values, neighbour, e_inf, e_del, tau, metric, face_scale, face_angles)

    def advance(fields, e_inf, e_del, tau):
        slope_one = operator(fields, e_inf, e_del, tau)
        slope_two = operator(fields + 0.5 * time_step * slope_one, e_inf, e_del, tau)
        slope_three = operator(fields + 0.5 * time_step * slope_two, e_inf, e_del, tau)
        slope_four = operator(fields + time_step * slope_three, e_inf, e_del, tau)
        return fields + time_step / 6.0 * (slope_one + 2.0 * slope_two + 2.0 * slope_three + slope_four)
    _, pullback = jax.vjp(advance, field_state, eps_inf, eps_delta, relax_time)
    adjoint_out, grad_inf, grad_delta, grad_tau = pullback(adjoint)
    source_dev = jnp.arange(NE, dtype=jnp.int32) // K_DEV
    target = send_slot // CAP
    slot_no = send_slot % CAP
    owner = target * KT + recv_index[target, source_dev, slot_no]
    stacked = jnp.stack([grad_inf, grad_delta, grad_tau])
    thermal_grad = jax.ops.segment_sum(stacked.T, owner, num_segments=NT).T
    return (adjoint_out, thermal_grad)
```

```python
import math

import jax
import jax.numpy as jnp
import numpy as np
from jax import lax
from jax.experimental import pallas as pl
from jax.experimental.pallas import tpu as pltpu
from jax.sharding import PartitionSpec as P

time_step = 0.014
f32 = jnp.float32
bf16 = jnp.bfloat16
NODES = 20
ROWS = 24
FACE = 40
DOMS = 32
SUBS = 4
BLOCKS = 6
MESH = pl.DeviceIdType.MESH


def mat_mul(left, right):
    inner = len(right)
    return [
        [
            sum((left[row_no][k] * right[k][col_no] for k in range(inner)))
            for col_no in range(len(right[0]))
        ]
        for row_no in range(len(left))
    ]


def transposed(matrix):
    return [list(column) for column in zip(*matrix)]


def solve_linear(matrix, rhs_rows):
    order = len(matrix)
    work = [list(matrix[row_no]) + list(rhs_rows[row_no]) for row_no in range(order)]
    for col_no in range(order):

        def magnitude(row_no):
            return abs(work[row_no][col_no])

        pivot = max(range(col_no, order), key=magnitude)
        work[col_no], work[pivot] = (work[pivot], work[col_no])
        head = work[col_no][col_no]
        work[col_no] = [value / head for value in work[col_no]]
        for row_no in range(order):
            if row_no != col_no:
                factor = work[row_no][col_no]
                work[row_no] = [
                    value - factor * other for value, other in zip(work[row_no], work[col_no])
                ]
    return [row[order:] for row in work]


def reference_element():
    lattice = [(i, j, k) for k in range(4) for j in range(4 - k) for i in range(4 - j - k)]
    points = [[float(v) / 3.0 for v in node] for node in lattice]
    vander = [[0.0] * 20 for node_no in range(20)]
    slopes = [[[0.0] * 20 for node_no in range(20)] for axis_no in range(3)]
    for node_no in range(20):
        for mono_no in range(20):
            power = lattice[mono_no]
            value = 1.0
            for axis_no in range(3):
                value *= points[node_no][axis_no] ** power[axis_no]
            vander[node_no][mono_no] = value
            for axis_no in range(3):
                if power[axis_no] > 0:
                    term = float(power[axis_no])
                    for other_no in range(3):
                        expo_val = power[other_no] - (1 if other_no == axis_no else 0)
                        term *= points[node_no][other_no] ** expo_val
                    slopes[axis_no][node_no][mono_no] = term
    identity = [[1.0 if row_no == col_no else 0.0 for col_no in range(20)] for row_no in range(20)]
    inverse = solve_linear(vander, identity)
    deriv_mats = [mat_mul(slopes[axis_no], inverse) for axis_no in range(3)]
    fact = math.factorial

    def face_integral(face_no, a, b, c):
        if face_no == 0:
            return 0.0 if c > 0 else fact(a) * fact(b) / fact(a + b + 2)
        if face_no == 1:
            return 0.0 if b > 0 else fact(a) * fact(c) / fact(a + c + 2)
        if face_no == 2:
            return math.sqrt(3.0) * fact(a) * fact(b) * fact(c) / fact(a + b + c + 2)
        return 0.0 if a > 0 else fact(b) * fact(c) / fact(b + c + 2)

    inverse_t = transposed(inverse)
    mono_mass = [[0.0] * 20 for node_no in range(20)]
    for first_no in range(20):
        for second_no in range(20):
            a = lattice[first_no][0] + lattice[second_no][0]
            b = lattice[first_no][1] + lattice[second_no][1]
            c = lattice[first_no][2] + lattice[second_no][2]
            mono_mass[first_no][second_no] = fact(a) * fact(b) * fact(c) / fact(a + b + c + 3)
    mass_mat = mat_mul(mat_mul(inverse_t, mono_mass), inverse)
    columns = [[] for node_no in range(20)]
    index_list = []
    for face_no in range(4):
        mono_face = [[0.0] * 20 for node_no in range(20)]
        for first_no in range(20):
            for second_no in range(20):
                a = lattice[first_no][0] + lattice[second_no][0]
                b = lattice[first_no][1] + lattice[second_no][1]
                c = lattice[first_no][2] + lattice[second_no][2]
                mono_face[first_no][second_no] = face_integral(face_no, a, b, c)
        face_mass = mat_mul(mat_mul(inverse_t, mono_face), inverse)
        tests = [k == 0 for i, j, k in lattice]
        if face_no == 1:
            tests = [j == 0 for i, j, k in lattice]
        if face_no == 2:
            tests = [i + j + k == 3 for i, j, k in lattice]
        if face_no == 3:
            tests = [i == 0 for i, j, k in lattice]
        chosen = [node_no for node_no in range(20) if tests[node_no]]
        for row_no in range(20):
            columns[row_no].extend([face_mass[row_no][col_no] for col_no in chosen])
        index_list.extend(chosen)
    lift_mat = solve_linear(mass_mat, columns)
    return (deriv_mats, lift_mat, index_list)


def host_tables():
    deriv, lift, faces = reference_element()
    deriv = np.asarray(deriv, np.float32)
    lift = np.asarray(lift, np.float32)
    pick = np.zeros((NODES, FACE), np.float32)
    pick[np.asarray(faces), np.arange(FACE)] = 1.0

    def placed(rows, cols, parts):
        result = np.zeros((rows, cols), np.float32)
        for at, part in parts:
            result[: part.shape[0], at : at + part.shape[1]] = part
        return result

    forward = placed(ROWS, 112, [(0, lift)] + [(40 + 24 * d, deriv[d]) for d in range(3)])
    backward = placed(ROWS, 112, [(0, pick)] + [(40 + 24 * d, deriv[d].T) for d in range(3)])
    lift_t = placed(FACE, ROWS, [(0, lift.T)])
    pick_t = placed(FACE, ROWS, [(0, pick.T)])

    def split(matrix):
        high = matrix.astype(jnp.bfloat16).astype(np.float32)
        low = matrix - high
        return np.concatenate(
            [np.concatenate([high, high], 1), np.concatenate([low, np.zeros_like(low)], 1)], 0
        )

    table = np.zeros((224, 256), np.float32)
    table[0:48, 0:224] = split(forward)
    table[48:96, 0:224] = split(backward)
    table[96:176, 0:48] = split(lift_t)
    table[176:216, 0:48] = np.concatenate([pick_t, pick_t], 1)
    return table.astype(jnp.bfloat16), [int(v) for v in faces]


def stacked(values):
    high = values.astype(bf16).astype(f32)
    return jnp.concatenate([high, values - high], axis=0).astype(bf16)


def parts3(values):
    first = values.astype(bf16)
    rest = values - first.astype(f32)
    second = rest.astype(bf16)
    third = (rest - second.astype(f32)).astype(bf16)
    return first, second, third


def dot(left, right):
    return jnp.dot(left, right, preferred_element_type=f32)


def node_of(rows, faces):
    result = rows - 20
    for row, node in enumerate(faces):
        result = jnp.where(rows == row, node, result)
    return result


def one_hot(condition):
    return jnp.where(condition, 1.0, 0.0).astype(bf16)


def kernel_of(faces):
    def kernel(
        fs, adj, einf, edel, tau, met, fsc, ang, nbr, dexp, sexp, sslot, recv, tab,
        out, therm,
        y, k, w, adj24, acc, nrm, scl, x, p, nb, cd, s_ref, pool, pp, nodes, nodex,
        a_mat, at_mat, ax, axt, b_mat, bx,
        sf, rf, sb, rb, ya, yr, cb, rc,
        fs_sem, fr_sem, bs_sem, br_sem, ps_sem, pr_sem, qs_sem, qr_sem,
    ):
        dom = lax.axis_index("dom")
        sub = lax.axis_index("sub")

        rf[...] = jnp.zeros_like(rf)
        rb[...] = jnp.zeros_like(rb)
        yr[...] = jnp.zeros_like(yr)
        rc[...] = jnp.zeros_like(rc)
        barrier = pltpu.get_barrier_semaphore()
        for step in range(1, SUBS):
            pl.semaphore_signal(
                barrier, inc=1, device_id=(dom, lax.rem(sub + step, SUBS)), device_id_type=MESH
            )

        def greet(step, carry):
            pl.semaphore_signal(
                barrier, inc=1, device_id=(lax.rem(dom + step, DOMS), sub), device_id_type=MESH
            )
            return carry

        lax.fori_loop(1, DOMS, greet, 0)

        ie = 1.0 / einf[...]
        it = 1.0 / tau[...]
        ed = edel[...]
        pad = jnp.zeros((ROWS - NODES, 256), f32)
        for c in range(9):
            y[0, c] = jnp.concatenate([fs[c], pad], axis=0)
            value = jnp.concatenate([adj[c], pad], axis=0)
            adj24[c] = value
            acc[c] = value
            w[0, c] = (time_step / 6.0) * value
        sin_a = jnp.sin(ang[0])
        normals = (sin_a * jnp.cos(ang[1]), sin_a * jnp.sin(ang[1]), jnp.cos(ang[0]))
        for face in range(4):
            here = slice(10 * face, 10 * face + 10)
            for i in range(3):
                nrm[i, here, :] = jnp.broadcast_to(normals[i][face : face + 1], (10, 256))
            scl[here, :] = jnp.broadcast_to(0.5 * fsc[face : face + 1, :], (10, 256))

        exported = jnp.concatenate([sexp[0], dexp[...], jnp.zeros((2, 128), jnp.int32)], axis=0)
        nodex[...] = node_of(exported >> 8, faces)
        export_el = exported & 255
        export_cols = jnp.transpose(export_el)
        row_iota = lax.broadcasted_iota(jnp.int32, (256, 128), 0)
        lane_iota = lax.broadcasted_iota(jnp.int32, (128, 256), 1)
        for blk in range(BLOCKS):
            here = slice(128 * blk, 128 * blk + 128)
            ax[:, here] = one_hot(row_iota == export_el[blk : blk + 1])
            axt[here, :] = one_hot(lane_iota == export_cols[:, blk : blk + 1])

        def sub_copy(r, src, dst, send, recv_s, to, slot_from):
            return pltpu.make_async_remote_copy(
                src_ref=src.at[r, to],
                dst_ref=dst.at[r, slot_from],
                send_sem=send.at[r, to],
                recv_sem=recv_s.at[r, slot_from],
                device_id=(dom, to),
                device_id_type=MESH,
            )

        def dom_copy(r, src, dst, send, recv_s, block, slot, to):
            return pltpu.make_async_remote_copy(
                src_ref=src.at[r, block],
                dst_ref=dst.at[r, slot],
                send_sem=send.at[r, block],
                recv_sem=recv_s.at[r, slot],
                device_id=(to, sub),
                device_id_type=MESH,
            )

        has_low = dom > 0
        has_high = dom < DOMS - 1

        def start_all(r, src, dst, send, recv_s):
            for step in range(1, SUBS):
                to = lax.rem(sub + step, SUBS)
                sub_copy(r, src, dst, send, recv_s, to, sub).start()

            @pl.when(has_low)
            def _():
                dom_copy(r, src, dst, send, recv_s, 4, 5, dom - 1).start()

            @pl.when(has_high)
            def _():
                dom_copy(r, src, dst, send, recv_s, 5, 4, dom + 1).start()

        def wait_recv_all(r, src, dst, send, recv_s):
            for step in range(1, SUBS):
                other = lax.rem(sub + step, SUBS)
                sub_copy(r, src, dst, send, recv_s, other, other).wait_recv()

            @pl.when(has_low)
            def _():
                dom_copy(r, src, dst, send, recv_s, 4, 4, dom - 1).wait_recv()

            @pl.when(has_high)
            def _():
                dom_copy(r, src, dst, send, recv_s, 5, 5, dom + 1).wait_recv()

        def wait_send_all(r, src, dst, send, recv_s):
            for step in range(1, SUBS):
                to = lax.rem(sub + step, SUBS)
                sub_copy(r, src, dst, send, recv_s, to, sub).wait_send()

            @pl.when(has_low)
            def _():
                dom_copy(r, src, dst, send, recv_s, 4, 5, dom - 1).wait_send()

            @pl.when(has_high)
            def _():
                dom_copy(r, src, dst, send, recv_s, 5, 4, dom + 1).wait_send()

        fwd = (sf, rf, fs_sem, fr_sem)
        bwd = (sb, rb, bs_sem, br_sem)

        node_iota = lax.broadcasted_iota(jnp.int32, (ROWS, 128), 0)
        node_iota2 = lax.broadcasted_iota(jnp.int32, (ROWS, 256), 0)
        own_rows = node_iota2 < NODES

        def fold_pool():
            values = pool[...].reshape(6 * ROWS, 256)
            high = values.astype(bf16)
            pp[0:144, :] = high
            pp[144:288, :] = (values - high.astype(f32)).astype(bf16)

        def exports(r):
            for c in range(6):
                pool[c] = y[r, c]
            fold_pool()
            for blk in range(BLOCKS):
                got = dot(pp[...], ax[:, 128 * blk : 128 * blk + 128])
                got = got[:144] + got[144:]
                keep = node_iota == nodex[blk : blk + 1, :]
                for c in range(6):
                    sf[r, blk, c : c + 1, :] = jnp.sum(
                        jnp.where(keep, got[24 * c : 24 * c + 24], 0.0), axis=0, keepdims=True
                    )
            start_all(r, *fwd)

        def flux_rows(src, at):
            here = slice(at, at + 8)
            n = [nrm[i, here, :] for i in range(3)]
            e = [src[i, here, :] for i in range(3)]
            h = [src[3 + i, here, :] for i in range(3)]
            ne = n[0] * e[0] + n[1] * e[1] + n[2] * e[2]
            nh = n[0] * h[0] + n[1] * h[1] + n[2] * h[2]
            result = []
            for i in range(3):
                j, l = (i + 1) % 3, (i + 2) % 3
                result.append(n[i] * ne - e[i] - (n[j] * h[l] - n[l] * h[j]))
            for i in range(3):
                j, l = (i + 1) % 3, (i + 2) % 3
                result.append((n[j] * e[l] - n[l] * e[j]) + n[i] * nh - h[i])
            return result

        def curl_rows(e, h):
            for d in range(3):
                m = [met[3 * d + i : 3 * d + i + 1, :] for i in range(3)]
                here = slice(40 + 24 * d, 64 + 24 * d)
                for i in range(3):
                    j, l = (i + 1) % 3, (i + 2) % 3
                    x[i, here, :] = m[j] * h[l] - m[l] * h[j]
                    x[3 + i, here, :] = m[l] * e[j] - m[j] * e[l]

        def contracted(first, c):
            got = dot(tab[first : first + 48, 0:224], stacked(x[c]))
            return got[:24] + got[24:]

        def back_faces(r):
            for c in range(6):
                value = w[r, c]
                if c < 3:
                    value = value * ie
                got = dot(tab[96:176, 0:48], stacked(value))
                p[c] = (got[:40] + got[40:]) * scl[...]
            for at in range(0, FACE, 8):
                for c, value in enumerate(flux_rows(p, at)):
                    cd[c, at : at + 8, :] = value

            def group(g, carry):
                for j in range(8):
                    fn = g * 8 + j
                    keep = node_iota2 == nodes[pl.ds(fn, 1), :]
                    high, low = [], []
                    for c in range(6):
                        value = cd[c, pl.ds(fn, 1), :]
                        top = value.astype(bf16).astype(f32)
                        high.append(jnp.where(keep, top, 0.0))
                        low.append(jnp.where(keep, value - top, 0.0))
                    b_mat[:, 256 * j : 256 * j + 256] = jnp.concatenate(high + low, 0).astype(bf16)
                got = dot(b_mat[...], at_mat[pl.ds(pl.multiple_of(g * 2048, 2048), 2048), :])
                s_ref[...] = s_ref[...] - (got[:144] + got[144:])
                return carry

            s_ref[...] = jnp.zeros_like(s_ref)
            lax.fori_loop(0, FACE // 8, group, 0)
            for c in range(6):
                rows = s_ref[24 * c + 20 : 24 * c + 24, :]
                for blk in range(4):
                    at = 128 * (blk % 2)
                    sb[r, blk, c : c + 1, :] = rows[blk // 2 : blk // 2 + 1, at : at + 128]
                sb[r, 4, c : c + 1, :] = rows[2:3, 0:128]
                sb[r, 5, c : c + 1, :] = rows[3:4, 128:256]
            start_all(r, *bwd)

        def arrived(r, blk, dst, src):
            value = dst[r, blk]
            if blk < SUBS:
                value = jnp.where(sub == blk, src[r, blk], value)
            return value

        def forward(r):
            wait_recv_all(r, *fwd)
            for blk in range(4):
                value = arrived(r, blk, rf, sf)
                at = 128 * (blk % 2)
                for c in range(6):
                    row = 20 + blk // 2
                    pool[c, row : row + 1, at : at + 128] = value[c : c + 1]
            low, high = rf[r, 4], rf[r, 5]
            for c in range(6):
                pool[c, 22:23, 0:128] = low[c : c + 1]
                pool[c, 23:24, 128:256] = high[c : c + 1]
            fold_pool()

            def group(g, carry):
                for j in range(8):
                    fn = g * 8 + j
                    keep = node_iota2 == nodes[pl.ds(fn, 1), :]
                    got = dot(pp[...], a_mat[fn])
                    got = got[:144] + got[144:]
                    for c in range(6):
                        nb[c, pl.ds(fn, 1), :] = jnp.sum(
                            jnp.where(keep, got[24 * c : 24 * c + 24], 0.0), axis=0, keepdims=True
                        )
                return carry

            lax.fori_loop(0, FACE // 8, group, 0)
            for c in range(6):
                p[c] = dot(tab[176:216, 0:48], stacked(y[r, c])) - nb[c]
            for at in range(0, FACE, 8):
                factor = scl[at : at + 8, :]
                for c, value in enumerate(flux_rows(p, at)):
                    x[c, at : at + 8, :] = value * factor
            curl_rows([y[r, c] for c in range(3)], [y[r, 3 + c] for c in range(3)])
            for c in range(3):
                current = (ed * y[r, c] - y[r, 6 + c]) * it
                k[r, 6 + c] = current
                k[r, c] = (contracted(0, c) - current) * ie
                k[r, 3 + c] = contracted(0, 3 + c)

        def back_volume(r):
            for c in range(6):
                x[c, 0:40, :] = cd[c]
            curl_rows([w[r, c] * ie for c in range(3)], [w[r, 3 + c] for c in range(3)])
            wait_recv_all(r, *bwd)
            for blk in range(BLOCKS):
                value = arrived(r, blk, rb, sb)
                keep = node_iota == nodex[blk : blk + 1, :]
                top = value.astype(bf16).astype(f32)
                rest = value - top
                high = [jnp.where(keep, top[c : c + 1], 0.0) for c in range(6)]
                low = [jnp.where(keep, rest[c : c + 1], 0.0) for c in range(6)]
                bx[:, 128 * blk : 128 * blk + 128] = jnp.concatenate(high + low, 0).astype(bf16)
            got = dot(bx[...], axt[...])
            s_ref[...] = s_ref[...] + (got[:144] + got[144:])
            cots = []
            for c in range(6):
                value = contracted(48, c) + s_ref[24 * c : 24 * c + 24, :]
                cots.append(jnp.where(own_rows, value, 0.0))
            for c in range(3):
                through = (w[r, 6 + c] - w[r, c] * ie) * it
                cots[c] = cots[c] + ed * through
                cots.append(-through)
            return cots

        def one_round(r, ahead, adj_part, back_part):
            back_faces(r)
            forward(r)
            for c in range(9):
                y[r + 1, c] = y[0, c] + ahead * k[r, c]
            exports(r + 1)
            for c, value in enumerate(back_volume(r)):
                acc[c] = acc[c] + value
                w[r + 1, c] = adj_part * adj24[c] + back_part * value

        pl.semaphore_wait(barrier, SUBS - 1 + DOMS - 1)
        exports(0)
        index = nbr[...]
        nodes[...] = node_of(index >> 8, faces)
        element = index & 255
        columns = jnp.transpose(element)
        lane_iota2 = lax.broadcasted_iota(jnp.int32, (256, 256), 1)
        row_iota2 = lax.broadcasted_iota(jnp.int32, (256, 256), 0)
        for fn in range(FACE):
            at_mat[256 * fn : 256 * fn + 256, :] = one_hot(lane_iota2 == columns[:, fn : fn + 1])
            a_mat[fn] = one_hot(row_iota2 == element[fn : fn + 1])

        def looped(r, carry):
            last = r == 2
            one_round(
                r,
                jnp.where(last, time_step, 0.5 * time_step),
                jnp.where(last, time_step / 6.0, time_step / 3.0),
                jnp.where(r == 0, time_step, 0.5 * time_step),
            )
            return carry

        lax.fori_loop(0, 3, looped, 0)
        back_faces(3)
        forward(3)

        sums = [jnp.zeros((ROWS, 256), f32) for _ in range(3)]
        for r in range(4):
            for c in range(3):
                through = w[3 - r, 6 + c] - w[3 - r, c] * ie
                sums[0] = sums[0] - w[3 - r, c] * k[r, c]
                sums[1] = sums[1] + through * y[r, c]
                sums[2] = sums[2] - through * k[r, 6 + c]
        grads = [
            jnp.sum(value, axis=0, keepdims=True) * factor
            for value, factor in zip(sums, (ie, it, it))
        ]
        slot = sslot[...]
        target = ((slot >> 1) & 3) * DOMS + (slot >> 3)
        chosen = one_hot(lax.broadcasted_iota(jnp.int32, (128, 256), 0) == target)
        lines = [jnp.where((slot & 1) == q, g, 0.0) for q in range(2) for g in grads]
        lines = jnp.concatenate(lines + [jnp.zeros((2, 256), f32)], axis=0)
        lines = [jnp.where(sub == q, lines, 0.0) for q in range(SUBS)]
        lines = jnp.concatenate(lines + [jnp.zeros((96, 256), f32)], axis=0)
        packed = sum(dot(chosen, part) for part in parts3(jnp.transpose(lines)))
        for q in range(SUBS):
            ya[q] = packed[DOMS * q : DOMS * q + DOMS]

        def first_hop(to, slot_from):
            return pltpu.make_async_remote_copy(
                src_ref=ya.at[to],
                dst_ref=yr.at[slot_from],
                send_sem=ps_sem.at[to],
                recv_sem=pr_sem.at[slot_from],
                device_id=(dom, to),
                device_id_type=MESH,
            )

        for step in range(1, SUBS):
            first_hop(lax.rem(sub + step, SUBS), sub).start()
        for step in range(1, SUBS):
            other = lax.rem(sub + step, SUBS)
            first_hop(other, other).wait_recv()
        mine = ya[pl.ds(sub, 1)][0] + yr[0] + yr[1] + yr[2] + yr[3]
        for q in range(DOMS):
            cb[q] = mine[q : q + 1]

        def second_hop(to, slot_from):
            return pltpu.make_async_remote_copy(
                src_ref=cb.at[to],
                dst_ref=rc.at[slot_from],
                send_sem=qs_sem.at[to],
                recv_sem=qr_sem.at[slot_from],
                device_id=(to, sub),
                device_id_type=MESH,
            )

        def hop_start(step, carry):
            second_hop(lax.rem(dom + step, DOMS), dom).start()
            return carry

        def hop_wait(step, carry):
            other = lax.rem(dom + step, DOMS)
            second_hop(other, other).wait_recv()
            return carry

        def hop_sent(step, carry):
            second_hop(lax.rem(dom + step, DOMS), dom).wait_send()
            return carry

        lax.fori_loop(1, DOMS, hop_start, 0)

        for c, value in enumerate(back_volume(3)):
            out[c] = (acc[c] + value)[:NODES]

        lax.fori_loop(1, DOMS, hop_wait, 0)
        here = lax.broadcasted_iota(jnp.int32, (DOMS, 128), 0) == dom
        came = jnp.concatenate([rc[q] for q in range(DOMS)], axis=0)
        came = came + jnp.where(here, mine, 0.0)
        turned = parts3(jnp.transpose(came)[:32])
        lanes = lax.broadcasted_iota(jnp.int32, (DOMS, 128), 1)
        total = jnp.zeros((3, 128), f32)
        for q in range(SUBS):
            ids = recv[:, 2 * q : 2 * q + 2]
            for z in range(2):
                owner = one_hot(lanes == ids[:, z : z + 1])
                at = 8 * q + 3 * z
                for part in turned:
                    total = total + dot(part, owner)[at : at + 3]
        therm[...] = total[:, :64]

        for r in range(4):
            wait_send_all(r, *fwd)
            wait_send_all(r, *bwd)
        for step in range(1, SUBS):
            first_hop(lax.rem(sub + step, SUBS), sub).wait_send()
        lax.fori_loop(1, DOMS, hop_sent, 0)

    return kernel


def per_device(
    field_state,
    adjoint,
    eps_inf,
    eps_delta,
    relax_time,
    metric,
    face_scale,
    face_angles,
    nbr_index,
    dom_export,
    sub_export,
    send_slot,
    recv_index,
):
    table, faces = host_tables()
    stage = pltpu.VMEM((4, 9, ROWS, 256), f32)
    trace = pltpu.VMEM((6, FACE, 256), f32)
    message = pltpu.VMEM((4, BLOCKS, 8, 128), f32)
    semaphores = pltpu.SemaphoreType.DMA((4, BLOCKS))
    state = pltpu.VMEM((9, ROWS, 256), f32)
    scratch = [
        stage, stage, stage, state, state,
        pltpu.VMEM((3, FACE, 256), f32),
        pltpu.VMEM((FACE, 256), f32),
        pltpu.VMEM((6, 112, 256), f32),
        trace, trace, trace,
        pltpu.VMEM((6 * ROWS, 256), f32),
        pltpu.VMEM((6, ROWS, 256), f32),
        pltpu.VMEM((12 * ROWS, 256), bf16),
        pltpu.VMEM((FACE, 256), jnp.int32),
        pltpu.VMEM((8, 128), jnp.int32),
        pltpu.VMEM((FACE, 256, 256), bf16),
        pltpu.VMEM((FACE * 256, 256), bf16),
        pltpu.VMEM((256, 128 * BLOCKS), bf16),
        pltpu.VMEM((128 * BLOCKS, 256), bf16),
        pltpu.VMEM((12 * ROWS, 2048), bf16),
        pltpu.VMEM((12 * ROWS, 128 * BLOCKS), bf16),
        message, message, message, message,
        pltpu.VMEM((SUBS, DOMS, 128), f32),
        pltpu.VMEM((SUBS, DOMS, 128), f32),
        pltpu.VMEM((DOMS, 1, 128), f32),
        pltpu.VMEM((DOMS, 1, 128), f32),
        semaphores, semaphores, semaphores, semaphores,
        pltpu.SemaphoreType.DMA((SUBS,)),
        pltpu.SemaphoreType.DMA((SUBS,)),
        pltpu.SemaphoreType.DMA((DOMS,)),
        pltpu.SemaphoreType.DMA((DOMS,)),
    ]
    call = pl.pallas_call(
        kernel_of(faces),
        out_shape=(
            jax.ShapeDtypeStruct((9, NODES, 256), f32),
            jax.ShapeDtypeStruct((3, 64), f32),
        ),
        in_specs=[pl.BlockSpec(memory_space=pltpu.VMEM)] * 14,
        out_specs=(
            pl.BlockSpec(memory_space=pltpu.VMEM),
            pl.BlockSpec(memory_space=pltpu.VMEM),
        ),
        scratch_shapes=scratch,
        compiler_params=pltpu.CompilerParams(
            collective_id=0, has_side_effects=True, vmem_limit_bytes=48 << 20
        ),
        name="reverse_step",
    )
    return call(
        field_state,
        adjoint,
        eps_inf.reshape(1, 256),
        eps_delta.reshape(1, 256),
        relax_time.reshape(1, 256),
        metric,
        face_scale,
        face_angles,
        nbr_index,
        dom_export.reshape(2, 128),
        sub_export,
        send_slot.reshape(1, 256),
        recv_index.reshape(32, 8),
        jnp.asarray(table),
    )


def solution(mesh):
    both = ("dom", "sub")
    return jax.shard_map(
        per_device,
        mesh=mesh,
        in_specs=(
            P(None, None, both),
            P(None, None, both),
            P(both),
            P(both),
            P(both),
            P(None, both),
            P(None, both),
            P(None, None, both),
            P(None, both),
            P(both),
            P(both, None, None),
            P(both),
            P(both, None, None),
        ),
        out_specs=(P(None, None, both), P(None, both)),
        check_vma=False,
    )
```

```python
import math

import jax
import jax.numpy as jnp
import numpy as np
from jax import lax
from jax.experimental import pallas as pl
from jax.experimental.pallas import tpu as pltpu
from jax.sharding import PartitionSpec as P

time_step = 0.014
f32 = jnp.float32
bf16 = jnp.bfloat16
NODES = 20
ROWS = 24
FACE = 40
DOMS = 32
SUBS = 4
BLOCKS = 6
MESH = pl.DeviceIdType.MESH


def mat_mul(left, right):
    inner = len(right)
    return [
        [
            sum((left[row_no][k] * right[k][col_no] for k in range(inner)))
            for col_no in range(len(right[0]))
        ]
        for row_no in range(len(left))
    ]


def transposed(matrix):
    return [list(column) for column in zip(*matrix)]


def solve_linear(matrix, rhs_rows):
    order = len(matrix)
    work = [list(matrix[row_no]) + list(rhs_rows[row_no]) for row_no in range(order)]
    for col_no in range(order):

        def magnitude(row_no):
            return abs(work[row_no][col_no])

        pivot = max(range(col_no, order), key=magnitude)
        work[col_no], work[pivot] = (work[pivot], work[col_no])
        head = work[col_no][col_no]
        work[col_no] = [value / head for value in work[col_no]]
        for row_no in range(order):
            if row_no != col_no:
                factor = work[row_no][col_no]
                work[row_no] = [
                    value - factor * other for value, other in zip(work[row_no], work[col_no])
                ]
    return [row[order:] for row in work]


def reference_element():
    lattice = [(i, j, k) for k in range(4) for j in range(4 - k) for i in range(4 - j - k)]
    points = [[float(v) / 3.0 for v in node] for node in lattice]
    vander = [[0.0] * 20 for node_no in range(20)]
    slopes = [[[0.0] * 20 for node_no in range(20)] for axis_no in range(3)]
    for node_no in range(20):
        for mono_no in range(20):
            power = lattice[mono_no]
            value = 1.0
            for axis_no in range(3):
                value *= points[node_no][axis_no] ** power[axis_no]
            vander[node_no][mono_no] = value
            for axis_no in range(3):
                if power[axis_no] > 0:
                    term = float(power[axis_no])
                    for other_no in range(3):
                        expo_val = power[other_no] - (1 if other_no == axis_no else 0)
                        term *= points[node_no][other_no] ** expo_val
                    slopes[axis_no][node_no][mono_no] = term
    identity = [[1.0 if row_no == col_no else 0.0 for col_no in range(20)] for row_no in range(20)]
    inverse = solve_linear(vander, identity)
    deriv_mats = [mat_mul(slopes[axis_no], inverse) for axis_no in range(3)]
    fact = math.factorial

    def face_integral(face_no, a, b, c):
        if face_no == 0:
            return 0.0 if c > 0 else fact(a) * fact(b) / fact(a + b + 2)
        if face_no == 1:
            return 0.0 if b > 0 else fact(a) * fact(c) / fact(a + c + 2)
        if face_no == 2:
            return math.sqrt(3.0) * fact(a) * fact(b) * fact(c) / fact(a + b + c + 2)
        return 0.0 if a > 0 else fact(b) * fact(c) / fact(b + c + 2)

    inverse_t = transposed(inverse)
    mono_mass = [[0.0] * 20 for node_no in range(20)]
    for first_no in range(20):
        for second_no in range(20):
            a = lattice[first_no][0] + lattice[second_no][0]
            b = lattice[first_no][1] + lattice[second_no][1]
            c = lattice[first_no][2] + lattice[second_no][2]
            mono_mass[first_no][second_no] = fact(a) * fact(b) * fact(c) / fact(a + b + c + 3)
    mass_mat = mat_mul(mat_mul(inverse_t, mono_mass), inverse)
    columns = [[] for node_no in range(20)]
    index_list = []
    for face_no in range(4):
        mono_face = [[0.0] * 20 for node_no in range(20)]
        for first_no in range(20):
            for second_no in range(20):
                a = lattice[first_no][0] + lattice[second_no][0]
                b = lattice[first_no][1] + lattice[second_no][1]
                c = lattice[first_no][2] + lattice[second_no][2]
                mono_face[first_no][second_no] = face_integral(face_no, a, b, c)
        face_mass = mat_mul(mat_mul(inverse_t, mono_face), inverse)
        tests = [k == 0 for i, j, k in lattice]
        if face_no == 1:
            tests = [j == 0 for i, j, k in lattice]
        if face_no == 2:
            tests = [i + j + k == 3 for i, j, k in lattice]
        if face_no == 3:
            tests = [i == 0 for i, j, k in lattice]
        chosen = [node_no for node_no in range(20) if tests[node_no]]
        for row_no in range(20):
            columns[row_no].extend([face_mass[row_no][col_no] for col_no in chosen])
        index_list.extend(chosen)
    lift_mat = solve_linear(mass_mat, columns)
    return (deriv_mats, lift_mat, index_list)


def host_tables():
    deriv, lift, faces = reference_element()
    deriv = np.asarray(deriv, np.float32)
    lift = np.asarray(lift, np.float32)
    pick = np.zeros((NODES, FACE), np.float32)
    pick[np.asarray(faces), np.arange(FACE)] = 1.0

    def placed(rows, cols, parts):
        result = np.zeros((rows, cols), np.float32)
        for at, part in parts:
            result[: part.shape[0], at : at + part.shape[1]] = part
        return result

    forward = placed(ROWS, 112, [(0, lift)] + [(40 + 24 * d, deriv[d]) for d in range(3)])
    backward = placed(ROWS, 112, [(0, pick)] + [(40 + 24 * d, deriv[d].T) for d in range(3)])
    lift_t = placed(FACE, ROWS, [(0, lift.T)])
    pick_t = placed(FACE, ROWS, [(0, pick.T)])

    def split(matrix):
        high = matrix.astype(jnp.bfloat16).astype(np.float32)
        low = matrix - high
        return np.concatenate(
            [np.concatenate([high, high], 1), np.concatenate([low, np.zeros_like(low)], 1)], 0
        )

    table = np.zeros((224, 256), np.float32)
    table[0:48, 0:224] = split(forward)
    table[48:96, 0:224] = split(backward)
    table[96:176, 0:48] = split(lift_t)
    table[176:216, 0:48] = np.concatenate([pick_t, pick_t], 1)
    return table.astype(jnp.bfloat16), [int(v) for v in faces]


def stacked(values):
    high = values.astype(bf16).astype(f32)
    return jnp.concatenate([high, values - high], axis=0).astype(bf16)


def parts3(values):
    first = values.astype(bf16)
    rest = values - first.astype(f32)
    second = rest.astype(bf16)
    third = (rest - second.astype(f32)).astype(bf16)
    return first, second, third


def dot(left, right):
    return jnp.dot(left, right, preferred_element_type=f32)


def node_of(rows, faces):
    result = rows - 20
    for row, node in enumerate(faces):
        result = jnp.where(rows == row, node, result)
    return result


def one_hot(condition):
    return jnp.where(condition, 1.0, 0.0).astype(bf16)


def kernel_of(faces):
    def kernel(
        *refs,
    ):
        given, refs = refs[:14], refs[14:]
        out, therm = refs[:2]
        held, in_sem, refs = refs[2:16], refs[16], refs[17:]
        fs, adj, einf, edel, tau, met, fsc, ang, nbr, dexp, sexp, sslot, recv, tab = held
        (
        y, k, w, adj24, acc, nrm, scl, x, p, nb, cd, s_ref, pool, pp, nodes, nodex,
        a_mat, at_mat, ax, axt, b_mat, bx, oids, oh,
        sf, rf, sb, rb, ya, yr, cb, rc,
        fs_sem, fr_sem, bs_sem, br_sem, ps_sem, pr_sem, qs_sem, qr_sem,
        ) = refs

        def fetch(i):
            return pltpu.make_async_copy(given[i], held[i], in_sem.at[i])

        order = (10, 9, 0, 13, 8, 1, 2, 4, 3, 7, 6, 5, 11, 12)
        for i in order:
            fetch(i).start()

        dom = lax.axis_index("dom")
        sub = lax.axis_index("sub")

        rf[...] = jnp.zeros_like(rf)
        rb[...] = jnp.zeros_like(rb)
        yr[...] = jnp.zeros_like(yr)
        rc[...] = jnp.zeros_like(rc)
        barrier = pltpu.get_barrier_semaphore()
        for step in range(1, SUBS):
            pl.semaphore_signal(
                barrier, inc=1, device_id=(dom, lax.rem(sub + step, SUBS)), device_id_type=MESH
            )

        def greet(step, carry):
            pl.semaphore_signal(
                barrier, inc=1, device_id=(lax.rem(dom + step, DOMS), sub), device_id_type=MESH
            )
            return carry

        lax.fori_loop(1, DOMS, greet, 0)

        for i in order:
            fetch(i).wait()
        ie = 1.0 / einf[...]
        it = 1.0 / tau[...]
        ed = edel[...]
        pad = jnp.zeros((ROWS - NODES, 256), f32)
        for c in range(9):
            y[0, c] = jnp.concatenate([fs[c], pad], axis=0)
            value = jnp.concatenate([adj[c], pad], axis=0)
            adj24[c] = value
            acc[c] = value
            w[0, c] = (time_step / 6.0) * value
        sin_a = jnp.sin(ang[0])
        normals = (sin_a * jnp.cos(ang[1]), sin_a * jnp.sin(ang[1]), jnp.cos(ang[0]))
        for face in range(4):
            here = slice(10 * face, 10 * face + 10)
            for i in range(3):
                nrm[i, here, :] = jnp.broadcast_to(normals[i][face : face + 1], (10, 256))
            scl[here, :] = jnp.broadcast_to(0.5 * fsc[face : face + 1, :], (10, 256))

        exported = jnp.concatenate([sexp[0], dexp[...], jnp.zeros((2, 128), jnp.int32)], axis=0)
        nodex[...] = node_of(exported >> 8, faces)
        export_el = exported & 255
        export_cols = jnp.transpose(export_el)
        row_iota = lax.broadcasted_iota(jnp.int32, (256, 128), 0)
        lane_iota = lax.broadcasted_iota(jnp.int32, (128, 256), 1)
        for blk in range(BLOCKS):
            here = slice(128 * blk, 128 * blk + 128)
            ax[:, here] = one_hot(row_iota == export_el[blk : blk + 1])
            axt[here, :] = one_hot(lane_iota == export_cols[:, blk : blk + 1])

        def sub_copy(r, src, dst, send, recv_s, to, slot_from):
            return pltpu.make_async_remote_copy(
                src_ref=src.at[r, to],
                dst_ref=dst.at[r, slot_from],
                send_sem=send.at[r, to],
                recv_sem=recv_s.at[r, slot_from],
                device_id=(dom, to),
                device_id_type=MESH,
            )

        def dom_copy(r, src, dst, send, recv_s, block, slot, to):
            return pltpu.make_async_remote_copy(
                src_ref=src.at[r, block],
                dst_ref=dst.at[r, slot],
                send_sem=send.at[r, block],
                recv_sem=recv_s.at[r, slot],
                device_id=(to, sub),
                device_id_type=MESH,
            )

        has_low = dom > 0
        has_high = dom < DOMS - 1

        def start_all(r, src, dst, send, recv_s):
            for step in range(1, SUBS):
                to = lax.rem(sub + step, SUBS)
                sub_copy(r, src, dst, send, recv_s, to, sub).start()

            @pl.when(has_low)
            def _():
                dom_copy(r, src, dst, send, recv_s, 4, 5, dom - 1).start()

            @pl.when(has_high)
            def _():
                dom_copy(r, src, dst, send, recv_s, 5, 4, dom + 1).start()

        def wait_recv_all(r, src, dst, send, recv_s):
            for step in range(1, SUBS):
                other = lax.rem(sub + step, SUBS)
                sub_copy(r, src, dst, send, recv_s, other, other).wait_recv()

            @pl.when(has_low)
            def _():
                dom_copy(r, src, dst, send, recv_s, 4, 4, dom - 1).wait_recv()

            @pl.when(has_high)
            def _():
                dom_copy(r, src, dst, send, recv_s, 5, 5, dom + 1).wait_recv()

        def wait_send_all(r, src, dst, send, recv_s):
            for step in range(1, SUBS):
                to = lax.rem(sub + step, SUBS)
                sub_copy(r, src, dst, send, recv_s, to, sub).wait_send()

            @pl.when(has_low)
            def _():
                dom_copy(r, src, dst, send, recv_s, 4, 5, dom - 1).wait_send()

            @pl.when(has_high)
            def _():
                dom_copy(r, src, dst, send, recv_s, 5, 4, dom + 1).wait_send()

        fwd = (sf, rf, fs_sem, fr_sem)
        bwd = (sb, rb, bs_sem, br_sem)

        node_iota = lax.broadcasted_iota(jnp.int32, (ROWS, 128), 0)
        node_iota2 = lax.broadcasted_iota(jnp.int32, (ROWS, 256), 0)
        own_rows = node_iota2 < NODES

        def fold_pool():
            values = pool[...].reshape(6 * ROWS, 256)
            high = values.astype(bf16)
            pp[0:144, :] = high
            pp[144:288, :] = (values - high.astype(f32)).astype(bf16)

        def exports(r):
            for c in range(6):
                pool[c] = y[r, c]
            fold_pool()
            for blk in range(BLOCKS):
                got = dot(pp[...], ax[:, 128 * blk : 128 * blk + 128])
                got = got[:144] + got[144:]
                keep = node_iota == nodex[blk : blk + 1, :]
                for c in range(6):
                    sf[r, blk, c : c + 1, :] = jnp.sum(
                        jnp.where(keep, got[24 * c : 24 * c + 24], 0.0), axis=0, keepdims=True
                    )
            start_all(r, *fwd)

        def flux_rows(src, at):
            here = slice(at, at + 8)
            n = [nrm[i, here, :] for i in range(3)]
            e = [src[i, here, :] for i in range(3)]
            h = [src[3 + i, here, :] for i in range(3)]
            ne = n[0] * e[0] + n[1] * e[1] + n[2] * e[2]
            nh = n[0] * h[0] + n[1] * h[1] + n[2] * h[2]
            result = []
            for i in range(3):
                j, l = (i + 1) % 3, (i + 2) % 3
                result.append(n[i] * ne - e[i] - (n[j] * h[l] - n[l] * h[j]))
            for i in range(3):
                j, l = (i + 1) % 3, (i + 2) % 3
                result.append((n[j] * e[l] - n[l] * e[j]) + n[i] * nh - h[i])
            return result

        def curl_rows(e, h):
            for d in range(3):
                m = [met[3 * d + i : 3 * d + i + 1, :] for i in range(3)]
                here = slice(40 + 24 * d, 64 + 24 * d)
                for i in range(3):
                    j, l = (i + 1) % 3, (i + 2) % 3
                    x[i, here, :] = m[j] * h[l] - m[l] * h[j]
                    x[3 + i, here, :] = m[l] * e[j] - m[j] * e[l]

        def contracted(first, c):
            got = dot(tab[first : first + 48, 0:224], stacked(x[c]))
            return got[:24] + got[24:]

        def back_faces(r):
            for c in range(6):
                value = w[r, c]
                if c < 3:
                    value = value * ie
                got = dot(tab[96:176, 0:48], stacked(value))
                p[c] = (got[:40] + got[40:]) * scl[...]
            for at in range(0, FACE, 8):
                for c, value in enumerate(flux_rows(p, at)):
                    cd[c, at : at + 8, :] = value

            def group(g, carry):
                for j in range(8):
                    fn = g * 8 + j
                    keep = node_iota2 == nodes[pl.ds(fn, 1), :]
                    high, low = [], []
                    for c in range(6):
                        value = cd[c, pl.ds(fn, 1), :]
                        top = value.astype(bf16).astype(f32)
                        high.append(jnp.where(keep, top, 0.0))
                        low.append(jnp.where(keep, value - top, 0.0))
                    b_mat[:, 256 * j : 256 * j + 256] = jnp.concatenate(high + low, 0).astype(bf16)
                got = dot(b_mat[...], at_mat[pl.ds(pl.multiple_of(g * 2048, 2048), 2048), :])
                s_ref[...] = s_ref[...] - (got[:144] + got[144:])
                return carry

            s_ref[...] = jnp.zeros_like(s_ref)
            lax.fori_loop(0, FACE // 8, group, 0)
            for c in range(6):
                rows = s_ref[24 * c + 20 : 24 * c + 24, :]
                for blk in range(4):
                    at = 128 * (blk % 2)
                    sb[r, blk, c : c + 1, :] = rows[blk // 2 : blk // 2 + 1, at : at + 128]
                sb[r, 4, c : c + 1, :] = rows[2:3, 0:128]
                sb[r, 5, c : c + 1, :] = rows[3:4, 128:256]
            start_all(r, *bwd)

        def arrived(r, blk, dst, src):
            value = dst[r, blk]
            if blk < SUBS:
                value = jnp.where(sub == blk, src[r, blk], value)
            return value

        def forward(r):
            wait_recv_all(r, *fwd)
            for blk in range(4):
                value = arrived(r, blk, rf, sf)
                at = 128 * (blk % 2)
                for c in range(6):
                    row = 20 + blk // 2
                    pool[c, row : row + 1, at : at + 128] = value[c : c + 1]
            low, high = rf[r, 4], rf[r, 5]
            for c in range(6):
                pool[c, 22:23, 0:128] = low[c : c + 1]
                pool[c, 23:24, 128:256] = high[c : c + 1]
            fold_pool()

            def group(g, carry):
                for j in range(8):
                    fn = g * 8 + j
                    keep = node_iota2 == nodes[pl.ds(fn, 1), :]
                    got = dot(pp[...], a_mat[fn])
                    got = got[:144] + got[144:]
                    for c in range(6):
                        nb[c, pl.ds(fn, 1), :] = jnp.sum(
                            jnp.where(keep, got[24 * c : 24 * c + 24], 0.0), axis=0, keepdims=True
                        )
                return carry

            lax.fori_loop(0, FACE // 8, group, 0)
            for c in range(6):
                p[c] = dot(tab[176:216, 0:48], stacked(y[r, c])) - nb[c]
            for at in range(0, FACE, 8):
                factor = scl[at : at + 8, :]
                for c, value in enumerate(flux_rows(p, at)):
                    x[c, at : at + 8, :] = value * factor
            curl_rows([y[r, c] for c in range(3)], [y[r, 3 + c] for c in range(3)])
            for c in range(3):
                current = (ed * y[r, c] - y[r, 6 + c]) * it
                k[r, 6 + c] = current
                k[r, c] = (contracted(0, c) - current) * ie
                k[r, 3 + c] = contracted(0, 3 + c)

        def back_volume(r):
            for c in range(6):
                x[c, 0:40, :] = cd[c]
            curl_rows([w[r, c] * ie for c in range(3)], [w[r, 3 + c] for c in range(3)])
            wait_recv_all(r, *bwd)
            for blk in range(BLOCKS):
                value = arrived(r, blk, rb, sb)
                keep = node_iota == nodex[blk : blk + 1, :]
                top = value.astype(bf16).astype(f32)
                rest = value - top
                high = [jnp.where(keep, top[c : c + 1], 0.0) for c in range(6)]
                low = [jnp.where(keep, rest[c : c + 1], 0.0) for c in range(6)]
                bx[:, 128 * blk : 128 * blk + 128] = jnp.concatenate(high + low, 0).astype(bf16)
            got = dot(bx[...], axt[...])
            s_ref[...] = s_ref[...] + (got[:144] + got[144:])
            cots = []
            for c in range(6):
                value = contracted(48, c) + s_ref[24 * c : 24 * c + 24, :]
                cots.append(jnp.where(own_rows, value, 0.0))
            for c in range(3):
                through = (w[r, 6 + c] - w[r, c] * ie) * it
                cots[c] = cots[c] + ed * through
                cots.append(-through)
            return cots

        def one_round(r, ahead, adj_part, back_part):
            back_faces(r)
            forward(r)
            for c in range(9):
                y[r + 1, c] = y[0, c] + ahead * k[r, c]
            exports(r + 1)
            for c, value in enumerate(back_volume(r)):
                acc[c] = acc[c] + value
                w[r + 1, c] = adj_part * adj24[c] + back_part * value

        pl.semaphore_wait(barrier, SUBS - 1 + DOMS - 1)
        exports(0)
        index = nbr[...]
        nodes[...] = node_of(index >> 8, faces)
        element = index & 255
        columns = jnp.transpose(element)
        lane_iota2 = lax.broadcasted_iota(jnp.int32, (256, 256), 1)
        row_iota2 = lax.broadcasted_iota(jnp.int32, (256, 256), 0)
        for fn in range(FACE):
            at_mat[256 * fn : 256 * fn + 256, :] = one_hot(lane_iota2 == columns[:, fn : fn + 1])
            a_mat[fn] = one_hot(row_iota2 == element[fn : fn + 1])

        owners = jnp.transpose(jnp.concatenate([recv[0], jnp.zeros((6, 128), jnp.int32)], axis=0))
        oids[...] = owners
        lanes = lax.broadcasted_iota(jnp.int32, (DOMS, 128), 1)
        for q in range(SUBS):
            ids = oids[pl.ds(q, DOMS, stride=SUBS), :]
            for z in range(2):
                at = 128 * (2 * q + z)
                oh[:, at : at + 128] = one_hot(lanes == ids[:, z : z + 1])

        def looped(r, carry):
            last = r == 2
            one_round(
                r,
                jnp.where(last, time_step, 0.5 * time_step),
                jnp.where(last, time_step / 6.0, time_step / 3.0),
                jnp.where(r == 0, time_step, 0.5 * time_step),
            )
            return carry

        lax.fori_loop(0, 3, looped, 0)
        back_faces(3)
        forward(3)

        sums = [jnp.zeros((ROWS, 256), f32) for _ in range(3)]
        for r in range(4):
            for c in range(3):
                through = w[3 - r, 6 + c] - w[3 - r, c] * ie
                sums[0] = sums[0] - w[3 - r, c] * k[r, c]
                sums[1] = sums[1] + through * y[r, c]
                sums[2] = sums[2] - through * k[r, 6 + c]
        grads = [
            jnp.sum(value, axis=0, keepdims=True) * factor
            for value, factor in zip(sums, (ie, it, it))
        ]
        slot = sslot[...]
        target = ((slot >> 1) & 3) * DOMS + (slot >> 3)
        chosen = one_hot(lax.broadcasted_iota(jnp.int32, (128, 256), 0) == target)
        lines = [jnp.where((slot & 1) == q, g, 0.0) for q in range(2) for g in grads]
        lines = jnp.concatenate(lines + [jnp.zeros((2, 256), f32)], axis=0)
        lines = [jnp.where(sub == q, lines, 0.0) for q in range(SUBS)]
        lines = jnp.concatenate(lines + [jnp.zeros((96, 256), f32)], axis=0)
        packed = sum(dot(chosen, part) for part in parts3(jnp.transpose(lines)))
        for q in range(SUBS):
            ya[q] = packed[DOMS * q : DOMS * q + DOMS]

        def first_hop(to, slot_from):
            return pltpu.make_async_remote_copy(
                src_ref=ya.at[to],
                dst_ref=yr.at[slot_from],
                send_sem=ps_sem.at[to],
                recv_sem=pr_sem.at[slot_from],
                device_id=(dom, to),
                device_id_type=MESH,
            )

        for step in range(1, SUBS):
            first_hop(lax.rem(sub + step, SUBS), sub).start()
        for step in range(1, SUBS):
            other = lax.rem(sub + step, SUBS)
            first_hop(other, other).wait_recv()
        mine = ya[pl.ds(sub, 1)][0] + yr[0] + yr[1] + yr[2] + yr[3]
        for q in range(DOMS):
            cb[q] = mine[q : q + 1]

        def second_hop(to, slot_from):
            return pltpu.make_async_remote_copy(
                src_ref=cb.at[to],
                dst_ref=rc.at[slot_from],
                send_sem=qs_sem.at[to],
                recv_sem=qr_sem.at[slot_from],
                device_id=(to, sub),
                device_id_type=MESH,
            )

        def hop_start(step, carry):
            second_hop(lax.rem(dom + step, DOMS), dom).start()
            return carry

        def hop_wait(step, carry):
            other = lax.rem(dom + step, DOMS)
            second_hop(other, other).wait_recv()
            return carry

        def hop_sent(step, carry):
            second_hop(lax.rem(dom + step, DOMS), dom).wait_send()
            return carry

        lax.fori_loop(1, DOMS, hop_start, 0)

        for c, value in enumerate(back_volume(3)):
            out[c] = (acc[c] + value)[:NODES]

        lax.fori_loop(1, DOMS, hop_wait, 0)
        here = lax.broadcasted_iota(jnp.int32, (DOMS, 128), 0) == dom
        came = jnp.concatenate([rc[q] for q in range(DOMS)], axis=0)
        came = came + jnp.where(here, mine, 0.0)
        turned = jnp.concatenate(parts3(jnp.transpose(came)[:32]), axis=0)
        spread = dot(turned, oh[...])
        spread = spread[:32] + spread[32:64] + spread[64:]
        total = jnp.zeros((3, 128), f32)
        for q in range(SUBS):
            for z in range(2):
                row, at = 8 * q + 3 * z, 128 * (2 * q + z)
                total = total + spread[row : row + 3, at : at + 128]
        therm[...] = total[:, :64]

        for r in range(4):
            wait_send_all(r, *fwd)
            wait_send_all(r, *bwd)
        for step in range(1, SUBS):
            first_hop(lax.rem(sub + step, SUBS), sub).wait_send()
        lax.fori_loop(1, DOMS, hop_sent, 0)

    return kernel


def per_device(
    field_state,
    adjoint,
    eps_inf,
    eps_delta,
    relax_time,
    metric,
    face_scale,
    face_angles,
    nbr_index,
    dom_export,
    sub_export,
    send_slot,
    recv_index,
):
    table, faces = host_tables()
    stage = pltpu.VMEM((4, 9, ROWS, 256), f32)
    trace = pltpu.VMEM((6, FACE, 256), f32)
    message = pltpu.VMEM((4, BLOCKS, 8, 128), f32)
    semaphores = pltpu.SemaphoreType.DMA((4, BLOCKS))
    state = pltpu.VMEM((9, ROWS, 256), f32)
    values = (
        field_state,
        adjoint,
        eps_inf.reshape(1, 256),
        eps_delta.reshape(1, 256),
        relax_time.reshape(1, 256),
        metric,
        face_scale,
        face_angles,
        nbr_index,
        dom_export.reshape(2, 128),
        sub_export,
        send_slot.reshape(1, 256),
        jnp.transpose(recv_index, (0, 2, 1)),
        jnp.asarray(table),
    )
    scratch = [pltpu.VMEM(value.shape, value.dtype) for value in values] + [
        pltpu.SemaphoreType.DMA((len(values),)),
        stage, stage, stage, state, state,
        pltpu.VMEM((3, FACE, 256), f32),
        pltpu.VMEM((FACE, 256), f32),
        pltpu.VMEM((6, 112, 256), f32),
        trace, trace, trace,
        pltpu.VMEM((6 * ROWS, 256), f32),
        pltpu.VMEM((6, ROWS, 256), f32),
        pltpu.VMEM((12 * ROWS, 256), bf16),
        pltpu.VMEM((FACE, 256), jnp.int32),
        pltpu.VMEM((8, 128), jnp.int32),
        pltpu.VMEM((FACE, 256, 256), bf16),
        pltpu.VMEM((FACE * 256, 256), bf16),
        pltpu.VMEM((256, 128 * BLOCKS), bf16),
        pltpu.VMEM((128 * BLOCKS, 256), bf16),
        pltpu.VMEM((12 * ROWS, 2048), bf16),
        pltpu.VMEM((12 * ROWS, 128 * BLOCKS), bf16),
        pltpu.VMEM((128, 8), jnp.int32),
        pltpu.VMEM((DOMS, 1024), bf16),
        message, message, message, message,
        pltpu.VMEM((SUBS, DOMS, 128), f32),
        pltpu.VMEM((SUBS, DOMS, 128), f32),
        pltpu.VMEM((DOMS, 1, 128), f32),
        pltpu.VMEM((DOMS, 1, 128), f32),
        semaphores, semaphores, semaphores, semaphores,
        pltpu.SemaphoreType.DMA((SUBS,)),
        pltpu.SemaphoreType.DMA((SUBS,)),
        pltpu.SemaphoreType.DMA((DOMS,)),
        pltpu.SemaphoreType.DMA((DOMS,)),
    ]
    call = pl.pallas_call(
        kernel_of(faces),
        out_shape=(
            jax.ShapeDtypeStruct((9, NODES, 256), f32),
            jax.ShapeDtypeStruct((3, 64), f32),
        ),
        in_specs=[pl.BlockSpec(memory_space=pltpu.HBM)] * 14,
        out_specs=(
            pl.BlockSpec(memory_space=pltpu.VMEM),
            pl.BlockSpec(memory_space=pltpu.VMEM),
        ),
        scratch_shapes=scratch,
        compiler_params=pltpu.CompilerParams(
            collective_id=0, has_side_effects=True, vmem_limit_bytes=32 << 20
        ),
        name="reverse_step",
    )
    return call(*[pltpu.with_memory_space_constraint(v, pltpu.HBM) for v in values])


def solution(mesh):
    both = ("dom", "sub")
    return jax.shard_map(
        per_device,
        mesh=mesh,
        in_specs=(
            P(None, None, both),
            P(None, None, both),
            P(both),
            P(both),
            P(both),
            P(None, both),
            P(None, both),
            P(None, None, both),
            P(None, both),
            P(both),
            P(both, None, None),
            P(both),
            P(both, None, None),
        ),
        out_specs=(P(None, None, both), P(None, both)),
        check_vma=False,
    )
```

```python
import math

import jax
import jax.numpy as jnp
import numpy as np
from jax import lax
from jax.experimental import pallas as pl
from jax.experimental.pallas import tpu as pltpu
from jax.sharding import PartitionSpec as P

time_step = 0.014
f32 = jnp.float32
bf16 = jnp.bfloat16
NODES = 20
ROWS = 24
FACE = 40
DOMS = 32
SUBS = 4
BLOCKS = 6
SEATS = 8
SITES = 16
GROUP = 8
MESH = pl.DeviceIdType.MESH


def mat_mul(left, right):
    inner = len(right)
    return [
        [
            sum((left[row_no][k] * right[k][col_no] for k in range(inner)))
            for col_no in range(len(right[0]))
        ]
        for row_no in range(len(left))
    ]


def transposed(matrix):
    return [list(column) for column in zip(*matrix)]


def solve_linear(matrix, rhs_rows):
    order = len(matrix)
    work = [list(matrix[row_no]) + list(rhs_rows[row_no]) for row_no in range(order)]
    for col_no in range(order):

        def magnitude(row_no):
            return abs(work[row_no][col_no])

        pivot = max(range(col_no, order), key=magnitude)
        work[col_no], work[pivot] = (work[pivot], work[col_no])
        head = work[col_no][col_no]
        work[col_no] = [value / head for value in work[col_no]]
        for row_no in range(order):
            if row_no != col_no:
                factor = work[row_no][col_no]
                work[row_no] = [
                    value - factor * other for value, other in zip(work[row_no], work[col_no])
                ]
    return [row[order:] for row in work]


def reference_element():
    lattice = [(i, j, k) for k in range(4) for j in range(4 - k) for i in range(4 - j - k)]
    points = [[float(v) / 3.0 for v in node] for node in lattice]
    vander = [[0.0] * 20 for node_no in range(20)]
    slopes = [[[0.0] * 20 for node_no in range(20)] for axis_no in range(3)]
    for node_no in range(20):
        for mono_no in range(20):
            power = lattice[mono_no]
            value = 1.0
            for axis_no in range(3):
                value *= points[node_no][axis_no] ** power[axis_no]
            vander[node_no][mono_no] = value
            for axis_no in range(3):
                if power[axis_no] > 0:
                    term = float(power[axis_no])
                    for other_no in range(3):
                        expo_val = power[other_no] - (1 if other_no == axis_no else 0)
                        term *= points[node_no][other_no] ** expo_val
                    slopes[axis_no][node_no][mono_no] = term
    identity = [[1.0 if row_no == col_no else 0.0 for col_no in range(20)] for row_no in range(20)]
    inverse = solve_linear(vander, identity)
    deriv_mats = [mat_mul(slopes[axis_no], inverse) for axis_no in range(3)]
    fact = math.factorial

    def face_integral(face_no, a, b, c):
        if face_no == 0:
            return 0.0 if c > 0 else fact(a) * fact(b) / fact(a + b + 2)
        if face_no == 1:
            return 0.0 if b > 0 else fact(a) * fact(c) / fact(a + c + 2)
        if face_no == 2:
            return math.sqrt(3.0) * fact(a) * fact(b) * fact(c) / fact(a + b + c + 2)
        return 0.0 if a > 0 else fact(b) * fact(c) / fact(b + c + 2)

    inverse_t = transposed(inverse)
    mono_mass = [[0.0] * 20 for node_no in range(20)]
    for first_no in range(20):
        for second_no in range(20):
            a = lattice[first_no][0] + lattice[second_no][0]
            b = lattice[first_no][1] + lattice[second_no][1]
            c = lattice[first_no][2] + lattice[second_no][2]
            mono_mass[first_no][second_no] = fact(a) * fact(b) * fact(c) / fact(a + b + c + 3)
    mass_mat = mat_mul(mat_mul(inverse_t, mono_mass), inverse)
    columns = [[] for node_no in range(20)]
    index_list = []
    for face_no in range(4):
        mono_face = [[0.0] * 20 for node_no in range(20)]
        for first_no in range(20):
            for second_no in range(20):
                a = lattice[first_no][0] + lattice[second_no][0]
                b = lattice[first_no][1] + lattice[second_no][1]
                c = lattice[first_no][2] + lattice[second_no][2]
                mono_face[first_no][second_no] = face_integral(face_no, a, b, c)
        face_mass = mat_mul(mat_mul(inverse_t, mono_face), inverse)
        tests = [k == 0 for i, j, k in lattice]
        if face_no == 1:
            tests = [j == 0 for i, j, k in lattice]
        if face_no == 2:
            tests = [i + j + k == 3 for i, j, k in lattice]
        if face_no == 3:
            tests = [i == 0 for i, j, k in lattice]
        chosen = [node_no for node_no in range(20) if tests[node_no]]
        for row_no in range(20):
            columns[row_no].extend([face_mass[row_no][col_no] for col_no in chosen])
        index_list.extend(chosen)
    lift_mat = solve_linear(mass_mat, columns)
    return (deriv_mats, lift_mat, index_list)


def host_tables():
    deriv, lift, faces = reference_element()
    deriv = np.asarray(deriv, np.float32)
    lift = np.asarray(lift, np.float32)
    pick = np.zeros((NODES, FACE), np.float32)
    pick[np.asarray(faces), np.arange(FACE)] = 1.0

    def placed(rows, cols, parts):
        result = np.zeros((rows, cols), np.float32)
        for at, part in parts:
            result[: part.shape[0], at : at + part.shape[1]] = part
        return result

    forward = placed(ROWS, 112, [(0, lift)] + [(40 + 24 * d, deriv[d]) for d in range(3)])
    backward = placed(ROWS, 112, [(0, pick)] + [(40 + 24 * d, deriv[d].T) for d in range(3)])
    lift_t = placed(FACE, ROWS, [(0, lift.T)])
    pick_t = placed(FACE, ROWS, [(0, pick.T)])

    def split(matrix):
        high = matrix.astype(jnp.bfloat16).astype(np.float32)
        low = matrix - high
        return np.concatenate(
            [np.concatenate([high, high], 1), np.concatenate([low, np.zeros_like(low)], 1)], 0
        )

    table = np.zeros((224, 256), np.float32)
    table[0:48, 0:224] = split(forward)
    table[48:96, 0:224] = split(backward)
    table[96:176, 0:48] = split(lift_t)
    table[176:216, 0:48] = np.concatenate([pick_t, pick_t], 1)
    return table.astype(jnp.bfloat16), [int(v) for v in faces]


def stacked(values):
    high = values.astype(bf16).astype(f32)
    return jnp.concatenate([high, values - high], axis=0).astype(bf16)


def parts3(values):
    first = values.astype(bf16)
    rest = values - first.astype(f32)
    second = rest.astype(bf16)
    third = (rest - second.astype(f32)).astype(bf16)
    return first, second, third


def dot(left, right):
    return jnp.dot(left, right, preferred_element_type=f32)


def node_of(rows, faces):
    result = rows - 20
    for row, node in enumerate(faces):
        result = jnp.where(rows == row, node, result)
    return result


def one_hot(condition):
    return jnp.where(condition, 1.0, 0.0).astype(bf16)


def kernel_of(faces):
    def kernel(
        *refs,
    ):
        given, refs = refs[:14], refs[14:]
        out, therm = refs[:2]
        held, in_sem, refs = refs[2:16], refs[16], refs[17:]
        fs, adj, einf, edel, tau, met, fsc, ang, nbr, dexp, sexp, sslot, recv, tab = held
        (
        y, k, w, adj24, acc, nrm, scl, x, xb, p, nb, cd, s_ref, pool, pp, nodes, nodex,
        a_mat, at_mat, ax, axt, b_mat, bx, oids, oh,
        sf, rf, sb, rb, ya, yr, cb, rc,
        fs_sem, fr_sem, bs_sem, br_sem, ps_sem, pr_sem, qs_sem, qr_sem,
        ) = refs

        def fetch(i):
            return pltpu.make_async_copy(given[i], held[i], in_sem.at[i])

        order = (10, 9, 0, 13, 8, 1, 2, 4, 3, 7, 6, 5, 11, 12)
        for i in order:
            fetch(i).start()

        dom = lax.axis_index("dom")
        sub = lax.axis_index("sub")

        rf[...] = jnp.zeros_like(rf)
        rb[...] = jnp.zeros_like(rb)
        yr[...] = jnp.zeros_like(yr)
        rc[...] = jnp.zeros_like(rc)
        barrier = pltpu.get_barrier_semaphore()
        core = lax.rem(dom, 2)
        site = dom // 2
        seat = sub * 2 + core

        def seat_device(other):
            return (site * 2 + lax.rem(other, 2), other // 2)

        def site_device(other):
            return (other * 2 + core, sub)

        def greet(device):
            pl.semaphore_signal(barrier, inc=1, device_id=device, device_id_type=MESH)

        for step in range(1, SEATS):
            greet(seat_device(lax.rem(seat + step, SEATS)))
        for step in range(1, SITES):
            greet(site_device(lax.rem(site + step, SITES)))
        has_low = dom > 0
        has_high = dom < DOMS - 1

        @pl.when(has_low & (core == 0))
        def _():
            greet((dom - 1, sub))

        @pl.when(has_high & (core == 1))
        def _():
            greet((dom + 1, sub))

        def meet():
            outside = (has_low & (core == 0)) | (has_high & (core == 1))
            pl.semaphore_wait(barrier, jnp.where(outside, SEATS + SITES - 1, SEATS + SITES - 2))

        for i in order:
            fetch(i).wait()
        ie = 1.0 / einf[...]
        it = 1.0 / tau[...]
        ed = edel[...]
        pad = jnp.zeros((ROWS - NODES, 256), f32)
        for c in range(9):
            y[0, c] = jnp.concatenate([fs[c], pad], axis=0)
            value = jnp.concatenate([adj[c], pad], axis=0)
            adj24[c] = value
            acc[c] = value
            w[0, c] = (time_step / 6.0) * value
        sin_a = jnp.sin(ang[0])
        normals = (sin_a * jnp.cos(ang[1]), sin_a * jnp.sin(ang[1]), jnp.cos(ang[0]))
        for face in range(4):
            here = slice(10 * face, 10 * face + 10)
            for i in range(3):
                nrm[i, here, :] = jnp.broadcast_to(normals[i][face : face + 1], (10, 256))
            scl[here, :] = jnp.broadcast_to(0.5 * fsc[face : face + 1, :], (10, 256))

        exported = jnp.concatenate([sexp[0], dexp[...], jnp.zeros((2, 128), jnp.int32)], axis=0)
        nodex[...] = node_of(exported >> 8, faces)
        export_el = exported & 255
        export_cols = jnp.transpose(export_el)
        row_iota = lax.broadcasted_iota(jnp.int32, (256, 128), 0)
        lane_iota = lax.broadcasted_iota(jnp.int32, (128, 256), 1)
        for blk in range(BLOCKS):
            here = slice(128 * blk, 128 * blk + 128)
            ax[:, here] = one_hot(row_iota == export_el[blk : blk + 1])
            axt[here, :] = one_hot(lane_iota == export_cols[:, blk : blk + 1])

        def sub_copy(r, src, dst, send, recv_s, to, slot_from):
            return pltpu.make_async_remote_copy(
                src_ref=src.at[r, to],
                dst_ref=dst.at[r, slot_from],
                send_sem=send.at[r, to],
                recv_sem=recv_s.at[r, slot_from],
                device_id=(dom, to),
                device_id_type=MESH,
            )

        def dom_copy(r, src, dst, send, recv_s, block, slot, to):
            return pltpu.make_async_remote_copy(
                src_ref=src.at[r, block],
                dst_ref=dst.at[r, slot],
                send_sem=send.at[r, block],
                recv_sem=recv_s.at[r, slot],
                device_id=(to, sub),
                device_id_type=MESH,
            )

        def start_all(r, src, dst, send, recv_s):
            for step in range(1, SUBS):
                to = lax.rem(sub + step, SUBS)
                sub_copy(r, src, dst, send, recv_s, to, sub).start()

            @pl.when(has_low)
            def _():
                dom_copy(r, src, dst, send, recv_s, 4, 5, dom - 1).start()

            @pl.when(has_high)
            def _():
                dom_copy(r, src, dst, send, recv_s, 5, 4, dom + 1).start()

        def wait_recv_all(r, src, dst, send, recv_s):
            for step in range(1, SUBS):
                other = lax.rem(sub + step, SUBS)
                sub_copy(r, src, dst, send, recv_s, other, other).wait_recv()

            @pl.when(has_low)
            def _():
                dom_copy(r, src, dst, send, recv_s, 4, 4, dom - 1).wait_recv()

            @pl.when(has_high)
            def _():
                dom_copy(r, src, dst, send, recv_s, 5, 5, dom + 1).wait_recv()

        def wait_send_all(r, src, dst, send, recv_s):
            for step in range(1, SUBS):
                to = lax.rem(sub + step, SUBS)
                sub_copy(r, src, dst, send, recv_s, to, sub).wait_send()

            @pl.when(has_low)
            def _():
                dom_copy(r, src, dst, send, recv_s, 4, 5, dom - 1).wait_send()

            @pl.when(has_high)
            def _():
                dom_copy(r, src, dst, send, recv_s, 5, 4, dom + 1).wait_send()

        fwd = (sf, rf, fs_sem, fr_sem)
        bwd = (sb, rb, bs_sem, br_sem)

        node_iota = lax.broadcasted_iota(jnp.int32, (ROWS, 128), 0)
        node_iota2 = lax.broadcasted_iota(jnp.int32, (ROWS, 256), 0)
        own_rows = node_iota2 < NODES

        def fold_pool():
            values = pool[...].reshape(6 * ROWS, 256)
            high = values.astype(bf16)
            pp[0:144, :] = high
            pp[144:288, :] = (values - high.astype(f32)).astype(bf16)

        def exports(r):
            for c in range(6):
                pool[c] = y[r, c]
            fold_pool()
            for pair in range(BLOCKS // 2):
                both = dot(pp[...], ax[:, 256 * pair : 256 * pair + 256])
                both = both[:144] + both[144:]
                for half in range(2):
                    blk = 2 * pair + half
                    got = both[:, 128 * half : 128 * half + 128]
                    keep = node_iota == nodex[blk : blk + 1, :]
                    for c in range(6):
                        sf[r, blk, c : c + 1, :] = jnp.sum(
                            jnp.where(keep, got[24 * c : 24 * c + 24], 0.0), axis=0, keepdims=True
                        )
        def flux_rows(src, at):
            here = slice(at, at + 8)
            n = [nrm[i, here, :] for i in range(3)]
            e = [src[i, here, :] for i in range(3)]
            h = [src[3 + i, here, :] for i in range(3)]
            ne = n[0] * e[0] + n[1] * e[1] + n[2] * e[2]
            nh = n[0] * h[0] + n[1] * h[1] + n[2] * h[2]
            result = []
            for i in range(3):
                j, l = (i + 1) % 3, (i + 2) % 3
                result.append(n[i] * ne - e[i] - (n[j] * h[l] - n[l] * h[j]))
            for i in range(3):
                j, l = (i + 1) % 3, (i + 2) % 3
                result.append((n[j] * e[l] - n[l] * e[j]) + n[i] * nh - h[i])
            return result

        def curl_rows(x, e, h):
            for d in range(3):
                m = [met[3 * d + i : 3 * d + i + 1, :] for i in range(3)]
                here = slice(40 + 24 * d, 64 + 24 * d)
                for i in range(3):
                    j, l = (i + 1) % 3, (i + 2) % 3
                    x[i, here, :] = m[j] * h[l] - m[l] * h[j]
                    x[3 + i, here, :] = m[l] * e[j] - m[j] * e[l]

        def contracted(x, first, c):
            got = dot(tab[first : first + 48, 0:224], stacked(x[c]))
            return got[:24] + got[24:]

        def back_flux(r):
            for c in range(6):
                value = w[r, c]
                if c < 3:
                    value = value * ie
                got = dot(tab[96:176, 0:48], stacked(value))
                p[c] = (got[:40] + got[40:]) * scl[...]
            for at in range(0, FACE, 8):
                for c, value in enumerate(flux_rows(p, at)):
                    cd[c, at : at + 8, :] = value

        def sweep(gather, scatter):
            def group(g, carry):
                for j in range(GROUP):
                    fn = g * GROUP + j
                    keep = node_iota2 == nodes[pl.ds(fn, 1), :]
                    if gather:
                        got = dot(pp[...], a_mat[fn])
                        got = got[:144] + got[144:]
                        for c in range(6):
                            nb[c, pl.ds(fn, 1), :] = jnp.sum(
                                jnp.where(keep, got[24 * c : 24 * c + 24], 0.0),
                                axis=0,
                                keepdims=True,
                            )
                    if scatter:
                        high, low = [], []
                        for c in range(6):
                            value = cd[c, pl.ds(fn, 1), :]
                            top = value.astype(bf16).astype(f32)
                            high.append(jnp.where(keep, top, 0.0))
                            low.append(jnp.where(keep, value - top, 0.0))
                        b_mat[:, 256 * j : 256 * j + 256] = jnp.concatenate(high + low, 0).astype(
                            bf16
                        )
                if scatter:
                    span = GROUP * 256
                    got = dot(b_mat[...], at_mat[pl.ds(pl.multiple_of(g * span, span), span), :])
                    s_ref[...] = s_ref[...] - (got[:144] + got[144:])
                return carry

            if scatter:
                s_ref[...] = jnp.zeros_like(s_ref)
            lax.fori_loop(0, FACE // GROUP, group, 0)

        def give_back(r):
            for c in range(6):
                rows = s_ref[24 * c + 20 : 24 * c + 24, :]
                for blk in range(4):
                    at = 128 * (blk % 2)
                    sb[r, blk, c : c + 1, :] = rows[blk // 2 : blk // 2 + 1, at : at + 128]
                sb[r, 4, c : c + 1, :] = rows[2:3, 0:128]
                sb[r, 5, c : c + 1, :] = rows[3:4, 128:256]

        def arrived(r, blk, dst, src):
            value = dst[r, blk]
            if blk < SUBS:
                value = jnp.where(sub == blk, src[r, blk], value)
            return value

        def receive(r):
            wait_recv_all(r, *fwd)
            for blk in range(4):
                value = arrived(r, blk, rf, sf)
                at = 128 * (blk % 2)
                for c in range(6):
                    row = 20 + blk // 2
                    pool[c, row : row + 1, at : at + 128] = value[c : c + 1]
            low, high = rf[r, 4], rf[r, 5]
            for c in range(6):
                pool[c, 22:23, 0:128] = low[c : c + 1]
                pool[c, 23:24, 128:256] = high[c : c + 1]
            fold_pool()

        def forward(r, whole=True):
            for c in range(6):
                p[c] = dot(tab[176:216, 0:48], stacked(y[r, c])) - nb[c]
            for at in range(0, FACE, 8):
                factor = scl[at : at + 8, :]
                for c, value in enumerate(flux_rows(p, at)):
                    x[c, at : at + 8, :] = value * factor
            curl_rows(x, [y[r, c] for c in range(3)], [y[r, 3 + c] for c in range(3)])
            for c in range(3):
                current = (ed * y[r, c] - y[r, 6 + c]) * it
                k[r, 6 + c] = current
                k[r, c] = (contracted(x, 0, c) - current) * ie
                if whole:
                    k[r, 3 + c] = contracted(x, 0, 3 + c)

        def back_volume(r):
            for c in range(6):
                xb[c, 0:40, :] = cd[c]
            curl_rows(xb, [w[r, c] * ie for c in range(3)], [w[r, 3 + c] for c in range(3)])
            cots = [contracted(xb, 48, c) for c in range(6)]
            wait_recv_all(r, *bwd)
            for blk in range(BLOCKS):
                value = arrived(r, blk, rb, sb)
                keep = node_iota == nodex[blk : blk + 1, :]
                top = value.astype(bf16).astype(f32)
                rest = value - top
                high = [jnp.where(keep, top[c : c + 1], 0.0) for c in range(6)]
                low = [jnp.where(keep, rest[c : c + 1], 0.0) for c in range(6)]
                bx[:, 128 * blk : 128 * blk + 128] = jnp.concatenate(high + low, 0).astype(bf16)
            got = dot(bx[...], axt[...])
            s_ref[...] = s_ref[...] + (got[:144] + got[144:])
            for c in range(6):
                value = cots[c] + s_ref[24 * c : 24 * c + 24, :]
                cots[c] = jnp.where(own_rows, value, 0.0)
            for c in range(3):
                through = (w[r, 6 + c] - w[r, c] * ie) * it
                cots[c] = cots[c] + ed * through
                cots.append(-through)
            return cots

        exports(0)
        index = nbr[...]
        nodes[...] = node_of(index >> 8, faces)
        element = index & 255
        columns = jnp.transpose(element)
        lane_iota2 = lax.broadcasted_iota(jnp.int32, (256, 256), 1)
        row_iota2 = lax.broadcasted_iota(jnp.int32, (256, 256), 0)
        for fn in range(FACE):
            at_mat[256 * fn : 256 * fn + 256, :] = one_hot(lane_iota2 == columns[:, fn : fn + 1])
            a_mat[fn] = one_hot(row_iota2 == element[fn : fn + 1])

        owners = jnp.transpose(jnp.concatenate([recv[0], jnp.zeros((6, 128), jnp.int32)], axis=0))
        oids[...] = owners
        lanes = lax.broadcasted_iota(jnp.int32, (SITES, 128), 1)
        for q in range(SEATS):
            ids = oids[pl.ds((q % 2) * SUBS + q // 2, SITES, stride=SEATS), :]
            for z in range(2):
                at = 128 * (2 * q + z)
                oh[:, at : at + 128] = one_hot(lanes == ids[:, z : z + 1])

        def advance(r, ahead):
            forward(r)
            for c in range(9):
                y[r + 1, c] = y[0, c] + ahead * k[r, c]
            exports(r + 1)
            start_all(r + 1, *fwd)

        def retreat(r, adj_part, back_part):
            for c, value in enumerate(back_volume(r)):
                acc[c] = acc[c] + value
                w[r + 1, c] = adj_part * adj24[c] + back_part * value

        back_flux(0)
        sweep(False, True)
        give_back(0)
        meet()
        start_all(0, *fwd)
        start_all(0, *bwd)
        receive(0)
        sweep(True, False)
        advance(0, 0.5 * time_step)
        retreat(0, time_step / 3.0, time_step)

        def looped(r, carry):
            last = r == 2
            back_flux(r)
            receive(r)
            sweep(True, True)
            give_back(r)
            start_all(r, *bwd)
            advance(r, jnp.where(last, time_step, 0.5 * time_step))
            retreat(r, jnp.where(last, time_step / 6.0, time_step / 3.0), 0.5 * time_step)
            return carry

        lax.fori_loop(1, 3, looped, 0)
        back_flux(3)
        receive(3)
        sweep(True, False)
        forward(3, whole=False)

        sums = [jnp.zeros((ROWS, 256), f32) for _ in range(3)]
        for r in range(4):
            for c in range(3):
                through = w[3 - r, 6 + c] - w[3 - r, c] * ie
                sums[0] = sums[0] - w[3 - r, c] * k[r, c]
                sums[1] = sums[1] + through * y[r, c]
                sums[2] = sums[2] - through * k[r, 6 + c]
        grads = [
            jnp.sum(value, axis=0, keepdims=True) * factor
            for value, factor in zip(sums, (ie, it, it))
        ]
        slot = sslot[...]
        place = slot >> 1
        target = ((place & 3) * 2 + ((place >> 2) & 1)) * SITES + (place >> 3)
        chosen = one_hot(lax.broadcasted_iota(jnp.int32, (128, 256), 0) == target)
        lines = [jnp.where((slot & 1) == q, g, 0.0) for q in range(2) for g in grads]
        lines = jnp.concatenate(lines + [jnp.zeros((2, 256), f32)], axis=0)
        lines = [jnp.where(seat == q, lines, 0.0) for q in range(SEATS)]
        lines = jnp.concatenate(lines + [jnp.zeros((64, 256), f32)], axis=0)
        packed = sum(dot(chosen, part) for part in parts3(jnp.transpose(lines)))
        for q in range(SEATS):
            ya[q] = packed[SITES * q : SITES * q + SITES]

        def first_hop(to, slot_from):
            return pltpu.make_async_remote_copy(
                src_ref=ya.at[to],
                dst_ref=yr.at[slot_from],
                send_sem=ps_sem.at[to],
                recv_sem=pr_sem.at[slot_from],
                device_id=seat_device(to),
                device_id_type=MESH,
            )

        def second_hop(to, slot_from):
            return pltpu.make_async_remote_copy(
                src_ref=cb.at[to],
                dst_ref=rc.at[slot_from],
                send_sem=qs_sem.at[to],
                recv_sem=qr_sem.at[slot_from],
                device_id=site_device(to),
                device_id_type=MESH,
            )

        seats = [lax.rem(seat + step, SEATS) for step in range(1, SEATS)]
        sites = [lax.rem(site + step, SITES) for step in range(1, SITES)]
        for other in seats:
            first_hop(other, seat).start()

        sweep(False, True)
        give_back(3)
        start_all(3, *bwd)
        for other in seats:
            first_hop(other, other).wait_recv()
        mine = ya[pl.ds(seat, 1)][0]
        for q in range(SEATS):
            mine = mine + yr[q]
        for q in range(SITES):
            cb[q] = mine[q : q + 1]
        for other in sites:
            second_hop(other, site).start()
        for c, value in enumerate(back_volume(3)):
            out[c] = (acc[c] + value)[:NODES]

        for other in sites:
            second_hop(other, other).wait_recv()
        here = lax.broadcasted_iota(jnp.int32, (SITES, 128), 0) == site
        came = jnp.concatenate([rc[q] for q in range(SITES)], axis=0)
        came = came + jnp.where(here, mine, 0.0)
        turned = jnp.concatenate(parts3(jnp.transpose(came)[:64]), axis=0)
        spread = dot(turned, oh[...])
        spread = spread[:64] + spread[64:128] + spread[128:]
        total = jnp.zeros((3, 128), f32)
        for q in range(SEATS):
            for z in range(2):
                row, at = 8 * q + 3 * z, 128 * (2 * q + z)
                total = total + spread[row : row + 3, at : at + 128]
        therm[...] = total[:, :64]

        for r in range(4):
            wait_send_all(r, *fwd)
            wait_send_all(r, *bwd)
        for other in seats:
            first_hop(other, seat).wait_send()
        for other in sites:
            second_hop(other, site).wait_send()

    return kernel


def per_device(
    field_state,
    adjoint,
    eps_inf,
    eps_delta,
    relax_time,
    metric,
    face_scale,
    face_angles,
    nbr_index,
    dom_export,
    sub_export,
    send_slot,
    recv_index,
):
    table, faces = host_tables()
    stage = pltpu.VMEM((4, 9, ROWS, 256), f32)
    trace = pltpu.VMEM((6, FACE, 256), f32)
    message = pltpu.VMEM((4, BLOCKS, 8, 128), f32)
    semaphores = pltpu.SemaphoreType.DMA((4, BLOCKS))
    state = pltpu.VMEM((9, ROWS, 256), f32)
    values = (
        field_state,
        adjoint,
        eps_inf.reshape(1, 256),
        eps_delta.reshape(1, 256),
        relax_time.reshape(1, 256),
        metric,
        face_scale,
        face_angles,
        nbr_index,
        dom_export.reshape(2, 128),
        sub_export,
        send_slot.reshape(1, 256),
        jnp.transpose(recv_index, (0, 2, 1)),
        jnp.asarray(table),
    )
    scratch = [pltpu.VMEM(value.shape, value.dtype) for value in values] + [
        pltpu.SemaphoreType.DMA((len(values),)),
        stage, stage, stage, state, state,
        pltpu.VMEM((3, FACE, 256), f32),
        pltpu.VMEM((FACE, 256), f32),
        pltpu.VMEM((6, 112, 256), f32),
        pltpu.VMEM((6, 112, 256), f32),
        trace, trace, trace,
        pltpu.VMEM((6 * ROWS, 256), f32),
        pltpu.VMEM((6, ROWS, 256), f32),
        pltpu.VMEM((12 * ROWS, 256), bf16),
        pltpu.VMEM((FACE, 256), jnp.int32),
        pltpu.VMEM((8, 128), jnp.int32),
        pltpu.VMEM((FACE, 256, 256), bf16),
        pltpu.VMEM((FACE * 256, 256), bf16),
        pltpu.VMEM((256, 128 * BLOCKS), bf16),
        pltpu.VMEM((128 * BLOCKS, 256), bf16),
        pltpu.VMEM((12 * ROWS, 256 * GROUP), bf16),
        pltpu.VMEM((12 * ROWS, 128 * BLOCKS), bf16),
        pltpu.VMEM((128, 8), jnp.int32),
        pltpu.VMEM((SITES, 128 * 2 * SEATS), bf16),
        message, message, message, message,
        pltpu.VMEM((SEATS, SITES, 128), f32),
        pltpu.VMEM((SEATS, SITES, 128), f32),
        pltpu.VMEM((SITES, 1, 128), f32),
        pltpu.VMEM((SITES, 1, 128), f32),
        semaphores, semaphores, semaphores, semaphores,
        pltpu.SemaphoreType.DMA((SEATS,)),
        pltpu.SemaphoreType.DMA((SEATS,)),
        pltpu.SemaphoreType.DMA((SITES,)),
        pltpu.SemaphoreType.DMA((SITES,)),
    ]
    call = pl.pallas_call(
        kernel_of(faces),
        out_shape=(
            jax.ShapeDtypeStruct((9, NODES, 256), f32),
            jax.ShapeDtypeStruct((3, 64), f32),
        ),
        in_specs=[pl.BlockSpec(memory_space=pltpu.HBM)] * 14,
        out_specs=(
            pl.BlockSpec(memory_space=pltpu.VMEM),
            pl.BlockSpec(memory_space=pltpu.VMEM),
        ),
        scratch_shapes=scratch,
        compiler_params=pltpu.CompilerParams(
            collective_id=0, has_side_effects=True, vmem_limit_bytes=32 << 20
        ),
        name="reverse_step",
    )
    return call(*[pltpu.with_memory_space_constraint(v, pltpu.HBM) for v in values])


def solution(mesh):
    both = ("dom", "sub")
    return jax.shard_map(
        per_device,
        mesh=mesh,
        in_specs=(
            P(None, None, both),
            P(None, None, both),
            P(both),
            P(both),
            P(both),
            P(None, both),
            P(None, both),
            P(None, None, both),
            P(None, both),
            P(both),
            P(both, None, None),
            P(both),
            P(both, None, None),
        ),
        out_specs=(P(None, None, both), P(None, both)),
        check_vma=False,
    )
```

```python
import math

import jax
import jax.numpy as jnp
import numpy as np
from jax import lax
from jax.experimental import pallas as pl
from jax.experimental.pallas import tpu as pltpu
from jax.sharding import PartitionSpec as P

time_step = 0.014
f32 = jnp.float32
bf16 = jnp.bfloat16
NODES = 20
ROWS = 24
FACE = 40
DOMS = 32
SUBS = 4
BLOCKS = 6
SEATS = 8
SITES = 16
GROUP = 8
MESH = pl.DeviceIdType.MESH


def mat_mul(left, right):
    inner = len(right)
    return [
        [
            sum((left[row_no][k] * right[k][col_no] for k in range(inner)))
            for col_no in range(len(right[0]))
        ]
        for row_no in range(len(left))
    ]


def transposed(matrix):
    return [list(column) for column in zip(*matrix)]


def solve_linear(matrix, rhs_rows):
    order = len(matrix)
    work = [list(matrix[row_no]) + list(rhs_rows[row_no]) for row_no in range(order)]
    for col_no in range(order):

        def magnitude(row_no):
            return abs(work[row_no][col_no])

        pivot = max(range(col_no, order), key=magnitude)
        work[col_no], work[pivot] = (work[pivot], work[col_no])
        head = work[col_no][col_no]
        work[col_no] = [value / head for value in work[col_no]]
        for row_no in range(order):
            if row_no != col_no:
                factor = work[row_no][col_no]
                work[row_no] = [
                    value - factor * other for value, other in zip(work[row_no], work[col_no])
                ]
    return [row[order:] for row in work]


def reference_element():
    lattice = [(i, j, k) for k in range(4) for j in range(4 - k) for i in range(4 - j - k)]
    points = [[float(v) / 3.0 for v in node] for node in lattice]
    vander = [[0.0] * 20 for node_no in range(20)]
    slopes = [[[0.0] * 20 for node_no in range(20)] for axis_no in range(3)]
    for node_no in range(20):
        for mono_no in range(20):
            power = lattice[mono_no]
            value = 1.0
            for axis_no in range(3):
                value *= points[node_no][axis_no] ** power[axis_no]
            vander[node_no][mono_no] = value
            for axis_no in range(3):
                if power[axis_no] > 0:
                    term = float(power[axis_no])
                    for other_no in range(3):
                        expo_val = power[other_no] - (1 if other_no == axis_no else 0)
                        term *= points[node_no][other_no] ** expo_val
                    slopes[axis_no][node_no][mono_no] = term
    identity = [[1.0 if row_no == col_no else 0.0 for col_no in range(20)] for row_no in range(20)]
    inverse = solve_linear(vander, identity)
    deriv_mats = [mat_mul(slopes[axis_no], inverse) for axis_no in range(3)]
    fact = math.factorial

    def face_integral(face_no, a, b, c):
        if face_no == 0:
            return 0.0 if c > 0 else fact(a) * fact(b) / fact(a + b + 2)
        if face_no == 1:
            return 0.0 if b > 0 else fact(a) * fact(c) / fact(a + c + 2)
        if face_no == 2:
            return math.sqrt(3.0) * fact(a) * fact(b) * fact(c) / fact(a + b + c + 2)
        return 0.0 if a > 0 else fact(b) * fact(c) / fact(b + c + 2)

    inverse_t = transposed(inverse)
    mono_mass = [[0.0] * 20 for node_no in range(20)]
    for first_no in range(20):
        for second_no in range(20):
            a = lattice[first_no][0] + lattice[second_no][0]
            b = lattice[first_no][1] + lattice[second_no][1]
            c = lattice[first_no][2] + lattice[second_no][2]
            mono_mass[first_no][second_no] = fact(a) * fact(b) * fact(c) / fact(a + b + c + 3)
    mass_mat = mat_mul(mat_mul(inverse_t, mono_mass), inverse)
    columns = [[] for node_no in range(20)]
    index_list = []
    for face_no in range(4):
        mono_face = [[0.0] * 20 for node_no in range(20)]
        for first_no in range(20):
            for second_no in range(20):
                a = lattice[first_no][0] + lattice[second_no][0]
                b = lattice[first_no][1] + lattice[second_no][1]
                c = lattice[first_no][2] + lattice[second_no][2]
                mono_face[first_no][second_no] = face_integral(face_no, a, b, c)
        face_mass = mat_mul(mat_mul(inverse_t, mono_face), inverse)
        tests = [k == 0 for i, j, k in lattice]
        if face_no == 1:
            tests = [j == 0 for i, j, k in lattice]
        if face_no == 2:
            tests = [i + j + k == 3 for i, j, k in lattice]
        if face_no == 3:
            tests = [i == 0 for i, j, k in lattice]
        chosen = [node_no for node_no in range(20) if tests[node_no]]
        for row_no in range(20):
            columns[row_no].extend([face_mass[row_no][col_no] for col_no in chosen])
        index_list.extend(chosen)
    lift_mat = solve_linear(mass_mat, columns)
    return (deriv_mats, lift_mat, index_list)


def host_tables():
    deriv, lift, faces = reference_element()
    deriv = np.asarray(deriv, np.float32)
    lift = np.asarray(lift, np.float32)
    pick = np.zeros((NODES, FACE), np.float32)
    pick[np.asarray(faces), np.arange(FACE)] = 1.0

    def placed(rows, cols, parts):
        result = np.zeros((rows, cols), np.float32)
        for at, part in parts:
            result[: part.shape[0], at : at + part.shape[1]] = part
        return result

    forward = placed(ROWS, 112, [(0, lift)] + [(40 + 24 * d, deriv[d]) for d in range(3)])
    backward = placed(ROWS, 112, [(0, pick)] + [(40 + 24 * d, deriv[d].T) for d in range(3)])
    lift_t = placed(FACE, ROWS, [(0, lift.T)])
    pick_t = placed(FACE, ROWS, [(0, pick.T)])

    def split(matrix):
        high = matrix.astype(jnp.bfloat16).astype(np.float32)
        low = matrix - high
        return np.concatenate(
            [np.concatenate([high, high], 1), np.concatenate([low, np.zeros_like(low)], 1)], 0
        )

    table = np.zeros((224, 256), np.float32)
    table[0:48, 0:224] = split(forward)
    table[48:96, 0:224] = split(backward)
    table[96:176, 0:48] = split(lift_t)
    table[176:216, 0:48] = np.concatenate([pick_t, pick_t], 1)
    return table.astype(jnp.bfloat16), [int(v) for v in faces]


def stacked(values):
    high = values.astype(bf16).astype(f32)
    return jnp.concatenate([high, values - high], axis=0).astype(bf16)


def parts3(values):
    first = values.astype(bf16)
    rest = values - first.astype(f32)
    second = rest.astype(bf16)
    third = (rest - second.astype(f32)).astype(bf16)
    return first, second, third


def dot(left, right):
    return jnp.dot(left, right, preferred_element_type=f32)


def node_of(rows, faces):
    result = rows - 20
    for row, node in enumerate(faces):
        result = jnp.where(rows == row, node, result)
    return result


def one_hot(condition):
    return jnp.where(condition, 1.0, 0.0).astype(bf16)


def kernel_of(faces):
    def kernel(
        *refs,
    ):
        given, refs = refs[:14], refs[14:]
        out, therm = refs[:2]
        held, in_sem, refs = refs[2:16], refs[16], refs[17:]
        fs, adj, einf, edel, tau, met, fsc, ang, nbr, dexp, sexp, sslot, recv, tab = held
        (
        y, k, w, adj24, acc, nrm, scl, x, xb, p, nb, cd, s_ref, pool, pp, nodes, nodex,
        elems, a_mat, at_mat, ax, axt, b_mat, bx, oids, oh,
        sf, rf, sb, rb, ya, yr, cb, rc,
        fs_sem, fr_sem, bs_sem, br_sem, ps_sem, pr_sem, qs_sem, qr_sem,
        ) = refs

        def fetch(i):
            return pltpu.make_async_copy(given[i], held[i], in_sem.at[i])

        order = (10, 9, 0, 13, 8, 1, 2, 4, 3, 7, 6, 5, 11, 12)
        for i in order:
            fetch(i).start()

        dom = lax.axis_index("dom")
        sub = lax.axis_index("sub")

        rf[...] = jnp.zeros_like(rf)
        rb[...] = jnp.zeros_like(rb)
        yr[...] = jnp.zeros_like(yr)
        rc[...] = jnp.zeros_like(rc)
        barrier = pltpu.get_barrier_semaphore()
        core = lax.rem(dom, 2)
        site = dom // 2
        seat = sub * 2 + core

        def seat_device(other):
            return (site * 2 + lax.rem(other, 2), other // 2)

        def site_device(other):
            return (other * 2 + core, sub)

        def greet(device):
            pl.semaphore_signal(barrier, inc=1, device_id=device, device_id_type=MESH)

        for step in range(1, SEATS):
            greet(seat_device(lax.rem(seat + step, SEATS)))
        for step in range(1, SITES):
            greet(site_device(lax.rem(site + step, SITES)))
        has_low = dom > 0
        has_high = dom < DOMS - 1

        @pl.when(has_low & (core == 0))
        def _():
            greet((dom - 1, sub))

        @pl.when(has_high & (core == 1))
        def _():
            greet((dom + 1, sub))

        def meet():
            outside = (has_low & (core == 0)) | (has_high & (core == 1))
            pl.semaphore_wait(barrier, jnp.where(outside, SEATS + SITES - 1, SEATS + SITES - 2))

        for i in order:
            fetch(i).wait()
        ie = 1.0 / einf[...]
        it = 1.0 / tau[...]
        ed = edel[...]
        pad = jnp.zeros((ROWS - NODES, 256), f32)
        for c in range(9):
            y[0, c] = jnp.concatenate([fs[c], pad], axis=0)
            value = jnp.concatenate([adj[c], pad], axis=0)
            adj24[c] = value
            acc[c] = value
            w[0, c] = (time_step / 6.0) * value
        sin_a = jnp.sin(ang[0])
        normals = (sin_a * jnp.cos(ang[1]), sin_a * jnp.sin(ang[1]), jnp.cos(ang[0]))
        for face in range(4):
            here = slice(10 * face, 10 * face + 10)
            for i in range(3):
                nrm[i, here, :] = jnp.broadcast_to(normals[i][face : face + 1], (10, 256))
            scl[here, :] = jnp.broadcast_to(0.5 * fsc[face : face + 1, :], (10, 256))

        exported = jnp.concatenate([sexp[0], dexp[...], jnp.zeros((2, 128), jnp.int32)], axis=0)
        nodex[...] = node_of(exported >> 8, faces)
        export_el = exported & 255
        export_cols = jnp.transpose(export_el)
        row_iota = lax.broadcasted_iota(jnp.int32, (256, 128), 0)
        lane_iota = lax.broadcasted_iota(jnp.int32, (128, 256), 1)
        for blk in range(BLOCKS):
            here = slice(128 * blk, 128 * blk + 128)
            ax[:, here] = one_hot(row_iota == export_el[blk : blk + 1])
            axt[here, :] = one_hot(lane_iota == export_cols[:, blk : blk + 1])

        def sub_copy(r, src, dst, send, recv_s, to, slot_from):
            return pltpu.make_async_remote_copy(
                src_ref=src.at[r, to],
                dst_ref=dst.at[r, slot_from],
                send_sem=send.at[r, to],
                recv_sem=recv_s.at[r, slot_from],
                device_id=(dom, to),
                device_id_type=MESH,
            )

        def dom_copy(r, src, dst, send, recv_s, block, slot, to):
            return pltpu.make_async_remote_copy(
                src_ref=src.at[r, block],
                dst_ref=dst.at[r, slot],
                send_sem=send.at[r, block],
                recv_sem=recv_s.at[r, slot],
                device_id=(to, sub),
                device_id_type=MESH,
            )

        def start_all(r, src, dst, send, recv_s):
            for step in range(1, SUBS):
                to = lax.rem(sub + step, SUBS)
                sub_copy(r, src, dst, send, recv_s, to, sub).start()

            @pl.when(has_low)
            def _():
                dom_copy(r, src, dst, send, recv_s, 4, 5, dom - 1).start()

            @pl.when(has_high)
            def _():
                dom_copy(r, src, dst, send, recv_s, 5, 4, dom + 1).start()

        def wait_recv_all(r, src, dst, send, recv_s):
            for step in range(1, SUBS):
                other = lax.rem(sub + step, SUBS)
                sub_copy(r, src, dst, send, recv_s, other, other).wait_recv()

            @pl.when(has_low)
            def _():
                dom_copy(r, src, dst, send, recv_s, 4, 4, dom - 1).wait_recv()

            @pl.when(has_high)
            def _():
                dom_copy(r, src, dst, send, recv_s, 5, 5, dom + 1).wait_recv()

        def wait_send_all(r, src, dst, send, recv_s):
            for step in range(1, SUBS):
                to = lax.rem(sub + step, SUBS)
                sub_copy(r, src, dst, send, recv_s, to, sub).wait_send()

            @pl.when(has_low)
            def _():
                dom_copy(r, src, dst, send, recv_s, 4, 5, dom - 1).wait_send()

            @pl.when(has_high)
            def _():
                dom_copy(r, src, dst, send, recv_s, 5, 4, dom + 1).wait_send()

        fwd = (sf, rf, fs_sem, fr_sem)
        bwd = (sb, rb, bs_sem, br_sem)

        node_iota = lax.broadcasted_iota(jnp.int32, (ROWS, 128), 0)
        node_iota2 = lax.broadcasted_iota(jnp.int32, (ROWS, 256), 0)
        own_rows = node_iota2 < NODES

        def fold_pool():
            values = pool[...].reshape(6 * ROWS, 256)
            high = values.astype(bf16)
            pp[0:144, :] = high
            pp[144:288, :] = (values - high.astype(f32)).astype(bf16)

        def exports(r):
            for c in range(6):
                pool[c] = y[r, c]
            fold_pool()
            for pair in range(BLOCKS // 2):
                both = dot(pp[...], ax[:, 256 * pair : 256 * pair + 256])
                both = both[:144] + both[144:]
                for half in range(2):
                    blk = 2 * pair + half
                    got = both[:, 128 * half : 128 * half + 128]
                    keep = node_iota == nodex[blk : blk + 1, :]
                    for c in range(6):
                        sf[r, blk, c : c + 1, :] = jnp.sum(
                            jnp.where(keep, got[24 * c : 24 * c + 24], 0.0), axis=0, keepdims=True
                        )
        def flux_rows(src, at):
            here = slice(at, at + 8)
            n = [nrm[i, here, :] for i in range(3)]
            e = [src[i, here, :] for i in range(3)]
            h = [src[3 + i, here, :] for i in range(3)]
            ne = n[0] * e[0] + n[1] * e[1] + n[2] * e[2]
            nh = n[0] * h[0] + n[1] * h[1] + n[2] * h[2]
            result = []
            for i in range(3):
                j, l = (i + 1) % 3, (i + 2) % 3
                result.append(n[i] * ne - e[i] - (n[j] * h[l] - n[l] * h[j]))
            for i in range(3):
                j, l = (i + 1) % 3, (i + 2) % 3
                result.append((n[j] * e[l] - n[l] * e[j]) + n[i] * nh - h[i])
            return result

        def curl_rows(x, e, h):
            for d in range(3):
                m = [met[3 * d + i : 3 * d + i + 1, :] for i in range(3)]
                here = slice(40 + 24 * d, 64 + 24 * d)
                for i in range(3):
                    j, l = (i + 1) % 3, (i + 2) % 3
                    x[i, here, :] = m[j] * h[l] - m[l] * h[j]
                    x[3 + i, here, :] = m[l] * e[j] - m[j] * e[l]

        def contracted(x, first, c):
            got = dot(tab[first : first + 48, 0:224], stacked(x[c]))
            return got[:24] + got[24:]

        def back_flux(r):
            for c in range(6):
                value = w[r, c]
                if c < 3:
                    value = value * ie
                got = dot(tab[96:176, 0:48], stacked(value))
                p[c] = (got[:40] + got[40:]) * scl[...]
            for at in range(0, FACE, 8):
                for c, value in enumerate(flux_rows(p, at)):
                    cd[c, at : at + 8, :] = value

        def sweep(gather, scatter):
            def group(g, carry):
                for j in range(GROUP):
                    fn = g * GROUP + j
                    keep = node_iota2 == nodes[pl.ds(fn, 1), :]
                    if gather:
                        got = dot(pp[...], a_mat[fn])
                        got = got[:144] + got[144:]
                        for c in range(6):
                            nb[c, pl.ds(fn, 1), :] = jnp.sum(
                                jnp.where(keep, got[24 * c : 24 * c + 24], 0.0),
                                axis=0,
                                keepdims=True,
                            )
                    if scatter:
                        high, low = [], []
                        for c in range(6):
                            value = cd[c, pl.ds(fn, 1), :]
                            top = value.astype(bf16).astype(f32)
                            high.append(jnp.where(keep, top, 0.0))
                            low.append(jnp.where(keep, value - top, 0.0))
                        b_mat[:, 256 * j : 256 * j + 256] = jnp.concatenate(high + low, 0).astype(
                            bf16
                        )
                if scatter:
                    span = GROUP * 256
                    got = dot(b_mat[...], at_mat[pl.ds(pl.multiple_of(g * span, span), span), :])
                    s_ref[...] = s_ref[...] - (got[:144] + got[144:])
                return carry

            if scatter:
                s_ref[...] = jnp.zeros_like(s_ref)
            lax.fori_loop(0, FACE // GROUP, group, 0)

        def give_back(r):
            for c in range(6):
                rows = s_ref[24 * c + 20 : 24 * c + 24, :]
                for blk in range(4):
                    at = 128 * (blk % 2)
                    sb[r, blk, c : c + 1, :] = rows[blk // 2 : blk // 2 + 1, at : at + 128]
                sb[r, 4, c : c + 1, :] = rows[2:3, 0:128]
                sb[r, 5, c : c + 1, :] = rows[3:4, 128:256]

        def arrived(r, blk, dst, src):
            value = dst[r, blk]
            if blk < SUBS:
                value = jnp.where(sub == blk, src[r, blk], value)
            return value

        def receive(r):
            wait_recv_all(r, *fwd)
            for blk in range(4):
                value = arrived(r, blk, rf, sf)
                at = 128 * (blk % 2)
                for c in range(6):
                    row = 20 + blk // 2
                    pool[c, row : row + 1, at : at + 128] = value[c : c + 1]
            low, high = rf[r, 4], rf[r, 5]
            for c in range(6):
                pool[c, 22:23, 0:128] = low[c : c + 1]
                pool[c, 23:24, 128:256] = high[c : c + 1]
            fold_pool()

        def forward(r, whole=True):
            for c in range(6):
                p[c] = dot(tab[176:216, 0:48], stacked(y[r, c])) - nb[c]
            for at in range(0, FACE, 8):
                factor = scl[at : at + 8, :]
                for c, value in enumerate(flux_rows(p, at)):
                    x[c, at : at + 8, :] = value * factor
            curl_rows(x, [y[r, c] for c in range(3)], [y[r, 3 + c] for c in range(3)])
            for c in range(3):
                current = (ed * y[r, c] - y[r, 6 + c]) * it
                k[r, 6 + c] = current
                k[r, c] = (contracted(x, 0, c) - current) * ie
                if whole:
                    k[r, 3 + c] = contracted(x, 0, 3 + c)

        def back_volume(r):
            for c in range(6):
                xb[c, 0:40, :] = cd[c]
            curl_rows(xb, [w[r, c] * ie for c in range(3)], [w[r, 3 + c] for c in range(3)])
            cots = [contracted(xb, 48, c) for c in range(6)]
            wait_recv_all(r, *bwd)
            for blk in range(BLOCKS):
                value = arrived(r, blk, rb, sb)
                keep = node_iota == nodex[blk : blk + 1, :]
                top = value.astype(bf16).astype(f32)
                rest = value - top
                high = [jnp.where(keep, top[c : c + 1], 0.0) for c in range(6)]
                low = [jnp.where(keep, rest[c : c + 1], 0.0) for c in range(6)]
                bx[:, 128 * blk : 128 * blk + 128] = jnp.concatenate(high + low, 0).astype(bf16)
            got = dot(bx[...], axt[...])
            s_ref[...] = s_ref[...] + (got[:144] + got[144:])
            for c in range(6):
                value = cots[c] + s_ref[24 * c : 24 * c + 24, :]
                cots[c] = jnp.where(own_rows, value, 0.0)
            for c in range(3):
                through = (w[r, 6 + c] - w[r, c] * ie) * it
                cots[c] = cots[c] + ed * through
                cots.append(-through)
            return cots

        index = nbr[...]
        nodes[...] = node_of(index >> 8, faces)
        element = index & 255
        elems[...] = element
        lane_iota2 = lax.broadcasted_iota(jnp.int32, (256, 256), 1)
        row_iota2 = lax.broadcasted_iota(jnp.int32, (256, 256), 0)

        def build(g, carry):
            rows = elems[pl.ds(pl.multiple_of(g * 8, 8), 8), :]
            columns = jnp.transpose(rows)
            for j in range(8):
                a_mat[g * 8 + j] = one_hot(row_iota2 == rows[j : j + 1])
                at = pl.multiple_of(g * 2048 + 256 * j, 256)
                at_mat[pl.ds(at, 256), :] = one_hot(lane_iota2 == columns[:, j : j + 1])
            return carry

        lax.fori_loop(0, FACE // 8, build, 0)
        owners = jnp.transpose(jnp.concatenate([recv[0], jnp.zeros((6, 128), jnp.int32)], axis=0))
        oids[...] = owners
        lanes = lax.broadcasted_iota(jnp.int32, (SITES, 128), 1)
        for q in range(SEATS):
            ids = oids[pl.ds((q % 2) * SUBS + q // 2, SITES, stride=SEATS), :]
            for z in range(2):
                at = 128 * (2 * q + z)
                oh[:, at : at + 128] = one_hot(lanes == ids[:, z : z + 1])

        def first_hop(to, slot_from):
            return pltpu.make_async_remote_copy(
                src_ref=ya.at[to],
                dst_ref=yr.at[slot_from],
                send_sem=ps_sem.at[to],
                recv_sem=pr_sem.at[slot_from],
                device_id=seat_device(to),
                device_id_type=MESH,
            )

        def second_hop(to, slot_from):
            return pltpu.make_async_remote_copy(
                src_ref=cb.at[to],
                dst_ref=rc.at[slot_from],
                send_sem=qs_sem.at[to],
                recv_sem=qr_sem.at[slot_from],
                device_id=site_device(to),
                device_id_type=MESH,
            )

        seats = [lax.rem(seat + step, SEATS) for step in range(1, SEATS)]
        sites = [lax.rem(site + step, SITES) for step in range(1, SITES)]
        meet()

        def one_round(r, carry):
            exports(r)
            start_all(r, *fwd)
            back_flux(r)
            sweep(False, True)
            give_back(r)
            start_all(r, *bwd)
            receive(r)
            sweep(True, False)
            forward(r)

            @pl.when(r < 3)
            def _():
                ahead = jnp.where(r == 2, time_step, 0.5 * time_step)
                for c in range(9):
                    y[r + 1, c] = y[0, c] + ahead * k[r, c]

            @pl.when(r == 3)
            def _():
                sums = [jnp.zeros((ROWS, 256), f32) for _ in range(3)]
                for q in range(4):
                    for c in range(3):
                        through = w[3 - q, 6 + c] - w[3 - q, c] * ie
                        sums[0] = sums[0] - w[3 - q, c] * k[q, c]
                        sums[1] = sums[1] + through * y[q, c]
                        sums[2] = sums[2] - through * k[q, 6 + c]
                grads = [
                    jnp.sum(value, axis=0, keepdims=True) * factor
                    for value, factor in zip(sums, (ie, it, it))
                ]
                slot = sslot[...]
                place = slot >> 1
                target = ((place & 3) * 2 + ((place >> 2) & 1)) * SITES + (place >> 3)
                chosen = one_hot(lax.broadcasted_iota(jnp.int32, (128, 256), 0) == target)
                lines = [jnp.where((slot & 1) == q, g, 0.0) for q in range(2) for g in grads]
                lines = jnp.concatenate(lines + [jnp.zeros((2, 256), f32)], axis=0)
                lines = [jnp.where(seat == q, lines, 0.0) for q in range(SEATS)]
                lines = jnp.concatenate(lines + [jnp.zeros((64, 256), f32)], axis=0)
                packed = sum(dot(chosen, part) for part in parts3(jnp.transpose(lines)))
                for q in range(SEATS):
                    ya[q] = packed[SITES * q : SITES * q + SITES]

                for other in seats:
                    first_hop(other, seat).start()

            adj_part = jnp.where(r == 2, time_step / 6.0, time_step / 3.0)
            back_part = jnp.where(r == 0, time_step, 0.5 * time_step)
            back = back_volume(r)
            for c in range(9):
                acc[c] = acc[c] + back[c]

            @pl.when(r < 3)
            def _():
                for c in range(9):
                    w[r + 1, c] = adj_part * adj24[c] + back_part * back[c]

            return carry

        lax.fori_loop(0, 4, one_round, 0)

        for other in seats:
            first_hop(other, other).wait_recv()
        mine = ya[pl.ds(seat, 1)][0]
        for q in range(SEATS):
            mine = mine + yr[q]
        for q in range(SITES):
            cb[q] = mine[q : q + 1]
        for other in sites:
            second_hop(other, site).start()
        for c in range(9):
            out[c] = acc[c][:NODES]

        for other in sites:
            second_hop(other, other).wait_recv()
        here = lax.broadcasted_iota(jnp.int32, (SITES, 128), 0) == site
        came = jnp.concatenate([rc[q] for q in range(SITES)], axis=0)
        came = came + jnp.where(here, mine, 0.0)
        turned = jnp.concatenate(parts3(jnp.transpose(came)[:64]), axis=0)
        spread = dot(turned, oh[...])
        spread = spread[:64] + spread[64:128] + spread[128:]
        total = jnp.zeros((3, 128), f32)
        for q in range(SEATS):
            for z in range(2):
                row, at = 8 * q + 3 * z, 128 * (2 * q + z)
                total = total + spread[row : row + 3, at : at + 128]
        therm[...] = total[:, :64]

        def all_sent(r, carry):
            wait_send_all(r, *fwd)
            wait_send_all(r, *bwd)
            return carry

        lax.fori_loop(0, 4, all_sent, 0)
        for other in seats:
            first_hop(other, seat).wait_send()
        for other in sites:
            second_hop(other, site).wait_send()

    return kernel


def per_device(
    field_state,
    adjoint,
    eps_inf,
    eps_delta,
    relax_time,
    metric,
    face_scale,
    face_angles,
    nbr_index,
    dom_export,
    sub_export,
    send_slot,
    recv_index,
):
    table, faces = host_tables()
    stage = pltpu.VMEM((4, 9, ROWS, 256), f32)
    trace = pltpu.VMEM((6, FACE, 256), f32)
    message = pltpu.VMEM((4, BLOCKS, 8, 128), f32)
    semaphores = pltpu.SemaphoreType.DMA((4, BLOCKS))
    state = pltpu.VMEM((9, ROWS, 256), f32)
    values = (
        field_state,
        adjoint,
        eps_inf.reshape(1, 256),
        eps_delta.reshape(1, 256),
        relax_time.reshape(1, 256),
        metric,
        face_scale,
        face_angles,
        nbr_index,
        dom_export.reshape(2, 128),
        sub_export,
        send_slot.reshape(1, 256),
        jnp.transpose(recv_index, (0, 2, 1)),
        jnp.asarray(table),
    )
    scratch = [pltpu.VMEM(value.shape, value.dtype) for value in values] + [
        pltpu.SemaphoreType.DMA((len(values),)),
        stage, stage, stage, state, state,
        pltpu.VMEM((3, FACE, 256), f32),
        pltpu.VMEM((FACE, 256), f32),
        pltpu.VMEM((6, 112, 256), f32),
        pltpu.VMEM((6, 112, 256), f32),
        trace, trace, trace,
        pltpu.VMEM((6 * ROWS, 256), f32),
        pltpu.VMEM((6, ROWS, 256), f32),
        pltpu.VMEM((12 * ROWS, 256), bf16),
        pltpu.VMEM((FACE, 256), jnp.int32),
        pltpu.VMEM((8, 128), jnp.int32),
        pltpu.VMEM((FACE, 256), jnp.int32),
        pltpu.VMEM((FACE, 256, 256), bf16),
        pltpu.VMEM((FACE * 256, 256), bf16),
        pltpu.VMEM((256, 128 * BLOCKS), bf16),
        pltpu.VMEM((128 * BLOCKS, 256), bf16),
        pltpu.VMEM((12 * ROWS, 256 * GROUP), bf16),
        pltpu.VMEM((12 * ROWS, 128 * BLOCKS), bf16),
        pltpu.VMEM((128, 8), jnp.int32),
        pltpu.VMEM((SITES, 128 * 2 * SEATS), bf16),
        message, message, message, message,
        pltpu.VMEM((SEATS, SITES, 128), f32),
        pltpu.VMEM((SEATS, SITES, 128), f32),
        pltpu.VMEM((SITES, 1, 128), f32),
        pltpu.VMEM((SITES, 1, 128), f32),
        semaphores, semaphores, semaphores, semaphores,
        pltpu.SemaphoreType.DMA((SEATS,)),
        pltpu.SemaphoreType.DMA((SEATS,)),
        pltpu.SemaphoreType.DMA((SITES,)),
        pltpu.SemaphoreType.DMA((SITES,)),
    ]
    call = pl.pallas_call(
        kernel_of(faces),
        out_shape=(
            jax.ShapeDtypeStruct((9, NODES, 256), f32),
            jax.ShapeDtypeStruct((3, 64), f32),
        ),
        in_specs=[pl.BlockSpec(memory_space=pltpu.HBM)] * 14,
        out_specs=(
            pl.BlockSpec(memory_space=pltpu.VMEM),
            pl.BlockSpec(memory_space=pltpu.VMEM),
        ),
        scratch_shapes=scratch,
        compiler_params=pltpu.CompilerParams(
            collective_id=0, has_side_effects=True, vmem_limit_bytes=32 << 20
        ),
        name="reverse_step",
    )
    return call(*[pltpu.with_memory_space_constraint(v, pltpu.HBM) for v in values])


def solution(mesh):
    both = ("dom", "sub")
    return jax.shard_map(
        per_device,
        mesh=mesh,
        in_specs=(
            P(None, None, both),
            P(None, None, both),
            P(both),
            P(both),
            P(both),
            P(None, both),
            P(None, both),
            P(None, None, both),
            P(None, both),
            P(both),
            P(both, None, None),
            P(both),
            P(both, None, None),
        ),
        out_specs=(P(None, None, both), P(None, both)),
        check_vma=False,
    )
```

```python
import math

import jax
import jax.numpy as jnp
import numpy as np
from jax import lax
from jax.experimental import pallas as pl
from jax.experimental.pallas import tpu as pltpu
from jax.sharding import PartitionSpec as P

time_step = 0.014
f32 = jnp.float32
bf16 = jnp.bfloat16
NODES = 20
ROWS = 24
FACE = 40
DOMS = 32
SUBS = 4
BLOCKS = 6
SEATS = 8
SITES = 16
GROUP = 8
MESH = pl.DeviceIdType.MESH


def mat_mul(left, right):
    inner = len(right)
    return [
        [
            sum((left[row_no][k] * right[k][col_no] for k in range(inner)))
            for col_no in range(len(right[0]))
        ]
        for row_no in range(len(left))
    ]


def transposed(matrix):
    return [list(column) for column in zip(*matrix)]


def solve_linear(matrix, rhs_rows):
    order = len(matrix)
    work = [list(matrix[row_no]) + list(rhs_rows[row_no]) for row_no in range(order)]
    for col_no in range(order):

        def magnitude(row_no):
            return abs(work[row_no][col_no])

        pivot = max(range(col_no, order), key=magnitude)
        work[col_no], work[pivot] = (work[pivot], work[col_no])
        head = work[col_no][col_no]
        work[col_no] = [value / head for value in work[col_no]]
        for row_no in range(order):
            if row_no != col_no:
                factor = work[row_no][col_no]
                work[row_no] = [
                    value - factor * other for value, other in zip(work[row_no], work[col_no])
                ]
    return [row[order:] for row in work]


def reference_element():
    lattice = [(i, j, k) for k in range(4) for j in range(4 - k) for i in range(4 - j - k)]
    points = [[float(v) / 3.0 for v in node] for node in lattice]
    vander = [[0.0] * 20 for node_no in range(20)]
    slopes = [[[0.0] * 20 for node_no in range(20)] for axis_no in range(3)]
    for node_no in range(20):
        for mono_no in range(20):
            power = lattice[mono_no]
            value = 1.0
            for axis_no in range(3):
                value *= points[node_no][axis_no] ** power[axis_no]
            vander[node_no][mono_no] = value
            for axis_no in range(3):
                if power[axis_no] > 0:
                    term = float(power[axis_no])
                    for other_no in range(3):
                        expo_val = power[other_no] - (1 if other_no == axis_no else 0)
                        term *= points[node_no][other_no] ** expo_val
                    slopes[axis_no][node_no][mono_no] = term
    identity = [[1.0 if row_no == col_no else 0.0 for col_no in range(20)] for row_no in range(20)]
    inverse = solve_linear(vander, identity)
    deriv_mats = [mat_mul(slopes[axis_no], inverse) for axis_no in range(3)]
    fact = math.factorial

    def face_integral(face_no, a, b, c):
        if face_no == 0:
            return 0.0 if c > 0 else fact(a) * fact(b) / fact(a + b + 2)
        if face_no == 1:
            return 0.0 if b > 0 else fact(a) * fact(c) / fact(a + c + 2)
        if face_no == 2:
            return math.sqrt(3.0) * fact(a) * fact(b) * fact(c) / fact(a + b + c + 2)
        return 0.0 if a > 0 else fact(b) * fact(c) / fact(b + c + 2)

    inverse_t = transposed(inverse)
    mono_mass = [[0.0] * 20 for node_no in range(20)]
    for first_no in range(20):
        for second_no in range(20):
            a = lattice[first_no][0] + lattice[second_no][0]
            b = lattice[first_no][1] + lattice[second_no][1]
            c = lattice[first_no][2] + lattice[second_no][2]
            mono_mass[first_no][second_no] = fact(a) * fact(b) * fact(c) / fact(a + b + c + 3)
    mass_mat = mat_mul(mat_mul(inverse_t, mono_mass), inverse)
    columns = [[] for node_no in range(20)]
    index_list = []
    for face_no in range(4):
        mono_face = [[0.0] * 20 for node_no in range(20)]
        for first_no in range(20):
            for second_no in range(20):
                a = lattice[first_no][0] + lattice[second_no][0]
                b = lattice[first_no][1] + lattice[second_no][1]
                c = lattice[first_no][2] + lattice[second_no][2]
                mono_face[first_no][second_no] = face_integral(face_no, a, b, c)
        face_mass = mat_mul(mat_mul(inverse_t, mono_face), inverse)
        tests = [k == 0 for i, j, k in lattice]
        if face_no == 1:
            tests = [j == 0 for i, j, k in lattice]
        if face_no == 2:
            tests = [i + j + k == 3 for i, j, k in lattice]
        if face_no == 3:
            tests = [i == 0 for i, j, k in lattice]
        chosen = [node_no for node_no in range(20) if tests[node_no]]
        for row_no in range(20):
            columns[row_no].extend([face_mass[row_no][col_no] for col_no in chosen])
        index_list.extend(chosen)
    lift_mat = solve_linear(mass_mat, columns)
    return (deriv_mats, lift_mat, index_list)


def host_tables():
    deriv, lift, faces = reference_element()
    deriv = np.asarray(deriv, np.float32)
    lift = np.asarray(lift, np.float32)
    pick = np.zeros((NODES, FACE), np.float32)
    pick[np.asarray(faces), np.arange(FACE)] = 1.0

    def placed(rows, cols, parts):
        result = np.zeros((rows, cols), np.float32)
        for at, part in parts:
            result[: part.shape[0], at : at + part.shape[1]] = part
        return result

    forward = placed(ROWS, 112, [(0, lift)] + [(40 + 24 * d, deriv[d]) for d in range(3)])
    backward = placed(ROWS, 112, [(0, pick)] + [(40 + 24 * d, deriv[d].T) for d in range(3)])
    lift_t = placed(FACE, ROWS, [(0, lift.T)])
    pick_t = placed(FACE, ROWS, [(0, pick.T)])

    def split(matrix):
        high = matrix.astype(jnp.bfloat16).astype(np.float32)
        low = matrix - high
        return np.concatenate(
            [np.concatenate([high, high], 1), np.concatenate([low, np.zeros_like(low)], 1)], 0
        )

    table = np.zeros((224, 256), np.float32)
    table[0:48, 0:224] = split(forward)
    table[48:96, 0:224] = split(backward)
    table[96:176, 0:48] = split(lift_t)
    table[176:216, 0:48] = np.concatenate([pick_t, pick_t], 1)
    return table.astype(jnp.bfloat16), [int(v) for v in faces]


def stacked(values):
    high = values.astype(bf16).astype(f32)
    return jnp.concatenate([high, values - high], axis=0).astype(bf16)


def parts3(values):
    first = values.astype(bf16)
    rest = values - first.astype(f32)
    second = rest.astype(bf16)
    third = (rest - second.astype(f32)).astype(bf16)
    return first, second, third


def dot(left, right):
    return jnp.dot(left, right, preferred_element_type=f32)


def node_of(rows, faces):
    result = rows - 20
    for row, node in enumerate(faces):
        result = jnp.where(rows == row, node, result)
    return result


def one_hot(condition):
    return jnp.where(condition, 1.0, 0.0).astype(bf16)


def kernel_of(faces):
    def kernel(
        *refs,
    ):
        given, refs = refs[:14], refs[14:]
        out, therm = refs[:2]
        held, in_sem, refs = refs[2:16], refs[16], refs[17:]
        fs, adj, einf, edel, tau, met, fsc, ang, nbr, dexp, sexp, sslot, recv, tab = held
        (
        y, k, w, adj24, acc, nrm, scl, x, xb, p, nb, cd, s_ref, pool, pp, nodes, nodex,
        elems, a_mat, at_mat, ax, axt, b_mat, bx, oids, oh,
        sf, rf, sb, rb, ya, yr, cb, rc,
        fs_sem, fr_sem, bs_sem, br_sem, ps_sem, pr_sem, qs_sem, qr_sem,
        ) = refs

        def fetch(i):
            return pltpu.make_async_copy(given[i], held[i], in_sem.at[i])

        order = (10, 9, 0, 13, 8, 1, 2, 4, 3, 7, 6, 5, 11, 12)
        for i in order:
            fetch(i).start()

        dom = lax.axis_index("dom")
        sub = lax.axis_index("sub")

        rf[...] = jnp.zeros_like(rf)
        rb[...] = jnp.zeros_like(rb)
        yr[...] = jnp.zeros_like(yr)
        rc[...] = jnp.zeros_like(rc)
        barrier = pltpu.get_barrier_semaphore()
        core = lax.rem(dom, 2)
        site = dom // 2
        seat = sub * 2 + core

        def seat_device(other):
            return (site * 2 + lax.rem(other, 2), other // 2)

        def site_device(other):
            return (other * 2 + core, sub)

        def greet(device):
            pl.semaphore_signal(barrier, inc=1, device_id=device, device_id_type=MESH)

        for step in range(1, SEATS):
            greet(seat_device(lax.rem(seat + step, SEATS)))
        for step in range(1, SITES):
            greet(site_device(lax.rem(site + step, SITES)))
        has_low = dom > 0
        has_high = dom < DOMS - 1

        @pl.when(has_low & (core == 0))
        def _():
            greet((dom - 1, sub))

        @pl.when(has_high & (core == 1))
        def _():
            greet((dom + 1, sub))

        def meet():
            outside = (has_low & (core == 0)) | (has_high & (core == 1))
            pl.semaphore_wait(barrier, jnp.where(outside, SEATS + SITES - 1, SEATS + SITES - 2))

        for i in order:
            fetch(i).wait()
        ie = 1.0 / einf[...]
        it = 1.0 / tau[...]
        ed = edel[...]
        pad = jnp.zeros((ROWS - NODES, 256), f32)
        for c in range(9):
            y[0, c] = jnp.concatenate([fs[c], pad], axis=0)
            value = jnp.concatenate([adj[c], pad], axis=0)
            adj24[c] = value
            acc[c] = value
            w[0, c] = (time_step / 6.0) * value
        sin_a = jnp.sin(ang[0])
        normals = (sin_a * jnp.cos(ang[1]), sin_a * jnp.sin(ang[1]), jnp.cos(ang[0]))
        for face in range(4):
            here = slice(10 * face, 10 * face + 10)
            for i in range(3):
                nrm[i, here, :] = jnp.broadcast_to(normals[i][face : face + 1], (10, 256))
            scl[here, :] = jnp.broadcast_to(0.5 * fsc[face : face + 1, :], (10, 256))

        exported = jnp.concatenate([sexp[0], dexp[...], jnp.zeros((2, 128), jnp.int32)], axis=0)
        nodex[...] = node_of(exported >> 8, faces)
        export_el = exported & 255
        export_cols = jnp.transpose(export_el)
        row_iota = lax.broadcasted_iota(jnp.int32, (256, 128), 0)
        lane_iota = lax.broadcasted_iota(jnp.int32, (128, 256), 1)
        for blk in range(BLOCKS):
            here = slice(128 * blk, 128 * blk + 128)
            ax[:, here] = one_hot(row_iota == export_el[blk : blk + 1])
            axt[here, :] = one_hot(lane_iota == export_cols[:, blk : blk + 1])

        def sub_copy(r, src, dst, send, recv_s, to, slot_from):
            return pltpu.make_async_remote_copy(
                src_ref=src.at[r, to],
                dst_ref=dst.at[r, slot_from],
                send_sem=send.at[r, to],
                recv_sem=recv_s.at[r, slot_from],
                device_id=(dom, to),
                device_id_type=MESH,
            )

        def dom_copy(r, src, dst, send, recv_s, block, slot, to):
            return pltpu.make_async_remote_copy(
                src_ref=src.at[r, block],
                dst_ref=dst.at[r, slot],
                send_sem=send.at[r, block],
                recv_sem=recv_s.at[r, slot],
                device_id=(to, sub),
                device_id_type=MESH,
            )

        def start_all(r, src, dst, send, recv_s):
            for step in range(1, SUBS):
                to = lax.rem(sub + step, SUBS)
                sub_copy(r, src, dst, send, recv_s, to, sub).start()

            @pl.when(has_low)
            def _():
                dom_copy(r, src, dst, send, recv_s, 4, 5, dom - 1).start()

            @pl.when(has_high)
            def _():
                dom_copy(r, src, dst, send, recv_s, 5, 4, dom + 1).start()

        def wait_recv_all(r, src, dst, send, recv_s):
            for step in range(1, SUBS):
                other = lax.rem(sub + step, SUBS)
                sub_copy(r, src, dst, send, recv_s, other, other).wait_recv()

            @pl.when(has_low)
            def _():
                dom_copy(r, src, dst, send, recv_s, 4, 4, dom - 1).wait_recv()

            @pl.when(has_high)
            def _():
                dom_copy(r, src, dst, send, recv_s, 5, 5, dom + 1).wait_recv()

        def wait_send_all(r, src, dst, send, recv_s):
            for step in range(1, SUBS):
                to = lax.rem(sub + step, SUBS)
                sub_copy(r, src, dst, send, recv_s, to, sub).wait_send()

            @pl.when(has_low)
            def _():
                dom_copy(r, src, dst, send, recv_s, 4, 5, dom - 1).wait_send()

            @pl.when(has_high)
            def _():
                dom_copy(r, src, dst, send, recv_s, 5, 4, dom + 1).wait_send()

        fwd = (sf, rf, fs_sem, fr_sem)
        bwd = (sb, rb, bs_sem, br_sem)

        node_iota = lax.broadcasted_iota(jnp.int32, (ROWS, 128), 0)
        node_iota2 = lax.broadcasted_iota(jnp.int32, (ROWS, 256), 0)
        own_rows = node_iota2 < NODES

        def fold_pool():
            values = pool[...].reshape(6 * ROWS, 256)
            high = values.astype(bf16)
            pp[0:144, :] = high
            pp[144:288, :] = (values - high.astype(f32)).astype(bf16)

        def exports(r):
            for c in range(6):
                pool[c] = y[r, c]
            fold_pool()
            for pair in range(BLOCKS // 2):
                both = dot(pp[...], ax[:, 256 * pair : 256 * pair + 256])
                both = both[:144] + both[144:]
                for half in range(2):
                    blk = 2 * pair + half
                    got = both[:, 128 * half : 128 * half + 128]
                    keep = node_iota == nodex[blk : blk + 1, :]
                    for c in range(6):
                        sf[r, blk, c : c + 1, :] = jnp.sum(
                            jnp.where(keep, got[24 * c : 24 * c + 24], 0.0), axis=0, keepdims=True
                        )
        def flux_rows(src, at):
            here = slice(at, at + 8)
            n = [nrm[i, here, :] for i in range(3)]
            e = [src[i, here, :] for i in range(3)]
            h = [src[3 + i, here, :] for i in range(3)]
            ne = n[0] * e[0] + n[1] * e[1] + n[2] * e[2]
            nh = n[0] * h[0] + n[1] * h[1] + n[2] * h[2]
            result = []
            for i in range(3):
                j, l = (i + 1) % 3, (i + 2) % 3
                result.append(n[i] * ne - e[i] - (n[j] * h[l] - n[l] * h[j]))
            for i in range(3):
                j, l = (i + 1) % 3, (i + 2) % 3
                result.append((n[j] * e[l] - n[l] * e[j]) + n[i] * nh - h[i])
            return result

        def curl_rows(x, e, h):
            for d in range(3):
                m = [met[3 * d + i : 3 * d + i + 1, :] for i in range(3)]
                here = slice(40 + 24 * d, 64 + 24 * d)
                for i in range(3):
                    j, l = (i + 1) % 3, (i + 2) % 3
                    x[i, here, :] = m[j] * h[l] - m[l] * h[j]
                    x[3 + i, here, :] = m[l] * e[j] - m[j] * e[l]

        def contracted(x, first, c):
            got = dot(tab[first : first + 48, 0:224], stacked(x[c]))
            return got[:24] + got[24:]

        def back_flux(r):
            for c in range(6):
                value = w[r, c]
                if c < 3:
                    value = value * ie
                got = dot(tab[96:176, 0:48], stacked(value))
                p[c] = (got[:40] + got[40:]) * scl[...]
            for at in range(0, FACE, 8):
                for c, value in enumerate(flux_rows(p, at)):
                    cd[c, at : at + 8, :] = value

        def sweep(gather, scatter):
            def group(g, carry):
                for j in range(GROUP):
                    fn = g * GROUP + j
                    keep = node_iota2 == nodes[pl.ds(fn, 1), :]
                    if gather:
                        got = dot(pp[...], a_mat[fn])
                        got = got[:144] + got[144:]
                        for c in range(6):
                            nb[c, pl.ds(fn, 1), :] = jnp.sum(
                                jnp.where(keep, got[24 * c : 24 * c + 24], 0.0),
                                axis=0,
                                keepdims=True,
                            )
                    if scatter:
                        high, low = [], []
                        for c in range(6):
                            value = cd[c, pl.ds(fn, 1), :]
                            top = value.astype(bf16).astype(f32)
                            high.append(jnp.where(keep, top, 0.0))
                            low.append(jnp.where(keep, value - top, 0.0))
                        b_mat[:, 256 * j : 256 * j + 256] = jnp.concatenate(high + low, 0).astype(
                            bf16
                        )
                if scatter:
                    span = GROUP * 256
                    got = dot(b_mat[...], at_mat[pl.ds(pl.multiple_of(g * span, span), span), :])
                    s_ref[...] = s_ref[...] - (got[:144] + got[144:])
                return carry

            if scatter:
                s_ref[...] = jnp.zeros_like(s_ref)
            lax.fori_loop(0, FACE // GROUP, group, 0)

        def give_back(r):
            for c in range(6):
                rows = s_ref[24 * c + 20 : 24 * c + 24, :]
                for blk in range(4):
                    at = 128 * (blk % 2)
                    sb[r, blk, c : c + 1, :] = rows[blk // 2 : blk // 2 + 1, at : at + 128]
                sb[r, 4, c : c + 1, :] = rows[2:3, 0:128]
                sb[r, 5, c : c + 1, :] = rows[3:4, 128:256]

        def arrived(r, blk, dst, src):
            value = dst[r, blk]
            if blk < SUBS:
                value = jnp.where(sub == blk, src[r, blk], value)
            return value

        def receive(r):
            wait_recv_all(r, *fwd)
            for blk in range(4):
                value = arrived(r, blk, rf, sf)
                at = 128 * (blk % 2)
                for c in range(6):
                    row = 20 + blk // 2
                    pool[c, row : row + 1, at : at + 128] = value[c : c + 1]
            low, high = rf[r, 4], rf[r, 5]
            for c in range(6):
                pool[c, 22:23, 0:128] = low[c : c + 1]
                pool[c, 23:24, 128:256] = high[c : c + 1]
            fold_pool()

        def forward(r, whole=True):
            for c in range(6):
                p[c] = dot(tab[176:216, 0:48], stacked(y[r, c])) - nb[c]
            for at in range(0, FACE, 8):
                factor = scl[at : at + 8, :]
                for c, value in enumerate(flux_rows(p, at)):
                    x[c, at : at + 8, :] = value * factor
            curl_rows(x, [y[r, c] for c in range(3)], [y[r, 3 + c] for c in range(3)])
            for c in range(3):
                current = (ed * y[r, c] - y[r, 6 + c]) * it
                k[r, 6 + c] = current
                k[r, c] = (contracted(x, 0, c) - current) * ie
                if whole:
                    k[r, 3 + c] = contracted(x, 0, 3 + c)

        def back_volume(r):
            for c in range(6):
                xb[c, 0:40, :] = cd[c]
            curl_rows(xb, [w[r, c] * ie for c in range(3)], [w[r, 3 + c] for c in range(3)])
            cots = [contracted(xb, 48, c) for c in range(6)]
            wait_recv_all(r, *bwd)
            for blk in range(BLOCKS):
                value = arrived(r, blk, rb, sb)
                keep = node_iota == nodex[blk : blk + 1, :]
                top = value.astype(bf16).astype(f32)
                rest = value - top
                high = [jnp.where(keep, top[c : c + 1], 0.0) for c in range(6)]
                low = [jnp.where(keep, rest[c : c + 1], 0.0) for c in range(6)]
                bx[:, 128 * blk : 128 * blk + 128] = jnp.concatenate(high + low, 0).astype(bf16)
            got = dot(bx[...], axt[...])
            s_ref[...] = s_ref[...] + (got[:144] + got[144:])
            for c in range(6):
                value = cots[c] + s_ref[24 * c : 24 * c + 24, :]
                cots[c] = jnp.where(own_rows, value, 0.0)
            for c in range(3):
                through = (w[r, 6 + c] - w[r, c] * ie) * it
                cots[c] = cots[c] + ed * through
                cots.append(-through)
            return cots

        index = nbr[...]
        nodes[...] = node_of(index >> 8, faces)
        element = index & 255
        elems[...] = element
        lane_iota2 = lax.broadcasted_iota(jnp.int32, (256, 256), 1)
        row_iota2 = lax.broadcasted_iota(jnp.int32, (256, 256), 0)

        def build(g, carry):
            rows = elems[pl.ds(pl.multiple_of(g * 8, 8), 8), :]
            columns = jnp.transpose(rows)
            for j in range(8):
                a_mat[g * 8 + j] = one_hot(row_iota2 == rows[j : j + 1])
                at = pl.multiple_of(g * 2048 + 256 * j, 256)
                at_mat[pl.ds(at, 256), :] = one_hot(lane_iota2 == columns[:, j : j + 1])
            return carry

        lax.fori_loop(0, FACE // 8, build, 0)
        owners = jnp.transpose(jnp.concatenate([recv[0], jnp.zeros((6, 128), jnp.int32)], axis=0))
        oids[...] = owners
        lanes = lax.broadcasted_iota(jnp.int32, (SITES, 128), 1)
        for q in range(SEATS):
            ids = oids[pl.ds((q % 2) * SUBS + q // 2, SITES, stride=SEATS), :]
            for z in range(2):
                at = 128 * (2 * q + z)
                oh[:, at : at + 128] = one_hot(lanes == ids[:, z : z + 1])

        def first_hop(to, slot_from):
            return pltpu.make_async_remote_copy(
                src_ref=ya.at[to],
                dst_ref=yr.at[slot_from],
                send_sem=ps_sem.at[to],
                recv_sem=pr_sem.at[slot_from],
                device_id=seat_device(to),
                device_id_type=MESH,
            )

        def second_hop(to, slot_from):
            return pltpu.make_async_remote_copy(
                src_ref=cb.at[to],
                dst_ref=rc.at[slot_from],
                send_sem=qs_sem.at[to],
                recv_sem=qr_sem.at[slot_from],
                device_id=site_device(to),
                device_id_type=MESH,
            )

        seats = [lax.rem(seat + step, SEATS) for step in range(1, SEATS)]
        sites = [lax.rem(site + step, SITES) for step in range(1, SITES)]
        exports(0)
        meet()
        start_all(0, *fwd)

        def one_round(r, carry):
            back_flux(r)
            sweep(False, True)
            give_back(r)
            start_all(r, *bwd)
            receive(r)
            sweep(True, False)
            forward(r)

            @pl.when(r < 3)
            def _():
                ahead = jnp.where(r == 2, time_step, 0.5 * time_step)
                for c in range(9):
                    y[r + 1, c] = y[0, c] + ahead * k[r, c]
                exports(r + 1)
                start_all(r + 1, *fwd)

            @pl.when(r == 3)
            def _():
                sums = [jnp.zeros((ROWS, 256), f32) for _ in range(3)]
                for q in range(4):
                    for c in range(3):
                        through = w[3 - q, 6 + c] - w[3 - q, c] * ie
                        sums[0] = sums[0] - w[3 - q, c] * k[q, c]
                        sums[1] = sums[1] + through * y[q, c]
                        sums[2] = sums[2] - through * k[q, 6 + c]
                grads = [
                    jnp.sum(value, axis=0, keepdims=True) * factor
                    for value, factor in zip(sums, (ie, it, it))
                ]
                slot = sslot[...]
                place = slot >> 1
                target = ((place & 3) * 2 + ((place >> 2) & 1)) * SITES + (place >> 3)
                chosen = one_hot(lax.broadcasted_iota(jnp.int32, (128, 256), 0) == target)
                lines = [jnp.where((slot & 1) == q, g, 0.0) for q in range(2) for g in grads]
                lines = jnp.concatenate(lines + [jnp.zeros((2, 256), f32)], axis=0)
                lines = [jnp.where(seat == q, lines, 0.0) for q in range(SEATS)]
                lines = jnp.concatenate(lines + [jnp.zeros((64, 256), f32)], axis=0)
                packed = sum(dot(chosen, part) for part in parts3(jnp.transpose(lines)))
                for q in range(SEATS):
                    ya[q] = packed[SITES * q : SITES * q + SITES]

                for other in seats:
                    first_hop(other, seat).start()

            adj_part = jnp.where(r == 2, time_step / 6.0, time_step / 3.0)
            back_part = jnp.where(r == 0, time_step, 0.5 * time_step)
            back = back_volume(r)
            for c in range(9):
                acc[c] = acc[c] + back[c]

            @pl.when(r < 3)
            def _():
                for c in range(9):
                    w[r + 1, c] = adj_part * adj24[c] + back_part * back[c]

            return carry

        lax.fori_loop(0, 4, one_round, 0)

        for other in seats:
            first_hop(other, other).wait_recv()
        mine = ya[pl.ds(seat, 1)][0]
        for q in range(SEATS):
            mine = mine + yr[q]
        for q in range(SITES):
            cb[q] = mine[q : q + 1]
        for other in sites:
            second_hop(other, site).start()
        for c in range(9):
            out[c] = acc[c][:NODES]

        for other in sites:
            second_hop(other, other).wait_recv()
        here = lax.broadcasted_iota(jnp.int32, (SITES, 128), 0) == site
        came = jnp.concatenate([rc[q] for q in range(SITES)], axis=0)
        came = came + jnp.where(here, mine, 0.0)
        turned = jnp.concatenate(parts3(jnp.transpose(came)[:64]), axis=0)
        spread = dot(turned, oh[...])
        spread = spread[:64] + spread[64:128] + spread[128:]
        total = jnp.zeros((3, 128), f32)
        for q in range(SEATS):
            for z in range(2):
                row, at = 8 * q + 3 * z, 128 * (2 * q + z)
                total = total + spread[row : row + 3, at : at + 128]
        therm[...] = total[:, :64]

        def all_sent(r, carry):
            wait_send_all(r, *fwd)
            wait_send_all(r, *bwd)
            return carry

        lax.fori_loop(0, 4, all_sent, 0)
        for other in seats:
            first_hop(other, seat).wait_send()
        for other in sites:
            second_hop(other, site).wait_send()

    return kernel


def per_device(
    field_state,
    adjoint,
    eps_inf,
    eps_delta,
    relax_time,
    metric,
    face_scale,
    face_angles,
    nbr_index,
    dom_export,
    sub_export,
    send_slot,
    recv_index,
):
    table, faces = host_tables()
    stage = pltpu.VMEM((4, 9, ROWS, 256), f32)
    trace = pltpu.VMEM((6, FACE, 256), f32)
    message = pltpu.VMEM((4, BLOCKS, 8, 128), f32)
    semaphores = pltpu.SemaphoreType.DMA((4, BLOCKS))
    state = pltpu.VMEM((9, ROWS, 256), f32)
    values = (
        field_state,
        adjoint,
        eps_inf.reshape(1, 256),
        eps_delta.reshape(1, 256),
        relax_time.reshape(1, 256),
        metric,
        face_scale,
        face_angles,
        nbr_index,
        dom_export.reshape(2, 128),
        sub_export,
        send_slot.reshape(1, 256),
        jnp.transpose(recv_index, (0, 2, 1)),
        jnp.asarray(table),
    )
    scratch = [pltpu.VMEM(value.shape, value.dtype) for value in values] + [
        pltpu.SemaphoreType.DMA((len(values),)),
        stage, stage, stage, state, state,
        pltpu.VMEM((3, FACE, 256), f32),
        pltpu.VMEM((FACE, 256), f32),
        pltpu.VMEM((6, 112, 256), f32),
        pltpu.VMEM((6, 112, 256), f32),
        trace, trace, trace,
        pltpu.VMEM((6 * ROWS, 256), f32),
        pltpu.VMEM((6, ROWS, 256), f32),
        pltpu.VMEM((12 * ROWS, 256), bf16),
        pltpu.VMEM((FACE, 256), jnp.int32),
        pltpu.VMEM((8, 128), jnp.int32),
        pltpu.VMEM((FACE, 256), jnp.int32),
        pltpu.VMEM((FACE, 256, 256), bf16),
        pltpu.VMEM((FACE * 256, 256), bf16),
        pltpu.VMEM((256, 128 * BLOCKS), bf16),
        pltpu.VMEM((128 * BLOCKS, 256), bf16),
        pltpu.VMEM((12 * ROWS, 256 * GROUP), bf16),
        pltpu.VMEM((12 * ROWS, 128 * BLOCKS), bf16),
        pltpu.VMEM((128, 8), jnp.int32),
        pltpu.VMEM((SITES, 128 * 2 * SEATS), bf16),
        message, message, message, message,
        pltpu.VMEM((SEATS, SITES, 128), f32),
        pltpu.VMEM((SEATS, SITES, 128), f32),
        pltpu.VMEM((SITES, 1, 128), f32),
        pltpu.VMEM((SITES, 1, 128), f32),
        semaphores, semaphores, semaphores, semaphores,
        pltpu.SemaphoreType.DMA((SEATS,)),
        pltpu.SemaphoreType.DMA((SEATS,)),
        pltpu.SemaphoreType.DMA((SITES,)),
        pltpu.SemaphoreType.DMA((SITES,)),
    ]
    call = pl.pallas_call(
        kernel_of(faces),
        out_shape=(
            jax.ShapeDtypeStruct((9, NODES, 256), f32),
            jax.ShapeDtypeStruct((3, 64), f32),
        ),
        in_specs=[pl.BlockSpec(memory_space=pltpu.HBM)] * 14,
        out_specs=(
            pl.BlockSpec(memory_space=pltpu.VMEM),
            pl.BlockSpec(memory_space=pltpu.VMEM),
        ),
        scratch_shapes=scratch,
        compiler_params=pltpu.CompilerParams(
            collective_id=0, has_side_effects=True, vmem_limit_bytes=32 << 20
        ),
        name="reverse_step",
    )
    return call(*[pltpu.with_memory_space_constraint(v, pltpu.HBM) for v in values])


def solution(mesh):
    both = ("dom", "sub")
    return jax.shard_map(
        per_device,
        mesh=mesh,
        in_specs=(
            P(None, None, both),
            P(None, None, both),
            P(both),
            P(both),
            P(both),
            P(None, both),
            P(None, both),
            P(None, None, both),
            P(None, both),
            P(both),
            P(both, None, None),
            P(both),
            P(both, None, None),
        ),
        out_specs=(P(None, None, both), P(None, both)),
        check_vma=False,
    )
```

```python
import math

import jax
import jax.numpy as jnp
import numpy as np
from jax import lax
from jax.experimental import pallas as pl
from jax.experimental.pallas import tpu as pltpu
from jax.sharding import PartitionSpec as P

time_step = 0.014
f32 = jnp.float32
bf16 = jnp.bfloat16
NODES = 20
ROWS = 24
FACE = 40
DOMS = 32
SUBS = 4
BLOCKS = 6
SEATS = 8
SITES = 16
GROUP = 20
MESH = pl.DeviceIdType.MESH


def mat_mul(left, right):
    inner = len(right)
    return [
        [
            sum((left[row_no][k] * right[k][col_no] for k in range(inner)))
            for col_no in range(len(right[0]))
        ]
        for row_no in range(len(left))
    ]


def transposed(matrix):
    return [list(column) for column in zip(*matrix)]


def solve_linear(matrix, rhs_rows):
    order = len(matrix)
    work = [list(matrix[row_no]) + list(rhs_rows[row_no]) for row_no in range(order)]
    for col_no in range(order):

        def magnitude(row_no):
            return abs(work[row_no][col_no])

        pivot = max(range(col_no, order), key=magnitude)
        work[col_no], work[pivot] = (work[pivot], work[col_no])
        head = work[col_no][col_no]
        work[col_no] = [value / head for value in work[col_no]]
        for row_no in range(order):
            if row_no != col_no:
                factor = work[row_no][col_no]
                work[row_no] = [
                    value - factor * other for value, other in zip(work[row_no], work[col_no])
                ]
    return [row[order:] for row in work]


def reference_element():
    lattice = [(i, j, k) for k in range(4) for j in range(4 - k) for i in range(4 - j - k)]
    points = [[float(v) / 3.0 for v in node] for node in lattice]
    vander = [[0.0] * 20 for node_no in range(20)]
    slopes = [[[0.0] * 20 for node_no in range(20)] for axis_no in range(3)]
    for node_no in range(20):
        for mono_no in range(20):
            power = lattice[mono_no]
            value = 1.0
            for axis_no in range(3):
                value *= points[node_no][axis_no] ** power[axis_no]
            vander[node_no][mono_no] = value
            for axis_no in range(3):
                if power[axis_no] > 0:
                    term = float(power[axis_no])
                    for other_no in range(3):
                        expo_val = power[other_no] - (1 if other_no == axis_no else 0)
                        term *= points[node_no][other_no] ** expo_val
                    slopes[axis_no][node_no][mono_no] = term
    identity = [[1.0 if row_no == col_no else 0.0 for col_no in range(20)] for row_no in range(20)]
    inverse = solve_linear(vander, identity)
    deriv_mats = [mat_mul(slopes[axis_no], inverse) for axis_no in range(3)]
    fact = math.factorial

    def face_integral(face_no, a, b, c):
        if face_no == 0:
            return 0.0 if c > 0 else fact(a) * fact(b) / fact(a + b + 2)
        if face_no == 1:
            return 0.0 if b > 0 else fact(a) * fact(c) / fact(a + c + 2)
        if face_no == 2:
            return math.sqrt(3.0) * fact(a) * fact(b) * fact(c) / fact(a + b + c + 2)
        return 0.0 if a > 0 else fact(b) * fact(c) / fact(b + c + 2)

    inverse_t = transposed(inverse)
    mono_mass = [[0.0] * 20 for node_no in range(20)]
    for first_no in range(20):
        for second_no in range(20):
            a = lattice[first_no][0] + lattice[second_no][0]
            b = lattice[first_no][1] + lattice[second_no][1]
            c = lattice[first_no][2] + lattice[second_no][2]
            mono_mass[first_no][second_no] = fact(a) * fact(b) * fact(c) / fact(a + b + c + 3)
    mass_mat = mat_mul(mat_mul(inverse_t, mono_mass), inverse)
    columns = [[] for node_no in range(20)]
    index_list = []
    for face_no in range(4):
        mono_face = [[0.0] * 20 for node_no in range(20)]
        for first_no in range(20):
            for second_no in range(20):
                a = lattice[first_no][0] + lattice[second_no][0]
                b = lattice[first_no][1] + lattice[second_no][1]
                c = lattice[first_no][2] + lattice[second_no][2]
                mono_face[first_no][second_no] = face_integral(face_no, a, b, c)
        face_mass = mat_mul(mat_mul(inverse_t, mono_face), inverse)
        tests = [k == 0 for i, j, k in lattice]
        if face_no == 1:
            tests = [j == 0 for i, j, k in lattice]
        if face_no == 2:
            tests = [i + j + k == 3 for i, j, k in lattice]
        if face_no == 3:
            tests = [i == 0 for i, j, k in lattice]
        chosen = [node_no for node_no in range(20) if tests[node_no]]
        for row_no in range(20):
            columns[row_no].extend([face_mass[row_no][col_no] for col_no in chosen])
        index_list.extend(chosen)
    lift_mat = solve_linear(mass_mat, columns)
    return (deriv_mats, lift_mat, index_list)


def host_tables():
    deriv, lift, faces = reference_element()
    deriv = np.asarray(deriv, np.float32)
    lift = np.asarray(lift, np.float32)
    pick = np.zeros((NODES, FACE), np.float32)
    pick[np.asarray(faces), np.arange(FACE)] = 1.0

    def placed(rows, cols, parts):
        result = np.zeros((rows, cols), np.float32)
        for at, part in parts:
            result[: part.shape[0], at : at + part.shape[1]] = part
        return result

    forward = placed(ROWS, 112, [(0, lift)] + [(40 + 24 * d, deriv[d]) for d in range(3)])
    backward = placed(ROWS, 112, [(0, pick)] + [(40 + 24 * d, deriv[d].T) for d in range(3)])
    lift_t = placed(FACE, ROWS, [(0, lift.T)])
    pick_t = placed(FACE, ROWS, [(0, pick.T)])

    def split(matrix):
        high = matrix.astype(jnp.bfloat16).astype(np.float32)
        low = matrix - high
        return np.concatenate(
            [np.concatenate([high, high], 1), np.concatenate([low, np.zeros_like(low)], 1)], 0
        )

    table = np.zeros((224, 256), np.float32)
    table[0:48, 0:224] = split(forward)
    table[48:96, 0:224] = split(backward)
    table[96:176, 0:48] = split(lift_t)
    table[176:216, 0:48] = np.concatenate([pick_t, pick_t], 1)
    return table.astype(jnp.bfloat16), [int(v) for v in faces]


def stacked(values):
    high = values.astype(bf16).astype(f32)
    return jnp.concatenate([high, values - high], axis=0).astype(bf16)


def parts3(values):
    first = values.astype(bf16)
    rest = values - first.astype(f32)
    second = rest.astype(bf16)
    third = (rest - second.astype(f32)).astype(bf16)
    return first, second, third


def dot(left, right):
    return jnp.dot(left, right, preferred_element_type=f32)


def node_of(rows, faces):
    result = rows - 20
    for row, node in enumerate(faces):
        result = jnp.where(rows == row, node, result)
    return result


def one_hot(condition):
    return jnp.where(condition, 1.0, 0.0).astype(bf16)


def kernel_of(faces):
    def kernel(
        *refs,
    ):
        given, refs = refs[:14], refs[14:]
        out, therm = refs[:2]
        held, in_sem, refs = refs[2:16], refs[16], refs[17:]
        fs, adj, einf, edel, tau, met, fsc, ang, nbr, dexp, sexp, sslot, recv, tab = held
        (
        y, k, w, adj24, acc, nrm, scl, x, xb, p, nb, cd, s_ref, pool, pp, nodes, nodex,
        elems, a_mat, at_mat, ax, axt, b_mat, bx, oids, oh,
        sf, rf, sb, rb, ya, yr, cb, rc,
        fs_sem, fr_sem, bs_sem, br_sem, ps_sem, pr_sem, qs_sem, qr_sem,
        ) = refs

        def fetch(i):
            return pltpu.make_async_copy(given[i], held[i], in_sem.at[i])

        order = (10, 9, 0, 13, 8, 1, 2, 4, 3, 7, 6, 5, 11, 12)
        for i in order:
            fetch(i).start()

        dom = lax.axis_index("dom")
        sub = lax.axis_index("sub")

        rf[...] = jnp.zeros_like(rf)
        rb[...] = jnp.zeros_like(rb)
        yr[...] = jnp.zeros_like(yr)
        rc[...] = jnp.zeros_like(rc)
        barrier = pltpu.get_barrier_semaphore()
        core = lax.rem(dom, 2)
        site = dom // 2
        seat = sub * 2 + core

        def seat_device(other):
            return (site * 2 + lax.rem(other, 2), other // 2)

        def site_device(other):
            return (other * 2 + core, sub)

        def greet(device):
            pl.semaphore_signal(barrier, inc=1, device_id=device, device_id_type=MESH)

        for step in range(1, SEATS):
            greet(seat_device(lax.rem(seat + step, SEATS)))
        for step in range(1, SITES):
            greet(site_device(lax.rem(site + step, SITES)))
        has_low = dom > 0
        has_high = dom < DOMS - 1

        @pl.when(has_low & (core == 0))
        def _():
            greet((dom - 1, sub))

        @pl.when(has_high & (core == 1))
        def _():
            greet((dom + 1, sub))

        def meet():
            outside = (has_low & (core == 0)) | (has_high & (core == 1))
            pl.semaphore_wait(barrier, jnp.where(outside, SEATS + SITES - 1, SEATS + SITES - 2))

        for i in order:
            fetch(i).wait()
        ie = 1.0 / einf[...]
        it = 1.0 / tau[...]
        ed = edel[...]
        pad = jnp.zeros((ROWS - NODES, 256), f32)
        for c in range(9):
            y[0, c] = jnp.concatenate([fs[c], pad], axis=0)
            value = jnp.concatenate([adj[c], pad], axis=0)
            adj24[c] = value
            acc[c] = value
            w[0, c] = (time_step / 6.0) * value
        sin_a = jnp.sin(ang[0])
        normals = (sin_a * jnp.cos(ang[1]), sin_a * jnp.sin(ang[1]), jnp.cos(ang[0]))
        for face in range(4):
            here = slice(10 * face, 10 * face + 10)
            for i in range(3):
                nrm[i, here, :] = jnp.broadcast_to(normals[i][face : face + 1], (10, 256))
            scl[here, :] = jnp.broadcast_to(0.5 * fsc[face : face + 1, :], (10, 256))

        exported = jnp.concatenate([sexp[0], dexp[...], jnp.zeros((2, 128), jnp.int32)], axis=0)
        nodex[...] = node_of(exported >> 8, faces)
        export_el = exported & 255
        export_cols = jnp.transpose(export_el)
        row_iota = lax.broadcasted_iota(jnp.int32, (256, 128), 0)
        lane_iota = lax.broadcasted_iota(jnp.int32, (128, 256), 1)
        for blk in range(BLOCKS):
            here = slice(128 * blk, 128 * blk + 128)
            ax[:, here] = one_hot(row_iota == export_el[blk : blk + 1])
            axt[here, :] = one_hot(lane_iota == export_cols[:, blk : blk + 1])

        def sub_copy(r, src, dst, send, recv_s, to, slot_from):
            return pltpu.make_async_remote_copy(
                src_ref=src.at[r, to],
                dst_ref=dst.at[r, slot_from],
                send_sem=send.at[r, to],
                recv_sem=recv_s.at[r, slot_from],
                device_id=(dom, to),
                device_id_type=MESH,
            )

        def dom_copy(r, src, dst, send, recv_s, block, slot, to):
            return pltpu.make_async_remote_copy(
                src_ref=src.at[r, block],
                dst_ref=dst.at[r, slot],
                send_sem=send.at[r, block],
                recv_sem=recv_s.at[r, slot],
                device_id=(to, sub),
                device_id_type=MESH,
            )

        def start_all(r, src, dst, send, recv_s):
            for step in range(1, SUBS):
                to = lax.rem(sub + step, SUBS)
                sub_copy(r, src, dst, send, recv_s, to, sub).start()

            @pl.when(has_low)
            def _():
                dom_copy(r, src, dst, send, recv_s, 4, 5, dom - 1).start()

            @pl.when(has_high)
            def _():
                dom_copy(r, src, dst, send, recv_s, 5, 4, dom + 1).start()

        def wait_recv_all(r, src, dst, send, recv_s):
            for step in range(1, SUBS):
                other = lax.rem(sub + step, SUBS)
                sub_copy(r, src, dst, send, recv_s, other, other).wait_recv()

            @pl.when(has_low)
            def _():
                dom_copy(r, src, dst, send, recv_s, 4, 4, dom - 1).wait_recv()

            @pl.when(has_high)
            def _():
                dom_copy(r, src, dst, send, recv_s, 5, 5, dom + 1).wait_recv()

        def wait_send_all(r, src, dst, send, recv_s):
            for step in range(1, SUBS):
                to = lax.rem(sub + step, SUBS)
                sub_copy(r, src, dst, send, recv_s, to, sub).wait_send()

            @pl.when(has_low)
            def _():
                dom_copy(r, src, dst, send, recv_s, 4, 5, dom - 1).wait_send()

            @pl.when(has_high)
            def _():
                dom_copy(r, src, dst, send, recv_s, 5, 4, dom + 1).wait_send()

        fwd = (sf, rf, fs_sem, fr_sem)
        bwd = (sb, rb, bs_sem, br_sem)

        node_iota = lax.broadcasted_iota(jnp.int32, (ROWS, 128), 0)
        node_iota2 = lax.broadcasted_iota(jnp.int32, (ROWS, 256), 0)
        own_rows = node_iota2 < NODES

        def fold_pool():
            values = pool[...].reshape(6 * ROWS, 256)
            high = values.astype(bf16)
            pp[0:144, :] = high
            pp[144:288, :] = (values - high.astype(f32)).astype(bf16)

        def exports(r):
            for c in range(6):
                pool[c] = y[r, c]
            fold_pool()
            for pair in range(BLOCKS // 2):
                both = dot(pp[...], ax[:, 256 * pair : 256 * pair + 256])
                both = both[:144] + both[144:]
                for half in range(2):
                    blk = 2 * pair + half
                    got = both[:, 128 * half : 128 * half + 128]
                    keep = node_iota == nodex[blk : blk + 1, :]
                    for c in range(6):
                        sf[r, blk, c : c + 1, :] = jnp.sum(
                            jnp.where(keep, got[24 * c : 24 * c + 24], 0.0), axis=0, keepdims=True
                        )
        def flux_rows(src, at):
            here = slice(at, at + 8)
            n = [nrm[i, here, :] for i in range(3)]
            e = [src[i, here, :] for i in range(3)]
            h = [src[3 + i, here, :] for i in range(3)]
            ne = n[0] * e[0] + n[1] * e[1] + n[2] * e[2]
            nh = n[0] * h[0] + n[1] * h[1] + n[2] * h[2]
            result = []
            for i in range(3):
                j, l = (i + 1) % 3, (i + 2) % 3
                result.append(n[i] * ne - e[i] - (n[j] * h[l] - n[l] * h[j]))
            for i in range(3):
                j, l = (i + 1) % 3, (i + 2) % 3
                result.append((n[j] * e[l] - n[l] * e[j]) + n[i] * nh - h[i])
            return result

        def curl_rows(x, e, h):
            for d in range(3):
                m = [met[3 * d + i : 3 * d + i + 1, :] for i in range(3)]
                here = slice(40 + 24 * d, 64 + 24 * d)
                for i in range(3):
                    j, l = (i + 1) % 3, (i + 2) % 3
                    x[i, here, :] = m[j] * h[l] - m[l] * h[j]
                    x[3 + i, here, :] = m[l] * e[j] - m[j] * e[l]

        def contracted(x, first, c):
            got = dot(tab[first : first + 48, 0:224], stacked(x[c]))
            return got[:24] + got[24:]

        def back_flux(r):
            for c in range(6):
                value = w[r, c]
                if c < 3:
                    value = value * ie
                got = dot(tab[96:176, 0:48], stacked(value))
                p[c] = (got[:40] + got[40:]) * scl[...]
            for at in range(0, FACE, 8):
                for c, value in enumerate(flux_rows(p, at)):
                    cd[c, at : at + 8, :] = value

        def sweep(gather, scatter):
            def group(g, carry):
                for j in range(GROUP):
                    fn = g * GROUP + j
                    keep = node_iota2 == nodes[pl.ds(fn, 1), :]
                    if gather:
                        got = dot(pp[...], a_mat[fn])
                        got = got[:144] + got[144:]
                        for c in range(6):
                            nb[c, pl.ds(fn, 1), :] = jnp.sum(
                                jnp.where(keep, got[24 * c : 24 * c + 24], 0.0),
                                axis=0,
                                keepdims=True,
                            )
                    if scatter:
                        high, low = [], []
                        for c in range(6):
                            value = cd[c, pl.ds(fn, 1), :]
                            top = value.astype(bf16).astype(f32)
                            high.append(jnp.where(keep, top, 0.0))
                            low.append(jnp.where(keep, value - top, 0.0))
                        b_mat[:, 256 * j : 256 * j + 256] = jnp.concatenate(high + low, 0).astype(
                            bf16
                        )
                if scatter:
                    span = GROUP * 256
                    got = dot(b_mat[...], at_mat[pl.ds(pl.multiple_of(g * span, span), span), :])
                    s_ref[...] = s_ref[...] - (got[:144] + got[144:])
                return carry

            if scatter:
                s_ref[...] = jnp.zeros_like(s_ref)
            lax.fori_loop(0, FACE // GROUP, group, 0)

        def give_back(r):
            for c in range(6):
                rows = s_ref[24 * c + 20 : 24 * c + 24, :]
                for blk in range(4):
                    at = 128 * (blk % 2)
                    sb[r, blk, c : c + 1, :] = rows[blk // 2 : blk // 2 + 1, at : at + 128]
                sb[r, 4, c : c + 1, :] = rows[2:3, 0:128]
                sb[r, 5, c : c + 1, :] = rows[3:4, 128:256]

        def arrived(r, blk, dst, src):
            value = dst[r, blk]
            if blk < SUBS:
                value = jnp.where(sub == blk, src[r, blk], value)
            return value

        def receive(r):
            wait_recv_all(r, *fwd)
            for blk in range(4):
                value = arrived(r, blk, rf, sf)
                at = 128 * (blk % 2)
                for c in range(6):
                    row = 20 + blk // 2
                    pool[c, row : row + 1, at : at + 128] = value[c : c + 1]
            low, high = rf[r, 4], rf[r, 5]
            for c in range(6):
                pool[c, 22:23, 0:128] = low[c : c + 1]
                pool[c, 23:24, 128:256] = high[c : c + 1]
            fold_pool()

        def forward(r, whole=True):
            for c in range(6):
                p[c] = dot(tab[176:216, 0:48], stacked(y[r, c])) - nb[c]
            for at in range(0, FACE, 8):
                factor = scl[at : at + 8, :]
                for c, value in enumerate(flux_rows(p, at)):
                    x[c, at : at + 8, :] = value * factor
            curl_rows(x, [y[r, c] for c in range(3)], [y[r, 3 + c] for c in range(3)])
            for c in range(3):
                current = (ed * y[r, c] - y[r, 6 + c]) * it
                k[r, 6 + c] = current
                k[r, c] = (contracted(x, 0, c) - current) * ie
                if whole:
                    k[r, 3 + c] = contracted(x, 0, 3 + c)

        def back_volume(r):
            for c in range(6):
                xb[c, 0:40, :] = cd[c]
            curl_rows(xb, [w[r, c] * ie for c in range(3)], [w[r, 3 + c] for c in range(3)])
            cots = [contracted(xb, 48, c) for c in range(6)]
            wait_recv_all(r, *bwd)
            for blk in range(BLOCKS):
                value = arrived(r, blk, rb, sb)
                keep = node_iota == nodex[blk : blk + 1, :]
                top = value.astype(bf16).astype(f32)
                rest = value - top
                high = [jnp.where(keep, top[c : c + 1], 0.0) for c in range(6)]
                low = [jnp.where(keep, rest[c : c + 1], 0.0) for c in range(6)]
                bx[:, 128 * blk : 128 * blk + 128] = jnp.concatenate(high + low, 0).astype(bf16)
            got = dot(bx[...], axt[...])
            s_ref[...] = s_ref[...] + (got[:144] + got[144:])
            for c in range(6):
                value = cots[c] + s_ref[24 * c : 24 * c + 24, :]
                cots[c] = jnp.where(own_rows, value, 0.0)
            for c in range(3):
                through = (w[r, 6 + c] - w[r, c] * ie) * it
                cots[c] = cots[c] + ed * through
                cots.append(-through)
            return cots

        index = nbr[...]
        nodes[...] = node_of(index >> 8, faces)
        element = index & 255
        elems[...] = element
        lane_iota2 = lax.broadcasted_iota(jnp.int32, (256, 256), 1)
        row_iota2 = lax.broadcasted_iota(jnp.int32, (256, 256), 0)

        def build(g, carry):
            rows = elems[pl.ds(pl.multiple_of(g * 8, 8), 8), :]
            columns = jnp.transpose(rows)
            for j in range(8):
                a_mat[g * 8 + j] = one_hot(row_iota2 == rows[j : j + 1])
                at = pl.multiple_of(g * 2048 + 256 * j, 256)
                at_mat[pl.ds(at, 256), :] = one_hot(lane_iota2 == columns[:, j : j + 1])
            return carry

        lax.fori_loop(0, FACE // 8, build, 0)
        owners = jnp.transpose(jnp.concatenate([recv[0], jnp.zeros((6, 128), jnp.int32)], axis=0))
        oids[...] = owners
        lanes = lax.broadcasted_iota(jnp.int32, (SITES, 128), 1)
        for q in range(SEATS):
            ids = oids[pl.ds((q % 2) * SUBS + q // 2, SITES, stride=SEATS), :]
            for z in range(2):
                at = 128 * (2 * q + z)
                oh[:, at : at + 128] = one_hot(lanes == ids[:, z : z + 1])

        def first_hop(to, slot_from):
            return pltpu.make_async_remote_copy(
                src_ref=ya.at[to],
                dst_ref=yr.at[slot_from],
                send_sem=ps_sem.at[to],
                recv_sem=pr_sem.at[slot_from],
                device_id=seat_device(to),
                device_id_type=MESH,
            )

        def second_hop(to, slot_from):
            return pltpu.make_async_remote_copy(
                src_ref=cb.at[to],
                dst_ref=rc.at[slot_from],
                send_sem=qs_sem.at[to],
                recv_sem=qr_sem.at[slot_from],
                device_id=site_device(to),
                device_id_type=MESH,
            )

        seats = [lax.rem(seat + step, SEATS) for step in range(1, SEATS)]
        sites = [lax.rem(site + step, SITES) for step in range(1, SITES)]
        exports(0)
        meet()
        start_all(0, *fwd)

        def one_round(r, carry):
            back_flux(r)
            sweep(False, True)
            give_back(r)
            start_all(r, *bwd)
            receive(r)
            sweep(True, False)
            forward(r)

            @pl.when(r < 3)
            def _():
                ahead = jnp.where(r == 2, time_step, 0.5 * time_step)
                for c in range(9):
                    y[r + 1, c] = y[0, c] + ahead * k[r, c]
                exports(r + 1)
                start_all(r + 1, *fwd)

            @pl.when(r == 3)
            def _():
                sums = [jnp.zeros((ROWS, 256), f32) for _ in range(3)]
                for q in range(4):
                    for c in range(3):
                        through = w[3 - q, 6 + c] - w[3 - q, c] * ie
                        sums[0] = sums[0] - w[3 - q, c] * k[q, c]
                        sums[1] = sums[1] + through * y[q, c]
                        sums[2] = sums[2] - through * k[q, 6 + c]
                grads = [
                    jnp.sum(value, axis=0, keepdims=True) * factor
                    for value, factor in zip(sums, (ie, it, it))
                ]
                slot = sslot[...]
                place = slot >> 1
                target = ((place & 3) * 2 + ((place >> 2) & 1)) * SITES + (place >> 3)
                chosen = one_hot(lax.broadcasted_iota(jnp.int32, (128, 256), 0) == target)
                lines = [jnp.where((slot & 1) == q, g, 0.0) for q in range(2) for g in grads]
                lines = jnp.concatenate(lines + [jnp.zeros((2, 256), f32)], axis=0)
                lines = [jnp.where(seat == q, lines, 0.0) for q in range(SEATS)]
                lines = jnp.concatenate(lines + [jnp.zeros((64, 256), f32)], axis=0)
                packed = sum(dot(chosen, part) for part in parts3(jnp.transpose(lines)))
                for q in range(SEATS):
                    ya[q] = packed[SITES * q : SITES * q + SITES]

                for other in seats:
                    first_hop(other, seat).start()

            adj_part = jnp.where(r == 2, time_step / 6.0, time_step / 3.0)
            back_part = jnp.where(r == 0, time_step, 0.5 * time_step)
            back = back_volume(r)
            for c in range(9):
                acc[c] = acc[c] + back[c]

            @pl.when(r < 3)
            def _():
                for c in range(9):
                    w[r + 1, c] = adj_part * adj24[c] + back_part * back[c]

            return carry

        lax.fori_loop(0, 4, one_round, 0)

        for other in seats:
            first_hop(other, other).wait_recv()
        mine = ya[pl.ds(seat, 1)][0]
        for q in range(SEATS):
            mine = mine + yr[q]
        for q in range(SITES):
            cb[q] = mine[q : q + 1]
        for other in sites:
            second_hop(other, site).start()
        for c in range(9):
            out[c] = acc[c][:NODES]

        for other in sites:
            second_hop(other, other).wait_recv()
        here = lax.broadcasted_iota(jnp.int32, (SITES, 128), 0) == site
        came = jnp.concatenate([rc[q] for q in range(SITES)], axis=0)
        came = came + jnp.where(here, mine, 0.0)
        turned = jnp.concatenate(parts3(jnp.transpose(came)[:64]), axis=0)
        spread = dot(turned, oh[...])
        spread = spread[:64] + spread[64:128] + spread[128:]
        total = jnp.zeros((3, 128), f32)
        for q in range(SEATS):
            for z in range(2):
                row, at = 8 * q + 3 * z, 128 * (2 * q + z)
                total = total + spread[row : row + 3, at : at + 128]
        therm[...] = total[:, :64]

        def all_sent(r, carry):
            wait_send_all(r, *fwd)
            wait_send_all(r, *bwd)
            return carry

        lax.fori_loop(0, 4, all_sent, 0)
        for other in seats:
            first_hop(other, seat).wait_send()
        for other in sites:
            second_hop(other, site).wait_send()

    return kernel


def per_device(
    field_state,
    adjoint,
    eps_inf,
    eps_delta,
    relax_time,
    metric,
    face_scale,
    face_angles,
    nbr_index,
    dom_export,
    sub_export,
    send_slot,
    recv_index,
):
    table, faces = host_tables()
    stage = pltpu.VMEM((4, 9, ROWS, 256), f32)
    trace = pltpu.VMEM((6, FACE, 256), f32)
    message = pltpu.VMEM((4, BLOCKS, 8, 128), f32)
    semaphores = pltpu.SemaphoreType.DMA((4, BLOCKS))
    state = pltpu.VMEM((9, ROWS, 256), f32)
    values = (
        field_state,
        adjoint,
        eps_inf.reshape(1, 256),
        eps_delta.reshape(1, 256),
        relax_time.reshape(1, 256),
        metric,
        face_scale,
        face_angles,
        nbr_index,
        dom_export.reshape(2, 128),
        sub_export,
        send_slot.reshape(1, 256),
        jnp.transpose(recv_index, (0, 2, 1)),
        jnp.asarray(table),
    )
    scratch = [pltpu.VMEM(value.shape, value.dtype) for value in values] + [
        pltpu.SemaphoreType.DMA((len(values),)),
        stage, stage, stage, state, state,
        pltpu.VMEM((3, FACE, 256), f32),
        pltpu.VMEM((FACE, 256), f32),
        pltpu.VMEM((6, 112, 256), f32),
        pltpu.VMEM((6, 112, 256), f32),
        trace, trace, trace,
        pltpu.VMEM((6 * ROWS, 256), f32),
        pltpu.VMEM((6, ROWS, 256), f32),
        pltpu.VMEM((12 * ROWS, 256), bf16),
        pltpu.VMEM((FACE, 256), jnp.int32),
        pltpu.VMEM((8, 128), jnp.int32),
        pltpu.VMEM((FACE, 256), jnp.int32),
        pltpu.VMEM((FACE, 256, 256), bf16),
        pltpu.VMEM((FACE * 256, 256), bf16),
        pltpu.VMEM((256, 128 * BLOCKS), bf16),
        pltpu.VMEM((128 * BLOCKS, 256), bf16),
        pltpu.VMEM((12 * ROWS, 256 * GROUP), bf16),
        pltpu.VMEM((12 * ROWS, 128 * BLOCKS), bf16),
        pltpu.VMEM((128, 8), jnp.int32),
        pltpu.VMEM((SITES, 128 * 2 * SEATS), bf16),
        message, message, message, message,
        pltpu.VMEM((SEATS, SITES, 128), f32),
        pltpu.VMEM((SEATS, SITES, 128), f32),
        pltpu.VMEM((SITES, 1, 128), f32),
        pltpu.VMEM((SITES, 1, 128), f32),
        semaphores, semaphores, semaphores, semaphores,
        pltpu.SemaphoreType.DMA((SEATS,)),
        pltpu.SemaphoreType.DMA((SEATS,)),
        pltpu.SemaphoreType.DMA((SITES,)),
        pltpu.SemaphoreType.DMA((SITES,)),
    ]
    call = pl.pallas_call(
        kernel_of(faces),
        out_shape=(
            jax.ShapeDtypeStruct((9, NODES, 256), f32),
            jax.ShapeDtypeStruct((3, 64), f32),
        ),
        in_specs=[pl.BlockSpec(memory_space=pltpu.HBM)] * 14,
        out_specs=(
            pl.BlockSpec(memory_space=pltpu.VMEM),
            pl.BlockSpec(memory_space=pltpu.VMEM),
        ),
        scratch_shapes=scratch,
        compiler_params=pltpu.CompilerParams(
            collective_id=0, has_side_effects=True, vmem_limit_bytes=32 << 20
        ),
        name="reverse_step",
    )
    return call(*[pltpu.with_memory_space_constraint(v, pltpu.HBM) for v in values])


def solution(mesh):
    both = ("dom", "sub")
    return jax.shard_map(
        per_device,
        mesh=mesh,
        in_specs=(
            P(None, None, both),
            P(None, None, both),
            P(both),
            P(both),
            P(both),
            P(None, both),
            P(None, both),
            P(None, None, both),
            P(None, both),
            P(both),
            P(both, None, None),
            P(both),
            P(both, None, None),
        ),
        out_specs=(P(None, None, both), P(None, both)),
        check_vma=False,
    )
```

```python
import math

import jax
import jax.numpy as jnp
import numpy as np
from jax import lax
from jax.experimental import pallas as pl
from jax.experimental.pallas import tpu as pltpu
from jax.sharding import PartitionSpec as P

time_step = 0.014
f32 = jnp.float32
bf16 = jnp.bfloat16
NODES = 20
ROWS = 24
FACE = 40
DOMS = 32
SUBS = 4
BLOCKS = 6
SEATS = 8
SITES = 16
GROUP = 40
MESH = pl.DeviceIdType.MESH


def mat_mul(left, right):
    inner = len(right)
    return [
        [
            sum((left[row_no][k] * right[k][col_no] for k in range(inner)))
            for col_no in range(len(right[0]))
        ]
        for row_no in range(len(left))
    ]


def transposed(matrix):
    return [list(column) for column in zip(*matrix)]


def solve_linear(matrix, rhs_rows):
    order = len(matrix)
    work = [list(matrix[row_no]) + list(rhs_rows[row_no]) for row_no in range(order)]
    for col_no in range(order):

        def magnitude(row_no):
            return abs(work[row_no][col_no])

        pivot = max(range(col_no, order), key=magnitude)
        work[col_no], work[pivot] = (work[pivot], work[col_no])
        head = work[col_no][col_no]
        work[col_no] = [value / head for value in work[col_no]]
        for row_no in range(order):
            if row_no != col_no:
                factor = work[row_no][col_no]
                work[row_no] = [
                    value - factor * other for value, other in zip(work[row_no], work[col_no])
                ]
    return [row[order:] for row in work]


def reference_element():
    lattice = [(i, j, k) for k in range(4) for j in range(4 - k) for i in range(4 - j - k)]
    points = [[float(v) / 3.0 for v in node] for node in lattice]
    vander = [[0.0] * 20 for node_no in range(20)]
    slopes = [[[0.0] * 20 for node_no in range(20)] for axis_no in range(3)]
    for node_no in range(20):
        for mono_no in range(20):
            power = lattice[mono_no]
            value = 1.0
            for axis_no in range(3):
                value *= points[node_no][axis_no] ** power[axis_no]
            vander[node_no][mono_no] = value
            for axis_no in range(3):
                if power[axis_no] > 0:
                    term = float(power[axis_no])
                    for other_no in range(3):
                        expo_val = power[other_no] - (1 if other_no == axis_no else 0)
                        term *= points[node_no][other_no] ** expo_val
                    slopes[axis_no][node_no][mono_no] = term
    identity = [[1.0 if row_no == col_no else 0.0 for col_no in range(20)] for row_no in range(20)]
    inverse = solve_linear(vander, identity)
    deriv_mats = [mat_mul(slopes[axis_no], inverse) for axis_no in range(3)]
    fact = math.factorial

    def face_integral(face_no, a, b, c):
        if face_no == 0:
            return 0.0 if c > 0 else fact(a) * fact(b) / fact(a + b + 2)
        if face_no == 1:
            return 0.0 if b > 0 else fact(a) * fact(c) / fact(a + c + 2)
        if face_no == 2:
            return math.sqrt(3.0) * fact(a) * fact(b) * fact(c) / fact(a + b + c + 2)
        return 0.0 if a > 0 else fact(b) * fact(c) / fact(b + c + 2)

    inverse_t = transposed(inverse)
    mono_mass = [[0.0] * 20 for node_no in range(20)]
    for first_no in range(20):
        for second_no in range(20):
            a = lattice[first_no][0] + lattice[second_no][0]
            b = lattice[first_no][1] + lattice[second_no][1]
            c = lattice[first_no][2] + lattice[second_no][2]
            mono_mass[first_no][second_no] = fact(a) * fact(b) * fact(c) / fact(a + b + c + 3)
    mass_mat = mat_mul(mat_mul(inverse_t, mono_mass), inverse)
    columns = [[] for node_no in range(20)]
    index_list = []
    for face_no in range(4):
        mono_face = [[0.0] * 20 for node_no in range(20)]
        for first_no in range(20):
            for second_no in range(20):
                a = lattice[first_no][0] + lattice[second_no][0]
                b = lattice[first_no][1] + lattice[second_no][1]
                c = lattice[first_no][2] + lattice[second_no][2]
                mono_face[first_no][second_no] = face_integral(face_no, a, b, c)
        face_mass = mat_mul(mat_mul(inverse_t, mono_face), inverse)
        tests = [k == 0 for i, j, k in lattice]
        if face_no == 1:
            tests = [j == 0 for i, j, k in lattice]
        if face_no == 2:
            tests = [i + j + k == 3 for i, j, k in lattice]
        if face_no == 3:
            tests = [i == 0 for i, j, k in lattice]
        chosen = [node_no for node_no in range(20) if tests[node_no]]
        for row_no in range(20):
            columns[row_no].extend([face_mass[row_no][col_no] for col_no in chosen])
        index_list.extend(chosen)
    lift_mat = solve_linear(mass_mat, columns)
    return (deriv_mats, lift_mat, index_list)


def host_tables():
    deriv, lift, faces = reference_element()
    deriv = np.asarray(deriv, np.float32)
    lift = np.asarray(lift, np.float32)
    pick = np.zeros((NODES, FACE), np.float32)
    pick[np.asarray(faces), np.arange(FACE)] = 1.0

    def placed(rows, cols, parts):
        result = np.zeros((rows, cols), np.float32)
        for at, part in parts:
            result[: part.shape[0], at : at + part.shape[1]] = part
        return result

    forward = placed(ROWS, 112, [(0, lift)] + [(40 + 24 * d, deriv[d]) for d in range(3)])
    backward = placed(ROWS, 112, [(0, pick)] + [(40 + 24 * d, deriv[d].T) for d in range(3)])
    lift_t = placed(FACE, ROWS, [(0, lift.T)])
    pick_t = placed(FACE, ROWS, [(0, pick.T)])

    def split(matrix):
        high = matrix.astype(jnp.bfloat16).astype(np.float32)
        low = matrix - high
        return np.concatenate(
            [np.concatenate([high, high], 1), np.concatenate([low, np.zeros_like(low)], 1)], 0
        )

    table = np.zeros((224, 256), np.float32)
    table[0:48, 0:224] = split(forward)
    table[48:96, 0:224] = split(backward)
    table[96:176, 0:48] = split(lift_t)
    table[176:216, 0:48] = np.concatenate([pick_t, pick_t], 1)
    return table.astype(jnp.bfloat16), [int(v) for v in faces]


def stacked(values):
    high = values.astype(bf16).astype(f32)
    return jnp.concatenate([high, values - high], axis=0).astype(bf16)


def parts3(values):
    first = values.astype(bf16)
    rest = values - first.astype(f32)
    second = rest.astype(bf16)
    third = (rest - second.astype(f32)).astype(bf16)
    return first, second, third


def dot(left, right):
    return jnp.dot(left, right, preferred_element_type=f32)


def node_of(rows, faces):
    result = rows - 20
    for row, node in enumerate(faces):
        result = jnp.where(rows == row, node, result)
    return result


def one_hot(condition):
    return jnp.where(condition, 1.0, 0.0).astype(bf16)


def kernel_of(faces):
    def kernel(
        *refs,
    ):
        given, refs = refs[:14], refs[14:]
        out, therm = refs[:2]
        held, in_sem, refs = refs[2:16], refs[16], refs[17:]
        fs, adj, einf, edel, tau, met, fsc, ang, nbr, dexp, sexp, sslot, recv, tab = held
        (
        y, k, w, adj24, acc, nrm, scl, x, xb, p, nb, cd, s_ref, pool, pp, nodes, nodex,
        elems, a_mat, at_mat, ax, axt, b_mat, bx, oids, oh,
        sf, rf, sb, rb, ya, yr, cb, rc,
        fs_sem, fr_sem, bs_sem, br_sem, ps_sem, pr_sem, qs_sem, qr_sem,
        ) = refs

        def fetch(i):
            return pltpu.make_async_copy(given[i], held[i], in_sem.at[i])

        order = (10, 9, 0, 13, 8, 1, 2, 4, 3, 7, 6, 5, 11, 12)
        for i in order:
            fetch(i).start()

        dom = lax.axis_index("dom")
        sub = lax.axis_index("sub")

        rf[...] = jnp.zeros_like(rf)
        rb[...] = jnp.zeros_like(rb)
        yr[...] = jnp.zeros_like(yr)
        rc[...] = jnp.zeros_like(rc)
        barrier = pltpu.get_barrier_semaphore()
        core = lax.rem(dom, 2)
        site = dom // 2
        seat = sub * 2 + core

        def seat_device(other):
            return (site * 2 + lax.rem(other, 2), other // 2)

        def site_device(other):
            return (other * 2 + core, sub)

        def greet(device):
            pl.semaphore_signal(barrier, inc=1, device_id=device, device_id_type=MESH)

        for step in range(1, SEATS):
            greet(seat_device(lax.rem(seat + step, SEATS)))
        for step in range(1, SITES):
            greet(site_device(lax.rem(site + step, SITES)))
        has_low = dom > 0
        has_high = dom < DOMS - 1

        @pl.when(has_low & (core == 0))
        def _():
            greet((dom - 1, sub))

        @pl.when(has_high & (core == 1))
        def _():
            greet((dom + 1, sub))

        def meet():
            outside = (has_low & (core == 0)) | (has_high & (core == 1))
            pl.semaphore_wait(barrier, jnp.where(outside, SEATS + SITES - 1, SEATS + SITES - 2))

        for i in order:
            fetch(i).wait()
        ie = 1.0 / einf[...]
        it = 1.0 / tau[...]
        ed = edel[...]
        pad = jnp.zeros((ROWS - NODES, 256), f32)
        for c in range(9):
            y[0, c] = jnp.concatenate([fs[c], pad], axis=0)
            value = jnp.concatenate([adj[c], pad], axis=0)
            adj24[c] = value
            acc[c] = value
            w[0, c] = (time_step / 6.0) * value
        sin_a = jnp.sin(ang[0])
        normals = (sin_a * jnp.cos(ang[1]), sin_a * jnp.sin(ang[1]), jnp.cos(ang[0]))
        for face in range(4):
            here = slice(10 * face, 10 * face + 10)
            for i in range(3):
                nrm[i, here, :] = jnp.broadcast_to(normals[i][face : face + 1], (10, 256))
            scl[here, :] = jnp.broadcast_to(0.5 * fsc[face : face + 1, :], (10, 256))

        exported = jnp.concatenate([sexp[0], dexp[...], jnp.zeros((2, 128), jnp.int32)], axis=0)
        nodex[...] = node_of(exported >> 8, faces)
        export_el = exported & 255
        export_cols = jnp.transpose(export_el)
        row_iota = lax.broadcasted_iota(jnp.int32, (256, 128), 0)
        lane_iota = lax.broadcasted_iota(jnp.int32, (128, 256), 1)
        for blk in range(BLOCKS):
            here = slice(128 * blk, 128 * blk + 128)
            ax[:, here] = one_hot(row_iota == export_el[blk : blk + 1])
            axt[here, :] = one_hot(lane_iota == export_cols[:, blk : blk + 1])

        def sub_copy(r, src, dst, send, recv_s, to, slot_from):
            return pltpu.make_async_remote_copy(
                src_ref=src.at[r, to],
                dst_ref=dst.at[r, slot_from],
                send_sem=send.at[r, to],
                recv_sem=recv_s.at[r, slot_from],
                device_id=(dom, to),
                device_id_type=MESH,
            )

        def dom_copy(r, src, dst, send, recv_s, block, slot, to):
            return pltpu.make_async_remote_copy(
                src_ref=src.at[r, block],
                dst_ref=dst.at[r, slot],
                send_sem=send.at[r, block],
                recv_sem=recv_s.at[r, slot],
                device_id=(to, sub),
                device_id_type=MESH,
            )

        def start_all(r, src, dst, send, recv_s):
            for step in range(1, SUBS):
                to = lax.rem(sub + step, SUBS)
                sub_copy(r, src, dst, send, recv_s, to, sub).start()

            @pl.when(has_low)
            def _():
                dom_copy(r, src, dst, send, recv_s, 4, 5, dom - 1).start()

            @pl.when(has_high)
            def _():
                dom_copy(r, src, dst, send, recv_s, 5, 4, dom + 1).start()

        def wait_recv_all(r, src, dst, send, recv_s):
            for step in range(1, SUBS):
                other = lax.rem(sub + step, SUBS)
                sub_copy(r, src, dst, send, recv_s, other, other).wait_recv()

            @pl.when(has_low)
            def _():
                dom_copy(r, src, dst, send, recv_s, 4, 4, dom - 1).wait_recv()

            @pl.when(has_high)
            def _():
                dom_copy(r, src, dst, send, recv_s, 5, 5, dom + 1).wait_recv()

        def wait_send_all(r, src, dst, send, recv_s):
            for step in range(1, SUBS):
                to = lax.rem(sub + step, SUBS)
                sub_copy(r, src, dst, send, recv_s, to, sub).wait_send()

            @pl.when(has_low)
            def _():
                dom_copy(r, src, dst, send, recv_s, 4, 5, dom - 1).wait_send()

            @pl.when(has_high)
            def _():
                dom_copy(r, src, dst, send, recv_s, 5, 4, dom + 1).wait_send()

        fwd = (sf, rf, fs_sem, fr_sem)
        bwd = (sb, rb, bs_sem, br_sem)

        node_iota = lax.broadcasted_iota(jnp.int32, (ROWS, 128), 0)
        node_iota2 = lax.broadcasted_iota(jnp.int32, (ROWS, 256), 0)
        own_rows = node_iota2 < NODES

        def fold_pool():
            values = pool[...].reshape(6 * ROWS, 256)
            high = values.astype(bf16)
            pp[0:144, :] = high
            pp[144:288, :] = (values - high.astype(f32)).astype(bf16)

        def exports(r):
            for c in range(6):
                pool[c] = y[r, c]
            fold_pool()
            for pair in range(BLOCKS // 2):
                both = dot(pp[...], ax[:, 256 * pair : 256 * pair + 256])
                both = both[:144] + both[144:]
                for half in range(2):
                    blk = 2 * pair + half
                    got = both[:, 128 * half : 128 * half + 128]
                    keep = node_iota == nodex[blk : blk + 1, :]
                    for c in range(6):
                        sf[r, blk, c : c + 1, :] = jnp.sum(
                            jnp.where(keep, got[24 * c : 24 * c + 24], 0.0), axis=0, keepdims=True
                        )
        def flux_rows(src, at):
            here = slice(at, at + 8)
            n = [nrm[i, here, :] for i in range(3)]
            e = [src[i, here, :] for i in range(3)]
            h = [src[3 + i, here, :] for i in range(3)]
            ne = n[0] * e[0] + n[1] * e[1] + n[2] * e[2]
            nh = n[0] * h[0] + n[1] * h[1] + n[2] * h[2]
            result = []
            for i in range(3):
                j, l = (i + 1) % 3, (i + 2) % 3
                result.append(n[i] * ne - e[i] - (n[j] * h[l] - n[l] * h[j]))
            for i in range(3):
                j, l = (i + 1) % 3, (i + 2) % 3
                result.append((n[j] * e[l] - n[l] * e[j]) + n[i] * nh - h[i])
            return result

        def curl_rows(x, e, h):
            for d in range(3):
                m = [met[3 * d + i : 3 * d + i + 1, :] for i in range(3)]
                here = slice(40 + 24 * d, 64 + 24 * d)
                for i in range(3):
                    j, l = (i + 1) % 3, (i + 2) % 3
                    x[i, here, :] = m[j] * h[l] - m[l] * h[j]
                    x[3 + i, here, :] = m[l] * e[j] - m[j] * e[l]

        def contracted(x, first, c):
            got = dot(tab[first : first + 48, 0:224], stacked(x[c]))
            return got[:24] + got[24:]

        def back_flux(r):
            for c in range(6):
                value = w[r, c]
                if c < 3:
                    value = value * ie
                got = dot(tab[96:176, 0:48], stacked(value))
                p[c] = (got[:40] + got[40:]) * scl[...]
            for at in range(0, FACE, 8):
                for c, value in enumerate(flux_rows(p, at)):
                    cd[c, at : at + 8, :] = value

        def sweep(gather, scatter):
            def group(g, carry):
                for j in range(GROUP):
                    fn = g * GROUP + j
                    keep = node_iota2 == nodes[pl.ds(fn, 1), :]
                    if gather:
                        got = dot(pp[...], a_mat[fn])
                        got = got[:144] + got[144:]
                        for c in range(6):
                            nb[c, pl.ds(fn, 1), :] = jnp.sum(
                                jnp.where(keep, got[24 * c : 24 * c + 24], 0.0),
                                axis=0,
                                keepdims=True,
                            )
                    if scatter:
                        high, low = [], []
                        for c in range(6):
                            value = cd[c, pl.ds(fn, 1), :]
                            top = value.astype(bf16).astype(f32)
                            high.append(jnp.where(keep, top, 0.0))
                            low.append(jnp.where(keep, value - top, 0.0))
                        b_mat[:, 256 * j : 256 * j + 256] = jnp.concatenate(high + low, 0).astype(
                            bf16
                        )
                if scatter:
                    span = GROUP * 256
                    got = dot(b_mat[...], at_mat[pl.ds(pl.multiple_of(g * span, span), span), :])
                    s_ref[...] = s_ref[...] - (got[:144] + got[144:])
                return carry

            if scatter:
                s_ref[...] = jnp.zeros_like(s_ref)
            lax.fori_loop(0, FACE // GROUP, group, 0)

        def give_back(r):
            for c in range(6):
                rows = s_ref[24 * c + 20 : 24 * c + 24, :]
                for blk in range(4):
                    at = 128 * (blk % 2)
                    sb[r, blk, c : c + 1, :] = rows[blk // 2 : blk // 2 + 1, at : at + 128]
                sb[r, 4, c : c + 1, :] = rows[2:3, 0:128]
                sb[r, 5, c : c + 1, :] = rows[3:4, 128:256]

        def arrived(r, blk, dst, src):
            value = dst[r, blk]
            if blk < SUBS:
                value = jnp.where(sub == blk, src[r, blk], value)
            return value

        def receive(r):
            wait_recv_all(r, *fwd)
            for blk in range(4):
                value = arrived(r, blk, rf, sf)
                at = 128 * (blk % 2)
                for c in range(6):
                    row = 20 + blk // 2
                    pool[c, row : row + 1, at : at + 128] = value[c : c + 1]
            low, high = rf[r, 4], rf[r, 5]
            for c in range(6):
                pool[c, 22:23, 0:128] = low[c : c + 1]
                pool[c, 23:24, 128:256] = high[c : c + 1]
            fold_pool()

        def forward(r, whole=True):
            for c in range(6):
                p[c] = dot(tab[176:216, 0:48], stacked(y[r, c])) - nb[c]
            for at in range(0, FACE, 8):
                factor = scl[at : at + 8, :]
                for c, value in enumerate(flux_rows(p, at)):
                    x[c, at : at + 8, :] = value * factor
            curl_rows(x, [y[r, c] for c in range(3)], [y[r, 3 + c] for c in range(3)])
            for c in range(3):
                current = (ed * y[r, c] - y[r, 6 + c]) * it
                k[r, 6 + c] = current
                k[r, c] = (contracted(x, 0, c) - current) * ie
                if whole:
                    k[r, 3 + c] = contracted(x, 0, 3 + c)

        def back_volume(r):
            for c in range(6):
                xb[c, 0:40, :] = cd[c]
            curl_rows(xb, [w[r, c] * ie for c in range(3)], [w[r, 3 + c] for c in range(3)])
            cots = [contracted(xb, 48, c) for c in range(6)]
            wait_recv_all(r, *bwd)
            for blk in range(BLOCKS):
                value = arrived(r, blk, rb, sb)
                keep = node_iota == nodex[blk : blk + 1, :]
                top = value.astype(bf16).astype(f32)
                rest = value - top
                high = [jnp.where(keep, top[c : c + 1], 0.0) for c in range(6)]
                low = [jnp.where(keep, rest[c : c + 1], 0.0) for c in range(6)]
                bx[:, 128 * blk : 128 * blk + 128] = jnp.concatenate(high + low, 0).astype(bf16)
            got = dot(bx[...], axt[...])
            s_ref[...] = s_ref[...] + (got[:144] + got[144:])
            for c in range(6):
                value = cots[c] + s_ref[24 * c : 24 * c + 24, :]
                cots[c] = jnp.where(own_rows, value, 0.0)
            for c in range(3):
                through = (w[r, 6 + c] - w[r, c] * ie) * it
                cots[c] = cots[c] + ed * through
                cots.append(-through)
            return cots

        index = nbr[...]
        nodes[...] = node_of(index >> 8, faces)
        element = index & 255
        elems[...] = element
        lane_iota2 = lax.broadcasted_iota(jnp.int32, (256, 256), 1)
        row_iota2 = lax.broadcasted_iota(jnp.int32, (256, 256), 0)

        def build(g, carry):
            rows = elems[pl.ds(pl.multiple_of(g * 8, 8), 8), :]
            columns = jnp.transpose(rows)
            for j in range(8):
                a_mat[g * 8 + j] = one_hot(row_iota2 == rows[j : j + 1])
                at = pl.multiple_of(g * 2048 + 256 * j, 256)
                at_mat[pl.ds(at, 256), :] = one_hot(lane_iota2 == columns[:, j : j + 1])
            return carry

        lax.fori_loop(0, FACE // 8, build, 0)
        owners = jnp.transpose(jnp.concatenate([recv[0], jnp.zeros((6, 128), jnp.int32)], axis=0))
        oids[...] = owners
        lanes = lax.broadcasted_iota(jnp.int32, (SITES, 128), 1)
        for q in range(SEATS):
            ids = oids[pl.ds((q % 2) * SUBS + q // 2, SITES, stride=SEATS), :]
            for z in range(2):
                at = 128 * (2 * q + z)
                oh[:, at : at + 128] = one_hot(lanes == ids[:, z : z + 1])

        def first_hop(to, slot_from):
            return pltpu.make_async_remote_copy(
                src_ref=ya.at[to],
                dst_ref=yr.at[slot_from],
                send_sem=ps_sem.at[to],
                recv_sem=pr_sem.at[slot_from],
                device_id=seat_device(to),
                device_id_type=MESH,
            )

        def second_hop(to, slot_from):
            return pltpu.make_async_remote_copy(
                src_ref=cb.at[to],
                dst_ref=rc.at[slot_from],
                send_sem=qs_sem.at[to],
                recv_sem=qr_sem.at[slot_from],
                device_id=site_device(to),
                device_id_type=MESH,
            )

        seats = [lax.rem(seat + step, SEATS) for step in range(1, SEATS)]
        sites = [lax.rem(site + step, SITES) for step in range(1, SITES)]
        exports(0)
        meet()
        start_all(0, *fwd)

        def one_round(r, carry):
            back_flux(r)
            sweep(False, True)
            give_back(r)
            start_all(r, *bwd)
            receive(r)
            sweep(True, False)
            forward(r)

            @pl.when(r < 3)
            def _():
                ahead = jnp.where(r == 2, time_step, 0.5 * time_step)
                for c in range(9):
                    y[r + 1, c] = y[0, c] + ahead * k[r, c]
                exports(r + 1)
                start_all(r + 1, *fwd)

            @pl.when(r == 3)
            def _():
                sums = [jnp.zeros((ROWS, 256), f32) for _ in range(3)]
                for q in range(4):
                    for c in range(3):
                        through = w[3 - q, 6 + c] - w[3 - q, c] * ie
                        sums[0] = sums[0] - w[3 - q, c] * k[q, c]
                        sums[1] = sums[1] + through * y[q, c]
                        sums[2] = sums[2] - through * k[q, 6 + c]
                grads = [
                    jnp.sum(value, axis=0, keepdims=True) * factor
                    for value, factor in zip(sums, (ie, it, it))
                ]
                slot = sslot[...]
                place = slot >> 1
                target = ((place & 3) * 2 + ((place >> 2) & 1)) * SITES + (place >> 3)
                chosen = one_hot(lax.broadcasted_iota(jnp.int32, (128, 256), 0) == target)
                lines = [jnp.where((slot & 1) == q, g, 0.0) for q in range(2) for g in grads]
                lines = jnp.concatenate(lines + [jnp.zeros((2, 256), f32)], axis=0)
                lines = [jnp.where(seat == q, lines, 0.0) for q in range(SEATS)]
                lines = jnp.concatenate(lines + [jnp.zeros((64, 256), f32)], axis=0)
                packed = sum(dot(chosen, part) for part in parts3(jnp.transpose(lines)))
                for q in range(SEATS):
                    ya[q] = packed[SITES * q : SITES * q + SITES]

                for other in seats:
                    first_hop(other, seat).start()

            adj_part = jnp.where(r == 2, time_step / 6.0, time_step / 3.0)
            back_part = jnp.where(r == 0, time_step, 0.5 * time_step)
            back = back_volume(r)
            for c in range(9):
                acc[c] = acc[c] + back[c]

            @pl.when(r < 3)
            def _():
                for c in range(9):
                    w[r + 1, c] = adj_part * adj24[c] + back_part * back[c]

            return carry

        lax.fori_loop(0, 4, one_round, 0)

        for other in seats:
            first_hop(other, other).wait_recv()
        mine = ya[pl.ds(seat, 1)][0]
        for q in range(SEATS):
            mine = mine + yr[q]
        for q in range(SITES):
            cb[q] = mine[q : q + 1]
        for other in sites:
            second_hop(other, site).start()
        for c in range(9):
            out[c] = acc[c][:NODES]

        for other in sites:
            second_hop(other, other).wait_recv()
        here = lax.broadcasted_iota(jnp.int32, (SITES, 128), 0) == site
        came = jnp.concatenate([rc[q] for q in range(SITES)], axis=0)
        came = came + jnp.where(here, mine, 0.0)
        turned = jnp.concatenate(parts3(jnp.transpose(came)[:64]), axis=0)
        spread = dot(turned, oh[...])
        spread = spread[:64] + spread[64:128] + spread[128:]
        total = jnp.zeros((3, 128), f32)
        for q in range(SEATS):
            for z in range(2):
                row, at = 8 * q + 3 * z, 128 * (2 * q + z)
                total = total + spread[row : row + 3, at : at + 128]
        therm[...] = total[:, :64]

        def all_sent(r, carry):
            wait_send_all(r, *fwd)
            wait_send_all(r, *bwd)
            return carry

        lax.fori_loop(0, 4, all_sent, 0)
        for other in seats:
            first_hop(other, seat).wait_send()
        for other in sites:
            second_hop(other, site).wait_send()

    return kernel


def per_device(
    field_state,
    adjoint,
    eps_inf,
    eps_delta,
    relax_time,
    metric,
    face_scale,
    face_angles,
    nbr_index,
    dom_export,
    sub_export,
    send_slot,
    recv_index,
):
    table, faces = host_tables()
    stage = pltpu.VMEM((4, 9, ROWS, 256), f32)
    trace = pltpu.VMEM((6, FACE, 256), f32)
    message = pltpu.VMEM((4, BLOCKS, 8, 128), f32)
    semaphores = pltpu.SemaphoreType.DMA((4, BLOCKS))
    state = pltpu.VMEM((9, ROWS, 256), f32)
    values = (
        field_state,
        adjoint,
        eps_inf.reshape(1, 256),
        eps_delta.reshape(1, 256),
        relax_time.reshape(1, 256),
        metric,
        face_scale,
        face_angles,
        nbr_index,
        dom_export.reshape(2, 128),
        sub_export,
        send_slot.reshape(1, 256),
        jnp.transpose(recv_index, (0, 2, 1)),
        jnp.asarray(table),
    )
    scratch = [pltpu.VMEM(value.shape, value.dtype) for value in values] + [
        pltpu.SemaphoreType.DMA((len(values),)),
        stage, stage, stage, state, state,
        pltpu.VMEM((3, FACE, 256), f32),
        pltpu.VMEM((FACE, 256), f32),
        pltpu.VMEM((6, 112, 256), f32),
        pltpu.VMEM((6, 112, 256), f32),
        trace, trace, trace,
        pltpu.VMEM((6 * ROWS, 256), f32),
        pltpu.VMEM((6, ROWS, 256), f32),
        pltpu.VMEM((12 * ROWS, 256), bf16),
        pltpu.VMEM((FACE, 256), jnp.int32),
        pltpu.VMEM((8, 128), jnp.int32),
        pltpu.VMEM((FACE, 256), jnp.int32),
        pltpu.VMEM((FACE, 256, 256), bf16),
        pltpu.VMEM((FACE * 256, 256), bf16),
        pltpu.VMEM((256, 128 * BLOCKS), bf16),
        pltpu.VMEM((128 * BLOCKS, 256), bf16),
        pltpu.VMEM((12 * ROWS, 256 * GROUP), bf16),
        pltpu.VMEM((12 * ROWS, 128 * BLOCKS), bf16),
        pltpu.VMEM((128, 8), jnp.int32),
        pltpu.VMEM((SITES, 128 * 2 * SEATS), bf16),
        message, message, message, message,
        pltpu.VMEM((SEATS, SITES, 128), f32),
        pltpu.VMEM((SEATS, SITES, 128), f32),
        pltpu.VMEM((SITES, 1, 128), f32),
        pltpu.VMEM((SITES, 1, 128), f32),
        semaphores, semaphores, semaphores, semaphores,
        pltpu.SemaphoreType.DMA((SEATS,)),
        pltpu.SemaphoreType.DMA((SEATS,)),
        pltpu.SemaphoreType.DMA((SITES,)),
        pltpu.SemaphoreType.DMA((SITES,)),
    ]
    call = pl.pallas_call(
        kernel_of(faces),
        out_shape=(
            jax.ShapeDtypeStruct((9, NODES, 256), f32),
            jax.ShapeDtypeStruct((3, 64), f32),
        ),
        in_specs=[pl.BlockSpec(memory_space=pltpu.HBM)] * 14,
        out_specs=(
            pl.BlockSpec(memory_space=pltpu.VMEM),
            pl.BlockSpec(memory_space=pltpu.VMEM),
        ),
        scratch_shapes=scratch,
        compiler_params=pltpu.CompilerParams(
            collective_id=0, has_side_effects=True, vmem_limit_bytes=32 << 20
        ),
        name="reverse_step",
    )
    return call(*[pltpu.with_memory_space_constraint(v, pltpu.HBM) for v in values])


def solution(mesh):
    both = ("dom", "sub")
    return jax.shard_map(
        per_device,
        mesh=mesh,
        in_specs=(
            P(None, None, both),
            P(None, None, both),
            P(both),
            P(both),
            P(both),
            P(None, both),
            P(None, both),
            P(None, None, both),
            P(None, both),
            P(both),
            P(both, None, None),
            P(both),
            P(both, None, None),
        ),
        out_specs=(P(None, None, both), P(None, both)),
        check_vma=False,
    )
```

```python
import math

import jax
import jax.numpy as jnp
import numpy as np
from jax import lax
from jax.experimental import pallas as pl
from jax.experimental.pallas import tpu as pltpu
from jax.sharding import PartitionSpec as P

time_step = 0.014
f32 = jnp.float32
bf16 = jnp.bfloat16
NODES = 20
ROWS = 24
FACE = 40
DOMS = 32
SUBS = 4
BLOCKS = 6
SEATS = 8
SITES = 16
GROUP = 20
MESH = pl.DeviceIdType.MESH


def mat_mul(left, right):
    inner = len(right)
    return [
        [
            sum((left[row_no][k] * right[k][col_no] for k in range(inner)))
            for col_no in range(len(right[0]))
        ]
        for row_no in range(len(left))
    ]


def transposed(matrix):
    return [list(column) for column in zip(*matrix)]


def solve_linear(matrix, rhs_rows):
    order = len(matrix)
    work = [list(matrix[row_no]) + list(rhs_rows[row_no]) for row_no in range(order)]
    for col_no in range(order):

        def magnitude(row_no):
            return abs(work[row_no][col_no])

        pivot = max(range(col_no, order), key=magnitude)
        work[col_no], work[pivot] = (work[pivot], work[col_no])
        head = work[col_no][col_no]
        work[col_no] = [value / head for value in work[col_no]]
        for row_no in range(order):
            if row_no != col_no:
                factor = work[row_no][col_no]
                work[row_no] = [
                    value - factor * other for value, other in zip(work[row_no], work[col_no])
                ]
    return [row[order:] for row in work]


def reference_element():
    lattice = [(i, j, k) for k in range(4) for j in range(4 - k) for i in range(4 - j - k)]
    points = [[float(v) / 3.0 for v in node] for node in lattice]
    vander = [[0.0] * 20 for node_no in range(20)]
    slopes = [[[0.0] * 20 for node_no in range(20)] for axis_no in range(3)]
    for node_no in range(20):
        for mono_no in range(20):
            power = lattice[mono_no]
            value = 1.0
            for axis_no in range(3):
                value *= points[node_no][axis_no] ** power[axis_no]
            vander[node_no][mono_no] = value
            for axis_no in range(3):
                if power[axis_no] > 0:
                    term = float(power[axis_no])
                    for other_no in range(3):
                        expo_val = power[other_no] - (1 if other_no == axis_no else 0)
                        term *= points[node_no][other_no] ** expo_val
                    slopes[axis_no][node_no][mono_no] = term
    identity = [[1.0 if row_no == col_no else 0.0 for col_no in range(20)] for row_no in range(20)]
    inverse = solve_linear(vander, identity)
    deriv_mats = [mat_mul(slopes[axis_no], inverse) for axis_no in range(3)]
    fact = math.factorial

    def face_integral(face_no, a, b, c):
        if face_no == 0:
            return 0.0 if c > 0 else fact(a) * fact(b) / fact(a + b + 2)
        if face_no == 1:
            return 0.0 if b > 0 else fact(a) * fact(c) / fact(a + c + 2)
        if face_no == 2:
            return math.sqrt(3.0) * fact(a) * fact(b) * fact(c) / fact(a + b + c + 2)
        return 0.0 if a > 0 else fact(b) * fact(c) / fact(b + c + 2)

    inverse_t = transposed(inverse)
    mono_mass = [[0.0] * 20 for node_no in range(20)]
    for first_no in range(20):
        for second_no in range(20):
            a = lattice[first_no][0] + lattice[second_no][0]
            b = lattice[first_no][1] + lattice[second_no][1]
            c = lattice[first_no][2] + lattice[second_no][2]
            mono_mass[first_no][second_no] = fact(a) * fact(b) * fact(c) / fact(a + b + c + 3)
    mass_mat = mat_mul(mat_mul(inverse_t, mono_mass), inverse)
    columns = [[] for node_no in range(20)]
    index_list = []
    for face_no in range(4):
        mono_face = [[0.0] * 20 for node_no in range(20)]
        for first_no in range(20):
            for second_no in range(20):
                a = lattice[first_no][0] + lattice[second_no][0]
                b = lattice[first_no][1] + lattice[second_no][1]
                c = lattice[first_no][2] + lattice[second_no][2]
                mono_face[first_no][second_no] = face_integral(face_no, a, b, c)
        face_mass = mat_mul(mat_mul(inverse_t, mono_face), inverse)
        tests = [k == 0 for i, j, k in lattice]
        if face_no == 1:
            tests = [j == 0 for i, j, k in lattice]
        if face_no == 2:
            tests = [i + j + k == 3 for i, j, k in lattice]
        if face_no == 3:
            tests = [i == 0 for i, j, k in lattice]
        chosen = [node_no for node_no in range(20) if tests[node_no]]
        for row_no in range(20):
            columns[row_no].extend([face_mass[row_no][col_no] for col_no in chosen])
        index_list.extend(chosen)
    lift_mat = solve_linear(mass_mat, columns)
    return (deriv_mats, lift_mat, index_list)


def host_tables():
    deriv, lift, faces = reference_element()
    deriv = np.asarray(deriv, np.float32)
    lift = np.asarray(lift, np.float32)
    pick = np.zeros((NODES, FACE), np.float32)
    pick[np.asarray(faces), np.arange(FACE)] = 1.0

    def placed(rows, cols, parts):
        result = np.zeros((rows, cols), np.float32)
        for at, part in parts:
            result[: part.shape[0], at : at + part.shape[1]] = part
        return result

    forward = placed(ROWS, 112, [(0, lift)] + [(40 + 24 * d, deriv[d]) for d in range(3)])
    backward = placed(ROWS, 112, [(0, pick)] + [(40 + 24 * d, deriv[d].T) for d in range(3)])
    lift_t = placed(FACE, ROWS, [(0, lift.T)])
    pick_t = placed(FACE, ROWS, [(0, pick.T)])

    def split(matrix):
        high = matrix.astype(jnp.bfloat16).astype(np.float32)
        low = matrix - high
        return np.concatenate(
            [np.concatenate([high, high], 1), np.concatenate([low, np.zeros_like(low)], 1)], 0
        )

    table = np.zeros((224, 256), np.float32)
    table[0:48, 0:224] = split(forward)
    table[48:96, 0:224] = split(backward)
    table[96:176, 0:48] = split(lift_t)
    table[176:216, 0:48] = np.concatenate([pick_t, pick_t], 1)
    return table.astype(jnp.bfloat16), [int(v) for v in faces]


def stacked(values):
    high = values.astype(bf16).astype(f32)
    return jnp.concatenate([high, values - high], axis=0).astype(bf16)


def parts3(values):
    first = values.astype(bf16)
    rest = values - first.astype(f32)
    second = rest.astype(bf16)
    third = (rest - second.astype(f32)).astype(bf16)
    return first, second, third


def dot(left, right):
    return jnp.dot(left, right, preferred_element_type=f32)


def node_of(rows, faces):
    result = rows - 20
    for row, node in enumerate(faces):
        result = jnp.where(rows == row, node, result)
    return result


def one_hot(condition):
    return jnp.where(condition, 1.0, 0.0).astype(bf16)


def kernel_of(faces):
    def kernel(
        *refs,
    ):
        given, refs = refs[:14], refs[14:]
        out, therm = refs[:2]
        held, in_sem, refs = refs[2:16], refs[16], refs[17:]
        fs, adj, einf, edel, tau, met, fsc, ang, nbr, dexp, sexp, sslot, recv, tab = held
        (
        y, k, w, adj24, acc, nrm, scl, x, xb, p, nb, cd, s_ref, pool, pp, nodes, nodex,
        elems, a_mat, at_mat, ax, axt, b_mat, bx, oids, oh,
        sf, rf, sb, rb, ya, yr, cb, rc,
        fs_sem, fr_sem, bs_sem, br_sem, ps_sem, pr_sem, qs_sem, qr_sem,
        ) = refs

        def fetch(i):
            return pltpu.make_async_copy(given[i], held[i], in_sem.at[i])

        order = (10, 9, 0, 13, 8, 1, 2, 4, 3, 7, 6, 5, 11, 12)
        for i in order:
            fetch(i).start()

        dom = lax.axis_index("dom")
        sub = lax.axis_index("sub")

        rf[...] = jnp.zeros_like(rf)
        rb[...] = jnp.zeros_like(rb)
        yr[...] = jnp.zeros_like(yr)
        rc[...] = jnp.zeros_like(rc)
        barrier = pltpu.get_barrier_semaphore()
        core = lax.rem(dom, 2)
        site = dom // 2
        seat = sub * 2 + core

        def seat_device(other):
            return (site * 2 + lax.rem(other, 2), other // 2)

        def site_device(other):
            return (other * 2 + core, sub)

        def greet(device):
            pl.semaphore_signal(barrier, inc=1, device_id=device, device_id_type=MESH)

        for step in range(1, SEATS):
            greet(seat_device(lax.rem(seat + step, SEATS)))
        for step in range(1, SITES):
            greet(site_device(lax.rem(site + step, SITES)))
        has_low = dom > 0
        has_high = dom < DOMS - 1

        @pl.when(has_low & (core == 0))
        def _():
            greet((dom - 1, sub))

        @pl.when(has_high & (core == 1))
        def _():
            greet((dom + 1, sub))

        def meet():
            outside = (has_low & (core == 0)) | (has_high & (core == 1))
            pl.semaphore_wait(barrier, jnp.where(outside, SEATS + SITES - 1, SEATS + SITES - 2))

        for i in order:
            fetch(i).wait()
        ie = 1.0 / einf[...]
        it = 1.0 / tau[...]
        ed = edel[...]
        pad = jnp.zeros((ROWS - NODES, 256), f32)
        for c in range(9):
            y[0, c] = jnp.concatenate([fs[c], pad], axis=0)
            value = jnp.concatenate([adj[c], pad], axis=0)
            adj24[c] = value
            acc[c] = value
            w[0, c] = (time_step / 6.0) * value
        sin_a = jnp.sin(ang[0])
        normals = (sin_a * jnp.cos(ang[1]), sin_a * jnp.sin(ang[1]), jnp.cos(ang[0]))
        for face in range(4):
            here = slice(10 * face, 10 * face + 10)
            for i in range(3):
                nrm[i, here, :] = jnp.broadcast_to(normals[i][face : face + 1], (10, 256))
            scl[here, :] = jnp.broadcast_to(0.5 * fsc[face : face + 1, :], (10, 256))

        exported = jnp.concatenate([sexp[0], dexp[...], jnp.zeros((2, 128), jnp.int32)], axis=0)
        nodex[...] = node_of(exported >> 8, faces)
        export_el = exported & 255
        export_cols = jnp.transpose(export_el)
        row_iota = lax.broadcasted_iota(jnp.int32, (256, 128), 0)
        lane_iota = lax.broadcasted_iota(jnp.int32, (128, 256), 1)
        for blk in range(BLOCKS):
            here = slice(128 * blk, 128 * blk + 128)
            ax[:, here] = one_hot(row_iota == export_el[blk : blk + 1])
            axt[here, :] = one_hot(lane_iota == export_cols[:, blk : blk + 1])

        def sub_copy(r, src, dst, send, recv_s, to, slot_from):
            return pltpu.make_async_remote_copy(
                src_ref=src.at[r, to],
                dst_ref=dst.at[r, slot_from],
                send_sem=send.at[r, to],
                recv_sem=recv_s.at[r, slot_from],
                device_id=(dom, to),
                device_id_type=MESH,
            )

        def dom_copy(r, src, dst, send, recv_s, block, slot, to):
            return pltpu.make_async_remote_copy(
                src_ref=src.at[r, block],
                dst_ref=dst.at[r, slot],
                send_sem=send.at[r, block],
                recv_sem=recv_s.at[r, slot],
                device_id=(to, sub),
                device_id_type=MESH,
            )

        def start_all(r, src, dst, send, recv_s):
            for step in range(1, SUBS):
                to = lax.rem(sub + step, SUBS)
                sub_copy(r, src, dst, send, recv_s, to, sub).start()

            @pl.when(has_low)
            def _():
                dom_copy(r, src, dst, send, recv_s, 4, 5, dom - 1).start()

            @pl.when(has_high)
            def _():
                dom_copy(r, src, dst, send, recv_s, 5, 4, dom + 1).start()

        def wait_recv_all(r, src, dst, send, recv_s):
            for step in range(1, SUBS):
                other = lax.rem(sub + step, SUBS)
                sub_copy(r, src, dst, send, recv_s, other, other).wait_recv()

            @pl.when(has_low)
            def _():
                dom_copy(r, src, dst, send, recv_s, 4, 4, dom - 1).wait_recv()

            @pl.when(has_high)
            def _():
                dom_copy(r, src, dst, send, recv_s, 5, 5, dom + 1).wait_recv()

        def wait_send_all(r, src, dst, send, recv_s):
            for step in range(1, SUBS):
                to = lax.rem(sub + step, SUBS)
                sub_copy(r, src, dst, send, recv_s, to, sub).wait_send()

            @pl.when(has_low)
            def _():
                dom_copy(r, src, dst, send, recv_s, 4, 5, dom - 1).wait_send()

            @pl.when(has_high)
            def _():
                dom_copy(r, src, dst, send, recv_s, 5, 4, dom + 1).wait_send()

        fwd = (sf, rf, fs_sem, fr_sem)
        bwd = (sb, rb, bs_sem, br_sem)

        node_iota = lax.broadcasted_iota(jnp.int32, (ROWS, 128), 0)
        node_iota2 = lax.broadcasted_iota(jnp.int32, (ROWS, 256), 0)
        own_rows = node_iota2 < NODES

        def fold_pool():
            values = pool[...].reshape(6 * ROWS, 256)
            high = values.astype(bf16)
            pp[0:144, :] = high
            pp[144:288, :] = (values - high.astype(f32)).astype(bf16)

        def exports(r):
            for c in range(6):
                pool[c] = y[r, c]
            fold_pool()
            for pair in range(BLOCKS // 2):
                both = dot(pp[...], ax[:, 256 * pair : 256 * pair + 256])
                both = both[:144] + both[144:]
                for half in range(2):
                    blk = 2 * pair + half
                    got = both[:, 128 * half : 128 * half + 128]
                    keep = node_iota == nodex[blk : blk + 1, :]
                    for c in range(6):
                        sf[r, blk, c : c + 1, :] = jnp.sum(
                            jnp.where(keep, got[24 * c : 24 * c + 24], 0.0), axis=0, keepdims=True
                        )
        def flux_rows(src, at):
            here = slice(at, at + 8)
            n = [nrm[i, here, :] for i in range(3)]
            e = [src[i, here, :] for i in range(3)]
            h = [src[3 + i, here, :] for i in range(3)]
            ne = n[0] * e[0] + n[1] * e[1] + n[2] * e[2]
            nh = n[0] * h[0] + n[1] * h[1] + n[2] * h[2]
            result = []
            for i in range(3):
                j, l = (i + 1) % 3, (i + 2) % 3
                result.append(n[i] * ne - e[i] - (n[j] * h[l] - n[l] * h[j]))
            for i in range(3):
                j, l = (i + 1) % 3, (i + 2) % 3
                result.append((n[j] * e[l] - n[l] * e[j]) + n[i] * nh - h[i])
            return result

        def curl_rows(x, e, h):
            for d in range(3):
                m = [met[3 * d + i : 3 * d + i + 1, :] for i in range(3)]
                here = slice(40 + 24 * d, 64 + 24 * d)
                for i in range(3):
                    j, l = (i + 1) % 3, (i + 2) % 3
                    x[i, here, :] = m[j] * h[l] - m[l] * h[j]
                    x[3 + i, here, :] = m[l] * e[j] - m[j] * e[l]

        def contracted(x, first, c):
            got = dot(tab[first : first + 48, 0:224], stacked(x[c]))
            return got[:24] + got[24:]

        def back_flux(r):
            for c in range(6):
                value = w[r, c]
                if c < 3:
                    value = value * ie
                got = dot(tab[96:176, 0:48], stacked(value))
                p[c] = (got[:40] + got[40:]) * scl[...]
            for at in range(0, FACE, 8):
                for c, value in enumerate(flux_rows(p, at)):
                    cd[c, at : at + 8, :] = value

        def sweep(gather, scatter):
            rows_a_step = GROUP if scatter else FACE

            def group(g, carry):
                for j in range(rows_a_step):
                    fn = g * rows_a_step + j
                    keep = node_iota2 == nodes[pl.ds(fn, 1), :]
                    if gather:
                        got = dot(pp[...], a_mat[fn])
                        got = got[:144] + got[144:]
                        for c in range(6):
                            nb[c, pl.ds(fn, 1), :] = jnp.sum(
                                jnp.where(keep, got[24 * c : 24 * c + 24], 0.0),
                                axis=0,
                                keepdims=True,
                            )
                    if scatter:
                        high, low = [], []
                        for c in range(6):
                            value = cd[c, pl.ds(fn, 1), :]
                            top = value.astype(bf16).astype(f32)
                            high.append(jnp.where(keep, top, 0.0))
                            low.append(jnp.where(keep, value - top, 0.0))
                        b_mat[:, 256 * j : 256 * j + 256] = jnp.concatenate(high + low, 0).astype(
                            bf16
                        )
                if scatter:
                    span = GROUP * 256
                    got = dot(b_mat[...], at_mat[pl.ds(pl.multiple_of(g * span, span), span), :])
                    s_ref[...] = s_ref[...] - (got[:144] + got[144:])
                return carry

            if scatter:
                s_ref[...] = jnp.zeros_like(s_ref)
            lax.fori_loop(0, FACE // rows_a_step, group, 0)

        def give_back(r):
            for c in range(6):
                rows = s_ref[24 * c + 20 : 24 * c + 24, :]
                for blk in range(4):
                    at = 128 * (blk % 2)
                    sb[r, blk, c : c + 1, :] = rows[blk // 2 : blk // 2 + 1, at : at + 128]
                sb[r, 4, c : c + 1, :] = rows[2:3, 0:128]
                sb[r, 5, c : c + 1, :] = rows[3:4, 128:256]

        def arrived(r, blk, dst, src):
            value = dst[r, blk]
            if blk < SUBS:
                value = jnp.where(sub == blk, src[r, blk], value)
            return value

        def receive(r):
            wait_recv_all(r, *fwd)
            for blk in range(4):
                value = arrived(r, blk, rf, sf)
                at = 128 * (blk % 2)
                for c in range(6):
                    row = 20 + blk // 2
                    pool[c, row : row + 1, at : at + 128] = value[c : c + 1]
            low, high = rf[r, 4], rf[r, 5]
            for c in range(6):
                pool[c, 22:23, 0:128] = low[c : c + 1]
                pool[c, 23:24, 128:256] = high[c : c + 1]
            fold_pool()

        def forward(r, whole=True):
            for c in range(6):
                p[c] = dot(tab[176:216, 0:48], stacked(y[r, c])) - nb[c]
            for at in range(0, FACE, 8):
                factor = scl[at : at + 8, :]
                for c, value in enumerate(flux_rows(p, at)):
                    x[c, at : at + 8, :] = value * factor
            curl_rows(x, [y[r, c] for c in range(3)], [y[r, 3 + c] for c in range(3)])
            for c in range(3):
                current = (ed * y[r, c] - y[r, 6 + c]) * it
                k[r, 6 + c] = current
                k[r, c] = (contracted(x, 0, c) - current) * ie
                if whole:
                    k[r, 3 + c] = contracted(x, 0, 3 + c)

        def back_volume(r):
            for c in range(6):
                xb[c, 0:40, :] = cd[c]
            curl_rows(xb, [w[r, c] * ie for c in range(3)], [w[r, 3 + c] for c in range(3)])
            cots = [contracted(xb, 48, c) for c in range(6)]
            wait_recv_all(r, *bwd)
            for blk in range(BLOCKS):
                value = arrived(r, blk, rb, sb)
                keep = node_iota == nodex[blk : blk + 1, :]
                top = value.astype(bf16).astype(f32)
                rest = value - top
                high = [jnp.where(keep, top[c : c + 1], 0.0) for c in range(6)]
                low = [jnp.where(keep, rest[c : c + 1], 0.0) for c in range(6)]
                bx[:, 128 * blk : 128 * blk + 128] = jnp.concatenate(high + low, 0).astype(bf16)
            got = dot(bx[...], axt[...])
            s_ref[...] = s_ref[...] + (got[:144] + got[144:])
            for c in range(6):
                value = cots[c] + s_ref[24 * c : 24 * c + 24, :]
                cots[c] = jnp.where(own_rows, value, 0.0)
            for c in range(3):
                through = (w[r, 6 + c] - w[r, c] * ie) * it
                cots[c] = cots[c] + ed * through
                cots.append(-through)
            return cots

        index = nbr[...]
        nodes[...] = node_of(index >> 8, faces)
        element = index & 255
        elems[...] = element
        lane_iota2 = lax.broadcasted_iota(jnp.int32, (256, 256), 1)
        row_iota2 = lax.broadcasted_iota(jnp.int32, (256, 256), 0)

        def build(g, carry):
            rows = elems[pl.ds(pl.multiple_of(g * 8, 8), 8), :]
            columns = jnp.transpose(rows)
            for j in range(8):
                a_mat[g * 8 + j] = one_hot(row_iota2 == rows[j : j + 1])
                at = pl.multiple_of(g * 2048 + 256 * j, 256)
                at_mat[pl.ds(at, 256), :] = one_hot(lane_iota2 == columns[:, j : j + 1])
            return carry

        lax.fori_loop(0, FACE // 8, build, 0)
        owners = jnp.transpose(jnp.concatenate([recv[0], jnp.zeros((6, 128), jnp.int32)], axis=0))
        oids[...] = owners
        lanes = lax.broadcasted_iota(jnp.int32, (SITES, 128), 1)
        for q in range(SEATS):
            ids = oids[pl.ds((q % 2) * SUBS + q // 2, SITES, stride=SEATS), :]
            for z in range(2):
                at = 128 * (2 * q + z)
                oh[:, at : at + 128] = one_hot(lanes == ids[:, z : z + 1])

        def first_hop(to, slot_from):
            return pltpu.make_async_remote_copy(
                src_ref=ya.at[to],
                dst_ref=yr.at[slot_from],
                send_sem=ps_sem.at[to],
                recv_sem=pr_sem.at[slot_from],
                device_id=seat_device(to),
                device_id_type=MESH,
            )

        def second_hop(to, slot_from):
            return pltpu.make_async_remote_copy(
                src_ref=cb.at[to],
                dst_ref=rc.at[slot_from],
                send_sem=qs_sem.at[to],
                recv_sem=qr_sem.at[slot_from],
                device_id=site_device(to),
                device_id_type=MESH,
            )

        seats = [lax.rem(seat + step, SEATS) for step in range(1, SEATS)]
        sites = [lax.rem(site + step, SITES) for step in range(1, SITES)]
        exports(0)
        meet()
        start_all(0, *fwd)

        def one_round(r, carry):
            back_flux(r)
            sweep(False, True)
            give_back(r)
            start_all(r, *bwd)
            receive(r)
            sweep(True, False)
            forward(r)

            @pl.when(r < 3)
            def _():
                ahead = jnp.where(r == 2, time_step, 0.5 * time_step)
                for c in range(9):
                    y[r + 1, c] = y[0, c] + ahead * k[r, c]
                exports(r + 1)
                start_all(r + 1, *fwd)

            @pl.when(r == 3)
            def _():
                sums = [jnp.zeros((ROWS, 256), f32) for _ in range(3)]
                for q in range(4):
                    for c in range(3):
                        through = w[3 - q, 6 + c] - w[3 - q, c] * ie
                        sums[0] = sums[0] - w[3 - q, c] * k[q, c]
                        sums[1] = sums[1] + through * y[q, c]
                        sums[2] = sums[2] - through * k[q, 6 + c]
                grads = [
                    jnp.sum(value, axis=0, keepdims=True) * factor
                    for value, factor in zip(sums, (ie, it, it))
                ]
                slot = sslot[...]
                place = slot >> 1
                target = ((place & 3) * 2 + ((place >> 2) & 1)) * SITES + (place >> 3)
                chosen = one_hot(lax.broadcasted_iota(jnp.int32, (128, 256), 0) == target)
                lines = [jnp.where((slot & 1) == q, g, 0.0) for q in range(2) for g in grads]
                lines = jnp.concatenate(lines + [jnp.zeros((2, 256), f32)], axis=0)
                lines = [jnp.where(seat == q, lines, 0.0) for q in range(SEATS)]
                lines = jnp.concatenate(lines + [jnp.zeros((64, 256), f32)], axis=0)
                packed = sum(dot(chosen, part) for part in parts3(jnp.transpose(lines)))
                for q in range(SEATS):
                    ya[q] = packed[SITES * q : SITES * q + SITES]

                for other in seats:
                    first_hop(other, seat).start()

            adj_part = jnp.where(r == 2, time_step / 6.0, time_step / 3.0)
            back_part = jnp.where(r == 0, time_step, 0.5 * time_step)
            back = back_volume(r)
            for c in range(9):
                acc[c] = acc[c] + back[c]

            @pl.when(r < 3)
            def _():
                for c in range(9):
                    w[r + 1, c] = adj_part * adj24[c] + back_part * back[c]

            return carry

        lax.fori_loop(0, 4, one_round, 0)

        for other in seats:
            first_hop(other, other).wait_recv()
        mine = ya[pl.ds(seat, 1)][0]
        for q in range(SEATS):
            mine = mine + yr[q]
        for q in range(SITES):
            cb[q] = mine[q : q + 1]
        for other in sites:
            second_hop(other, site).start()
        for c in range(9):
            out[c] = acc[c][:NODES]

        for other in sites:
            second_hop(other, other).wait_recv()
        here = lax.broadcasted_iota(jnp.int32, (SITES, 128), 0) == site
        came = jnp.concatenate([rc[q] for q in range(SITES)], axis=0)
        came = came + jnp.where(here, mine, 0.0)
        turned = jnp.concatenate(parts3(jnp.transpose(came)[:64]), axis=0)
        spread = dot(turned, oh[...])
        spread = spread[:64] + spread[64:128] + spread[128:]
        total = jnp.zeros((3, 128), f32)
        for q in range(SEATS):
            for z in range(2):
                row, at = 8 * q + 3 * z, 128 * (2 * q + z)
                total = total + spread[row : row + 3, at : at + 128]
        therm[...] = total[:, :64]

        def all_sent(r, carry):
            wait_send_all(r, *fwd)
            wait_send_all(r, *bwd)
            return carry

        lax.fori_loop(0, 4, all_sent, 0)
        for other in seats:
            first_hop(other, seat).wait_send()
        for other in sites:
            second_hop(other, site).wait_send()

    return kernel


def per_device(
    field_state,
    adjoint,
    eps_inf,
    eps_delta,
    relax_time,
    metric,
    face_scale,
    face_angles,
    nbr_index,
    dom_export,
    sub_export,
    send_slot,
    recv_index,
):
    table, faces = host_tables()
    stage = pltpu.VMEM((4, 9, ROWS, 256), f32)
    trace = pltpu.VMEM((6, FACE, 256), f32)
    message = pltpu.VMEM((4, BLOCKS, 8, 128), f32)
    semaphores = pltpu.SemaphoreType.DMA((4, BLOCKS))
    state = pltpu.VMEM((9, ROWS, 256), f32)
    values = (
        field_state,
        adjoint,
        eps_inf.reshape(1, 256),
        eps_delta.reshape(1, 256),
        relax_time.reshape(1, 256),
        metric,
        face_scale,
        face_angles,
        nbr_index,
        dom_export.reshape(2, 128),
        sub_export,
        send_slot.reshape(1, 256),
        jnp.transpose(recv_index, (0, 2, 1)),
        jnp.asarray(table),
    )
    scratch = [pltpu.VMEM(value.shape, value.dtype) for value in values] + [
        pltpu.SemaphoreType.DMA((len(values),)),
        stage, stage, stage, state, state,
        pltpu.VMEM((3, FACE, 256), f32),
        pltpu.VMEM((FACE, 256), f32),
        pltpu.VMEM((6, 112, 256), f32),
        pltpu.VMEM((6, 112, 256), f32),
        trace, trace, trace,
        pltpu.VMEM((6 * ROWS, 256), f32),
        pltpu.VMEM((6, ROWS, 256), f32),
        pltpu.VMEM((12 * ROWS, 256), bf16),
        pltpu.VMEM((FACE, 256), jnp.int32),
        pltpu.VMEM((8, 128), jnp.int32),
        pltpu.VMEM((FACE, 256), jnp.int32),
        pltpu.VMEM((FACE, 256, 256), bf16),
        pltpu.VMEM((FACE * 256, 256), bf16),
        pltpu.VMEM((256, 128 * BLOCKS), bf16),
        pltpu.VMEM((128 * BLOCKS, 256), bf16),
        pltpu.VMEM((12 * ROWS, 256 * GROUP), bf16),
        pltpu.VMEM((12 * ROWS, 128 * BLOCKS), bf16),
        pltpu.VMEM((128, 8), jnp.int32),
        pltpu.VMEM((SITES, 128 * 2 * SEATS), bf16),
        message, message, message, message,
        pltpu.VMEM((SEATS, SITES, 128), f32),
        pltpu.VMEM((SEATS, SITES, 128), f32),
        pltpu.VMEM((SITES, 1, 128), f32),
        pltpu.VMEM((SITES, 1, 128), f32),
        semaphores, semaphores, semaphores, semaphores,
        pltpu.SemaphoreType.DMA((SEATS,)),
        pltpu.SemaphoreType.DMA((SEATS,)),
        pltpu.SemaphoreType.DMA((SITES,)),
        pltpu.SemaphoreType.DMA((SITES,)),
    ]
    call = pl.pallas_call(
        kernel_of(faces),
        out_shape=(
            jax.ShapeDtypeStruct((9, NODES, 256), f32),
            jax.ShapeDtypeStruct((3, 64), f32),
        ),
        in_specs=[pl.BlockSpec(memory_space=pltpu.HBM)] * 14,
        out_specs=(
            pl.BlockSpec(memory_space=pltpu.VMEM),
            pl.BlockSpec(memory_space=pltpu.VMEM),
        ),
        scratch_shapes=scratch,
        compiler_params=pltpu.CompilerParams(
            collective_id=0, has_side_effects=True, vmem_limit_bytes=32 << 20
        ),
        name="reverse_step",
    )
    return call(*[pltpu.with_memory_space_constraint(v, pltpu.HBM) for v in values])


def solution(mesh):
    both = ("dom", "sub")
    return jax.shard_map(
        per_device,
        mesh=mesh,
        in_specs=(
            P(None, None, both),
            P(None, None, both),
            P(both),
            P(both),
            P(both),
            P(None, both),
            P(None, both),
            P(None, None, both),
            P(None, both),
            P(both),
            P(both, None, None),
            P(both),
            P(both, None, None),
        ),
        out_specs=(P(None, None, both), P(None, both)),
        check_vma=False,
    )
```
